512 devices in a mesh: slab: 16 (over z_hi, y), dom: 32 (over z_lo, x, core).
Axes of the slice: x: 4, y: 8, z: 8 (z_hi: 2, z_lo: 4; z = z_hi * 4 + z_lo), core: 2. Of those that a mesh axis runs over, the one named last changes fastest.
Arguments:
- velocity: float32 [3, 343, 65536], P(None, None, ('slab', 'dom')), may hold values from -17 to 17
- slot_map: int32 [16, 32, 128], P('slab', 'dom'), may hold values from 0 to 127, each once within a row
- class_index: int32 [16, 32, 128], P('slab', 'dom'), may hold values from 0 to 15, as said below
- schur_blocks: float32 [16, 218, 218], replicated, may hold values from -1.21 to 8.75, as said below
Outputs:
- pressure: float32 [218, 65536], P(None, ('slab', 'dom'))
- residual: float32 [218, 65536], P(None, ('slab', 'dom'))
The draws below stay inside these ranges and needn't reach their ends.
Inputs may be any that keep to these rules, and one draw needn't show every extreme that they name: On each device the entries of slot_map are a permutation of the brick positions (bx * 8 + by) * 16 + bz: every position holds one element. `class_index`: on every device each of the 16 classes holds exactly 8 of its elements. `schur_blocks`: every block is symmetric and positive definite.
All inputs are finite; a program needn't handle non-finite values.
Results may differ from the reference program's by a relative error of at most 0.0003.
Values sent between devices are 32-bit elements; how exact they have to be, the bound alone decides.
No kernel may reach another device: no remote copies, remote signals or barrier semaphores. Data moves between devices by JAX's collectives and lax.ppermute only.
A program may use at most 64 MiB of HBM per device.

```python
import math
import jax
import jax.numpy as jnp
import numpy as np
from jax import lax

BX = 1
BY = 8
BZ = 16
CLASSES = 16
MODES = 218
NODES = 343
ITERS = 2
E_DEV = 128
SLABS = 16
DOMAINS = 32
ELEMENTS = 65536


def draw_velocity(key, part):
    noise_key, spread_key = jax.random.split(jax.random.fold_in(key, 11), 2)
    position = jnp.arange(ELEMENTS, dtype=jnp.float32) / ELEMENTS
    spread = jnp.exp(jax.random.uniform(spread_key, (ELEMENTS,), jnp.float32, math.log(0.4), math.log(1.4)))
    scaling = (1.0 + 2.0 * position) * spread
    noise = jnp.clip(jax.random.normal(noise_key, (3, NODES, ELEMENTS), jnp.float32), -4.0, 4.0)
    return (noise * scaling).astype(jnp.float32)


def draw_class_index(key, part):
    base_row = jnp.arange(E_DEV, dtype=jnp.int32) % CLASSES
    stacked = jnp.broadcast_to(base_row, (SLABS * DOMAINS, E_DEV))
    mixed = jax.random.permutation(jax.random.fold_in(key, 5), stacked, axis=1, independent=True)
    return mixed.reshape(SLABS, DOMAINS, E_DEV).astype(jnp.int32)


def draw_schur_blocks(key, part):
    base_key = jax.random.fold_in(key, 23)
    off_key, diag_key, edge_key, first_key, second_key = jax.random.split(base_key, 5)
    raw_noise = jax.random.uniform(off_key, (CLASSES, MODES, MODES), jnp.float32, -1.35, 1.35) / (MODES - 1)
    symmetric = 0.5 * (raw_noise + jnp.swapaxes(raw_noise, 1, 2))
    identity = jnp.eye(MODES, dtype=jnp.float32)
    first_offset = jax.random.randint(first_key, (CLASSES,), 1, 55)
    second_offset = first_offset + jax.random.randint(second_key, (CLASSES,), 1, 55)
    excess = jax.random.uniform(diag_key, (CLASSES, MODES), jnp.float32, 0.4, 1.6)
    edge_weights = jax.random.uniform(edge_key, (2, CLASSES, MODES), jnp.float32, 0.3, 1.2)
    mode_ids = jnp.arange(MODES, dtype=jnp.int32)
    coupling = jnp.zeros((CLASSES, MODES, MODES), jnp.float32)
    degree = jnp.zeros((CLASSES, MODES), jnp.float32)
    for member, offset in ((0, first_offset), (1, second_offset)):
        weight = edge_weights[member]
        partner = (mode_ids[None, :] + offset[:, None]) % MODES
        forward = (mode_ids[None, None, :] == partner[:, :, None]).astype(jnp.float32) * weight[:, :, None]
        coupling = coupling + forward + jnp.swapaxes(forward, 1, 2)
        source_row = ((mode_ids[None, :] - offset[:, None]) % MODES).astype(jnp.int32)
        degree = degree + weight + jnp.take_along_axis(weight, source_row, axis=1)
    diagonal = 1.0 + excess + 1.35 + degree
    return (symmetric * (1.0 - identity) - coupling + identity * diagonal[:, :, None]).astype(jnp.float32)


def setup_inputs(seed: int = 0) -> dict:
    splits = jax.random.split(jax.random.key(seed), 5)
    velocity = draw_velocity(jax.random.fold_in(splits[4], 71), 0)
    slot_map = jax.vmap(lambda own: jax.random.permutation(own, E_DEV))(jax.random.split(splits[1], SLABS * DOMAINS)).reshape((SLABS, DOMAINS, E_DEV)).astype(jnp.int32)
    class_index = draw_class_index(jax.random.fold_in(splits[4], 71), 0)
    schur_blocks = draw_schur_blocks(jax.random.fold_in(splits[4], 71), 0)
    return dict(velocity=velocity, slot_map=slot_map, class_index=class_index, schur_blocks=schur_blocks)


DELTA_T = 0.05
EINSUM_FORMS = ('pa,kabcm->kpbcm', 'pb,kabcm->kapcm', 'pc,kabcm->kabpm')


def gll_tables():
    degree = 6
    outer_point = 0.830223896278566929872
    inner_point = 0.468848793470714213803
    points = np.array([-1.0, -outer_point, -inner_point, 0.0, inner_point, outer_point, 1.0])
    values = (231.0 * points ** 6 - 315.0 * points ** 4 + 105.0 * points ** 2 - 5.0) / 16.0
    weights = 2.0 / (degree * (degree + 1) * values ** 2)
    derivative = np.zeros((7, 7))
    for target in range(7):
        for source in range(7):
            if target != source:
                derivative[target, source] = values[target] / (values[source] * (points[target] - points[source]))
    derivative[0, 0] = -degree * (degree + 1) / 4.0
    derivative[6, 6] = degree * (degree + 1) / 4.0
    return derivative, weights


def shell_tables():
    surface = np.array([index for index in range(343) if (index // 49) in (0, 6) or ((index // 7) % 7) in (0, 6) or (index % 7) in (0, 6)])
    factor = np.where((np.arange(7) == 0) | (np.arange(7) == 6), 2.0, 1.0)
    multiple = (factor[:, None, None] * factor[None, :, None] * factor[None, None, :]).reshape(-1)
    return surface, 1.0 / multiple


def cube_weights(weights_np):
    return (weights_np[:, None, None] * weights_np[None, :, None] * weights_np[None, None, :]).reshape(-1)


def derive(derivative, nodal_cube, axis_index):
    return jnp.einsum(EINSUM_FORMS[axis_index], derivative, nodal_cube, precision=lax.Precision.HIGHEST)


def to_grid(stored, slot_map):
    components, row_count = stored.shape[0], stored.shape[1]
    blocks = stored.reshape(components, row_count, SLABS * DOMAINS, E_DEV)
    arrival = jnp.argsort(slot_map.reshape(SLABS * DOMAINS, E_DEV), axis=1).astype(jnp.int32)
    indices = jnp.broadcast_to(arrival[None, None], blocks.shape)
    brick_field = jnp.take_along_axis(blocks, indices, axis=3)
    brick_field = brick_field.reshape(components, row_count, SLABS, DOMAINS, BX, BY, BZ).transpose(0, 1, 2, 4, 3, 5, 6)
    return brick_field.reshape(components, row_count, ELEMENTS)


def from_grid(grid_field, slot_map):
    components, row_count = grid_field.shape[0], grid_field.shape[1]
    brick_field = grid_field.reshape(components, row_count, SLABS, BX, DOMAINS, BY, BZ).transpose(0, 1, 2, 4, 3, 5, 6)
    brick_field = brick_field.reshape(components, row_count, SLABS * DOMAINS, E_DEV)
    indices = jnp.broadcast_to(slot_map.reshape(SLABS * DOMAINS, E_DEV).astype(jnp.int32)[None, None], brick_field.shape)
    return jnp.take_along_axis(brick_field, indices, axis=3).reshape(components, row_count, ELEMENTS)


def assemble_grid(grid_field):
    components = grid_field.shape[0]
    nodal_cube = grid_field.reshape(components, 7, 7, 7, SLABS * BX, DOMAINS * BY, BZ)
    for node_axis in (1, 2, 3):
        element_axis = node_axis + 3
        low_face = lax.slice_in_dim(nodal_cube, 0, 1, axis=node_axis)
        high_face = lax.slice_in_dim(nodal_cube, 6, 7, axis=node_axis)
        middle = lax.slice_in_dim(nodal_cube, 1, 6, axis=node_axis)
        nodal_cube = jnp.concatenate([low_face + jnp.roll(high_face, 1, axis=element_axis), middle, high_face + jnp.roll(low_face, -1, axis=element_axis)], axis=node_axis)
    return nodal_cube.reshape(grid_field.shape)


def reference(velocity, slot_map, class_index, schur_blocks):
    derivative_np, weights_np = gll_tables()
    surface, inverse_np = shell_tables()
    derivative = jnp.asarray(derivative_np, jnp.float32)
    quadrature = jnp.asarray(cube_weights(weights_np), jnp.float32)
    full_weight = jnp.asarray(inverse_np, jnp.float32)
    shell_weight = jnp.asarray(inverse_np[surface], jnp.float32)

    grid_vel = to_grid(velocity, slot_map)
    nodal_cube = grid_vel.reshape(3, 7, 7, 7, ELEMENTS)
    advect = nodal_cube[0] * derive(derivative, nodal_cube, 0) + nodal_cube[1] * derive(derivative, nodal_cube, 1) + nodal_cube[2] * derive(derivative, nodal_cube, 2)
    averaged = assemble_grid(advect.reshape(3, NODES, ELEMENTS)) * full_weight[:, None]
    intermediate = (grid_vel - DELTA_T * averaged).reshape(3, 7, 7, 7, ELEMENTS)
    diverge = derive(derivative, intermediate[0:1], 0) + derive(derivative, intermediate[1:2], 1) + derive(derivative, intermediate[2:3], 2)
    source = (-1.0 / DELTA_T) * quadrature[:, None] * diverge.reshape(NODES, ELEMENTS)
    pressure_load = jnp.take(assemble_grid(source[None])[0], surface, axis=0)

    class_grid = to_grid(class_index.reshape(1, 1, ELEMENTS), slot_map).reshape(ELEMENTS)
    class_order = jnp.argsort(class_grid, stable=True).astype(jnp.int32)
    restore = jnp.argsort(class_order).astype(jnp.int32)

    def operate(vector):
        grouped = jnp.take(vector, class_order, axis=1).reshape(MODES, CLASSES, ELEMENTS // CLASSES)
        product = jnp.einsum('cij,jcn->icn', schur_blocks, grouped, precision=lax.Precision.HIGHEST)
        element_out = jnp.take(product.reshape(MODES, ELEMENTS), restore, axis=1)
        padded = jnp.zeros((1, NODES, ELEMENTS), jnp.float32).at[0, surface].set(element_out)
        return jnp.take(assemble_grid(padded)[0], surface, axis=0)

    def weighted(first_vec, second_vec):
        return jnp.sum(first_vec * second_vec * shell_weight[:, None])

    solution = jnp.zeros_like(pressure_load)
    residual = pressure_load
    direction = pressure_load
    current = weighted(residual, residual)
    for iteration in range(ITERS):
        applied = operate(direction)
        step_size = current / weighted(direction, applied)
        solution = solution + step_size * direction
        residual = residual - step_size * applied
        if iteration + 1 < ITERS:
            following = weighted(residual, residual)
            direction = residual + (following / current) * direction
            current = following
    return from_grid(solution[None], slot_map)[0], from_grid(residual[None], slot_map)[0]
```

```python
import functools

import jax
import jax.numpy as jnp
import numpy as np
from jax import lax
from jax.experimental import pallas as pl
from jax.experimental.pallas import tpu as pltpu
from jax.sharding import PartitionSpec as P

CLASSES = 16
MODES = 218
NODES = 343
LANES = 128
BZ = 16
BY = 8
DELTA_T = 0.05
HIGH = lax.Precision.HIGHEST
F32 = jnp.float32


def gll_tables():
    degree = 6
    outer_point = 0.830223896278567
    inner_point = 0.46884879347071423
    points = np.array([-1.0, -outer_point, -inner_point, 0.0, inner_point, outer_point, 1.0])
    values = (231.0 * points**6 - 315.0 * points**4 + 105.0 * points**2 - 5.0) / 16.0
    weights = 2.0 / (degree * (degree + 1) * values**2)
    derivative = np.zeros((7, 7))
    for target in range(7):
        for source in range(7):
            if target != source:
                derivative[target, source] = values[target] / (
                    values[source] * (points[target] - points[source])
                )
    derivative[0, 0] = -degree * (degree + 1) / 4.0
    derivative[6, 6] = degree * (degree + 1) / 4.0
    return derivative, weights


DERIV, WEIGHTS = gll_tables()
FACTOR = np.where((np.arange(7) == 0) | (np.arange(7) == 6), 2.0, 1.0)


def shell_runs():
    runs, offset = [], 0
    for a in range(7):
        for b in range(7):
            base = 8 * (7 * a + b)
            if a in (0, 6) or b in (0, 6):
                runs.append((offset, base, 7))
                offset += 7
            else:
                runs.append((offset, base, 1))
                runs.append((offset + 1, base + 6, 1))
                offset += 2
    return runs


RUNS = shell_runs()


def constant_tables():
    rolls = np.zeros((8, 8, LANES))
    for shift in range(8):
        for target in range(7):
            source = (target - shift) % 8
            if source < 7:
                rolls[shift, target] = DERIV[target, source]
    span = np.zeros((2, 8, LANES))
    span[0, :7] = WEIGHTS[:, None]
    span[1, :7] = 1.0 / FACTOR[:, None]
    multiple = (FACTOR[:, None, None] * FACTOR[None, :, None] * FACTOR[None, None, :]).reshape(-1)
    surface = [
        i for i in range(NODES) if i // 49 in (0, 6) or i // 7 % 7 in (0, 6) or i % 7 in (0, 6)
    ]
    shell = np.zeros((224, LANES))
    shell[:MODES] = (1.0 / multiple[surface])[:, None]
    return rolls.astype(np.float32), span.astype(np.float32), shell.astype(np.float32)


ROLLS, SPAN, SHELL = constant_tables()


def iotas(shape):
    lane = lax.broadcasted_iota(jnp.int32, shape, len(shape) - 1)
    node = lax.broadcasted_iota(jnp.int32, shape, len(shape) - 2)
    return lane % BZ, lane // BZ, node


def join_local(sheet):
    bz, by, node = iotas(sheet.shape)
    low = pltpu.roll(sheet, 2, 1)
    low = jnp.where(bz == 0, pltpu.roll(low, LANES - 15, 2), pltpu.roll(low, 1, 2))
    high = pltpu.roll(sheet, 6, 1)
    high = jnp.where(bz == BZ - 1, pltpu.roll(high, 15, 2), pltpu.roll(high, LANES - 1, 2))
    sheet = sheet + jnp.where(node == 0, low, jnp.where(node == 6, high, 0.0))
    first, last = sheet[0], sheet[6]
    first_by = by[0]
    new_first = first + jnp.where(first_by > 0, pltpu.roll(last, BZ, 1), 0.0)
    new_last = last + jnp.where(first_by < BY - 1, pltpu.roll(first, LANES - BZ, 1), 0.0)
    return jnp.concatenate([new_first[None], sheet[1:6], new_last[None]], axis=0)


def add_received(a, sheet, low_x, high_x, low_y, high_y):
    if a == 0:
        sheet = sheet + low_x
    if a == 6:
        sheet = sheet + high_x
    _, by, _ = iotas(sheet.shape[1:])
    first = sheet[0] + jnp.where(by == 0, low_y, 0.0)
    last = sheet[6] + jnp.where(by == BY - 1, high_y, 0.0)
    return jnp.concatenate([first[None], sheet[1:6], last[None]], axis=0)


def derive_sheets(sheets, target):
    total = float(DERIV[target, 0]) * sheets[0]
    for source in range(1, 7):
        total = total + float(DERIV[target, source]) * sheets[source]
    return total


def derive_span(rolls_ref, sheet):
    total = rolls_ref[0] * sheet
    for shift in range(1, 8):
        total = total + rolls_ref[shift] * pltpu.roll(sheet, shift, 1)
    return total


def permutation(slot_ref):
    position = lax.broadcasted_iota(jnp.int32, (LANES, LANES), 0)
    return jnp.where(position == slot_ref[...], 1.0, 0.0).astype(F32)


def emit_faces(part_ref, up_ref, down_ref, index):
    up_ref[index] = part_ref[index, 6]
    down_ref[index] = part_ref[index, 0]


def advect_kernel(vel_ref, slot_ref, class_ref, rolls_ref, brick_ref, part_ref, up_ref, down_ref, class_out):
    one_hot = permutation(slot_ref)
    nt = (((1,), (1,)), ((), ()))
    class_out[...] = lax.dot_general(
        jnp.broadcast_to(class_ref[...].astype(F32), (8, LANES)), one_hot, nt, precision=HIGH
    )
    for i in range(3):
        moved = lax.dot_general(vel_ref[i], one_hot, nt, precision=HIGH, preferred_element_type=F32)
        brick_ref[i] = jnp.zeros((7, 7, 8, LANES), F32)
        for a in range(7):
            for b in range(7):
                row = 7 * (7 * a + b)
                brick_ref[i, a, b, 0:7, :] = moved[row : row + 7]

    def component(i, carry):
        sheets = [brick_ref[i, a] for a in range(7)]
        for a in range(7):
            along_a = derive_sheets(sheets, a)
            sheet = sheets[a]
            along_b = jnp.stack(
                [derive_sheets([sheet[b] for b in range(7)], target) for target in range(7)], axis=0
            )
            along_c = derive_span(rolls_ref, sheet)
            advect = (
                brick_ref[0, a] * along_a + brick_ref[1, a] * along_b + brick_ref[2, a] * along_c
            )
            part_ref[i, a] = join_local(advect)
        emit_faces(part_ref, up_ref, down_ref, i)
        return carry

    lax.fori_loop(0, 3, component, 0)


def side_kernel(part_ref, low_x_ref, high_x_ref, up_ref, down_ref):
    for i in range(part_ref.shape[0]):
        for a in range(7):
            first, last = part_ref[i, a, 0], part_ref[i, a, 6]
            if a == 0:
                first, last = first + low_x_ref[i, 0], last + low_x_ref[i, 6]
            if a == 6:
                first, last = first + high_x_ref[i, 0], last + high_x_ref[i, 6]
            up_ref[i, a] = pltpu.roll(last, BZ, 1)
            down_ref[i, a] = pltpu.roll(first, LANES - BZ, 1)


def source_kernel(
    part_ref, low_x_ref, high_x_ref, low_y_ref, high_y_ref, brick_ref, rolls_ref, span_ref,
    out_ref, up_ref, down_ref, middle_ref,
):
    for i in range(3):
        for a in range(7):
            sheet = add_received(
                a, part_ref[i, a], low_x_ref[i], high_x_ref[i], low_y_ref[i, a], high_y_ref[i, a]
            )
            scaled = [
                sheet[b] * (span_ref[1] * float(DELTA_T / (FACTOR[a] * FACTOR[b]))) for b in range(7)
            ]
            middle_ref[i, a] = brick_ref[i, a] - jnp.stack(scaled, axis=0)
    sheets = [middle_ref[0, a] for a in range(7)]
    for a in range(7):
        along_a = derive_sheets(sheets, a)
        second = middle_ref[1, a]
        along_b = jnp.stack(
            [derive_sheets([second[b] for b in range(7)], target) for target in range(7)], axis=0
        )
        diverge = along_a + along_b + derive_span(rolls_ref, middle_ref[2, a])
        source = [
            diverge[b] * (span_ref[0] * float(-1.0 / DELTA_T * WEIGHTS[a] * WEIGHTS[b]))
            for b in range(7)
        ]
        out_ref[0, a] = join_local(jnp.stack(source, axis=0))
    emit_faces(out_ref, up_ref, down_ref, 0)


def gather_modes(part_ref, low_x_ref, high_x_ref, low_y_ref, high_y_ref, full_ref, modes_ref):
    for a in range(7):
        sheet = add_received(
            a, part_ref[0, a], low_x_ref[0], high_x_ref[0], low_y_ref[0, a], high_y_ref[0, a]
        )
        full_ref[56 * a : 56 * a + 56] = sheet.reshape(56, LANES)
    modes_ref[216:224] = jnp.zeros((8, LANES), F32)
    for compact, padded, rows in RUNS:
        modes_ref[compact : compact + rows] = full_ref[padded : padded + rows]


def multiply_blocks(schur_ref, class_ref, modes_ref, image_ref):
    mine = class_ref[0:1, :]
    modes = modes_ref[0:MODES]
    total = jnp.zeros((MODES, LANES), F32)
    for c in range(CLASSES):
        chosen = jnp.where(jnp.abs(mine - float(c)) < 0.5, modes, 0.0)
        total = total + jnp.dot(schur_ref[c], chosen, precision=HIGH, preferred_element_type=F32)
    image_ref[0:MODES] = total
    image_ref[MODES:224] = jnp.zeros((224 - MODES, LANES), F32)


def scatter_modes(image_ref, full_ref, out_ref, up_ref, down_ref):
    full_ref[...] = jnp.zeros((392, LANES), F32)
    for compact, padded, rows in RUNS:
        full_ref[padded : padded + rows] = image_ref[compact : compact + rows]
    for a in range(7):
        out_ref[0, a] = join_local(full_ref[56 * a : 56 * a + 56].reshape(7, 8, LANES))
    emit_faces(out_ref, up_ref, down_ref, 0)


def total_of(values):
    return jnp.sum(jnp.sum(values, axis=0, keepdims=True), axis=1, keepdims=True)


def first_apply_kernel(
    part_ref, low_x_ref, high_x_ref, low_y_ref, high_y_ref, schur_ref, class_ref,
    load_ref, image_ref, out_ref, up_ref, down_ref, full_ref,
):
    gather_modes(part_ref, low_x_ref, high_x_ref, low_y_ref, high_y_ref, full_ref, load_ref)
    multiply_blocks(schur_ref, class_ref, load_ref, image_ref)
    scatter_modes(image_ref, full_ref, out_ref, up_ref, down_ref)


def second_apply_kernel(
    part_ref, low_x_ref, high_x_ref, low_y_ref, high_y_ref, schur_ref, class_ref, load_ref,
    first_ref, shell_ref, power_ref, dots_ref, out_ref, up_ref, down_ref, image_ref, full_ref,
):
    gather_modes(part_ref, low_x_ref, high_x_ref, low_y_ref, high_y_ref, full_ref, power_ref)
    multiply_blocks(schur_ref, class_ref, power_ref, image_ref)
    scatter_modes(image_ref, full_ref, out_ref, up_ref, down_ref)
    load, power, shell = load_ref[...], power_ref[...], shell_ref[...]
    first, image = first_ref[...], image_ref[...]
    lane = lax.broadcasted_iota(jnp.int32, (1, LANES), 1)
    dots = jnp.zeros((1, LANES), F32)
    values = (
        load * load * shell, load * first, power * power * shell, load * image, power * image
    )
    for k, value in enumerate(values):
        dots = dots + jnp.where(lane == k, total_of(value), 0.0)
    dots_ref[...] = dots


def finish_kernel(
    part_ref, low_x_ref, high_x_ref, low_y_ref, high_y_ref, load_ref, power_ref, dots_ref, slot_ref,
    pressure_ref, residual_ref, full_ref, modes_ref,
):
    gather_modes(part_ref, low_x_ref, high_x_ref, low_y_ref, high_y_ref, full_ref, modes_ref)
    dots = jnp.sum(dots_ref[...], axis=0)
    square, energy, power_square, cross, power_energy = (dots[:, k : k + 1] for k in range(5))
    step = square / energy
    fresh = square - 2.0 * step * energy + step * step * power_square
    ratio = fresh / square
    grow = 1.0 + ratio
    curvature = (
        grow * grow * energy
        - step * grow * (cross + power_square)
        + step * step * power_energy
    )
    second = fresh / curvature
    load, power, twice = load_ref[...], power_ref[...], modes_ref[...]
    pressure = step * load + second * (grow * load - step * power)
    residual = load - step * power - second * (grow * power - step * twice)
    one_hot = permutation(slot_ref)
    pressure_ref[...] = jnp.dot(pressure, one_hot, precision=HIGH, preferred_element_type=F32)[:MODES]
    residual_ref[...] = jnp.dot(residual, one_hot, precision=HIGH, preferred_element_type=F32)[:MODES]


def call(kernel, outs, args, scratch=(), name=None):
    vmem = pl.BlockSpec(memory_space=pltpu.VMEM)
    return pl.pallas_call(
        kernel,
        out_shape=tuple(jax.ShapeDtypeStruct(shape, F32) for shape in outs),
        in_specs=[vmem] * len(args),
        out_specs=tuple([vmem] * len(outs)),
        scratch_shapes=[pltpu.VMEM(shape, F32) for shape in scratch],
        compiler_params=pltpu.CompilerParams(vmem_limit_bytes=48 << 20),
        name=name,
    )(*args)


def ring(axis, upward, downward):
    count = lax.axis_size(axis)
    up = [(i, (i + 1) % count) for i in range(count)]
    down = [(j, i) for i, j in up]
    return lax.ppermute(upward, axis, up), lax.ppermute(downward, axis, down)


def exchange(part, upward, downward):
    low_x, high_x = ring("slab", upward, downward)
    k = part.shape[0]
    up, down = call(
        side_kernel, [(k, 7, 8, LANES)] * 2, (part, low_x, high_x), name="side"
    )
    low_y, high_y = ring("dom", up, down)
    return part, low_x, high_x, low_y, high_y


def gather_sum(row, axis):
    count = lax.axis_size(axis)
    return lax.all_to_all(jnp.broadcast_to(row[None], (count, 1, LANES)), axis, 0, 0)


def per_device(velocity, slot_map, class_index, schur_blocks):
    slots = slot_map.reshape(1, LANES)
    rolls, span, shell = jnp.asarray(ROLLS), jnp.asarray(SPAN), jnp.asarray(SHELL)
    face = (7, 8, LANES)
    whole = (7, 7, 8, LANES)
    modes = (224, LANES)
    brick, part, up, down, classes = call(
        advect_kernel,
        [(3, *whole), (3, *whole), (3, *face), (3, *face), (8, LANES)],
        (velocity, slots, class_index.reshape(1, LANES), rolls),
        name="advect",
    )
    part, up, down = call(
        source_kernel,
        [(1, *whole), (1, *face), (1, *face)],
        (*exchange(part, up, down), brick, rolls, span),
        [(3, *whole)],
        name="source",
    )
    load, first, part, up, down = call(
        first_apply_kernel,
        [modes, modes, (1, *whole), (1, *face), (1, *face)],
        (*exchange(part, up, down), schur_blocks, classes),
        [(392, LANES)],
        name="first",
    )
    power, dots, part, up, down = call(
        second_apply_kernel,
        [modes, (1, LANES), (1, *whole), (1, *face), (1, *face)],
        (*exchange(part, up, down), schur_blocks, classes, load, first, shell),
        [modes, (392, LANES)],
        name="second",
    )
    dots = gather_sum(dots, "dom").sum(axis=0)
    dots = gather_sum(dots, "slab")
    return call(
        finish_kernel,
        [(MODES, LANES), (MODES, LANES)],
        (*exchange(part, up, down), load, power, dots, slots),
        [(392, LANES), modes],
        name="finish",
    )


def solution(mesh):
    return jax.shard_map(
        per_device,
        mesh=mesh,
        in_specs=(
            P(None, None, ("slab", "dom")),
            P("slab", "dom", None),
            P("slab", "dom", None),
            P(),
        ),
        out_specs=(P(None, ("slab", "dom")), P(None, ("slab", "dom"))),
        check_vma=False,
    )
```

```python
import jax
import jax.numpy as jnp
import numpy as np
from jax import lax
from jax.experimental import pallas as pl
from jax.experimental.pallas import tpu as pltpu
from jax.sharding import PartitionSpec as P

CLASSES = 16
MODES = 218
NODES = 343
LANES = 128
BZ = 16
BY = 8
DELTA_T = 0.05
HIGH = lax.Precision.HIGHEST
F32 = jnp.float32


def gll_tables():
    degree = 6
    outer_point = 0.830223896278567
    inner_point = 0.46884879347071423
    points = np.array([-1.0, -outer_point, -inner_point, 0.0, inner_point, outer_point, 1.0])
    values = (231.0 * points**6 - 315.0 * points**4 + 105.0 * points**2 - 5.0) / 16.0
    weights = 2.0 / (degree * (degree + 1) * values**2)
    derivative = np.zeros((7, 7))
    for target in range(7):
        for source in range(7):
            if target != source:
                derivative[target, source] = values[target] / (
                    values[source] * (points[target] - points[source])
                )
    derivative[0, 0] = -degree * (degree + 1) / 4.0
    derivative[6, 6] = degree * (degree + 1) / 4.0
    return derivative, weights


DERIV, WEIGHTS = gll_tables()
FACTOR = np.where((np.arange(7) == 0) | (np.arange(7) == 6), 2.0, 1.0)


def shell_runs():
    runs, offset = [], 0
    for a in range(7):
        for b in range(7):
            base = 8 * (7 * a + b)
            if a in (0, 6) or b in (0, 6):
                runs.append((offset, base, 7))
                offset += 7
            else:
                runs.append((offset, base, 1))
                runs.append((offset + 1, base + 6, 1))
                offset += 2
    return runs


RUNS = shell_runs()


def shell_table():
    multiple = (FACTOR[:, None, None] * FACTOR[None, :, None] * FACTOR[None, None, :]).reshape(-1)
    surface = [
        i for i in range(NODES) if i // 49 in (0, 6) or i // 7 % 7 in (0, 6) or i % 7 in (0, 6)
    ]
    shell = np.zeros((224, LANES))
    shell[:MODES] = (1.0 / multiple[surface])[:, None]
    return shell.astype(np.float32)


SHELL = shell_table()


def span_vector(values):
    node = lax.broadcasted_iota(jnp.int32, (8, LANES), 0)
    table = jnp.zeros((8, LANES), F32)
    for c in range(7):
        table = jnp.where(node == c, float(values[c]), table)
    return table


def span_rolls():
    tables = []
    for shift in range(8):
        sources = [(target - shift) % 8 for target in range(7)]
        tables.append(
            span_vector([DERIV[t, c] if c < 7 else 0.0 for t, c in zip(range(7), sources)])
        )
    return tables


def even_place(axis, like):
    return jnp.full(like.shape, lax.axis_index(axis) % 2, jnp.int32) == 0


def lower_upper(axis, near, far):
    even = even_place(axis, near)
    return jnp.where(even, far, near), jnp.where(even, near, far)


def iotas(shape):
    lane = lax.broadcasted_iota(jnp.int32, shape, len(shape) - 1)
    node = lax.broadcasted_iota(jnp.int32, shape, len(shape) - 2)
    return lane % BZ, lane // BZ, node


def join_local(sheet):
    bz, by, node = iotas(sheet.shape)
    low = pltpu.roll(sheet, 2, 1)
    low = jnp.where(bz == 0, pltpu.roll(low, LANES - 15, 2), pltpu.roll(low, 1, 2))
    high = pltpu.roll(sheet, 6, 1)
    high = jnp.where(bz == BZ - 1, pltpu.roll(high, 15, 2), pltpu.roll(high, LANES - 1, 2))
    sheet = sheet + jnp.where(node == 0, low, jnp.where(node == 6, high, 0.0))
    first, last = sheet[0], sheet[6]
    first_by = by[0]
    new_first = first + jnp.where(first_by > 0, pltpu.roll(last, BZ, 1), 0.0)
    new_last = last + jnp.where(first_by < BY - 1, pltpu.roll(first, LANES - BZ, 1), 0.0)
    return jnp.concatenate([new_first[None], sheet[1:6], new_last[None]], axis=0)


def add_received(a, sheet, far_x, near_x, far_y, near_y):
    if a == 0:
        sheet = sheet + lower_upper("slab", near_x, far_x)[0]
    if a == 6:
        sheet = sheet + lower_upper("slab", near_x, far_x)[1]
    low_y, high_y = lower_upper("dom", near_y, far_y)
    _, by, _ = iotas(sheet.shape[1:])
    first = sheet[0] + jnp.where(by == 0, low_y, 0.0)
    last = sheet[6] + jnp.where(by == BY - 1, high_y, 0.0)
    return jnp.concatenate([first[None], sheet[1:6], last[None]], axis=0)


def derive_sheets(sheets, target):
    total = float(DERIV[target, 0]) * sheets[0]
    for source in range(1, 7):
        total = total + float(DERIV[target, source]) * sheets[source]
    return total


def derive_span(rolls, sheet):
    total = rolls[0] * sheet
    for shift in range(1, 8):
        total = total + rolls[shift] * pltpu.roll(sheet, shift, 1)
    return total


def permutation(slot_ref):
    position = lax.broadcasted_iota(jnp.int32, (LANES, LANES), 0)
    return jnp.where(position == slot_ref[...], 1.0, 0.0).astype(F32)


def emit_faces(part_ref, far_ref, near_ref, index):
    low, high = part_ref[index, 0], part_ref[index, 6]
    even = even_place("slab", low)
    far_ref[index] = jnp.where(even, low, high)
    near_ref[index] = jnp.where(even, high, low)


def advect_kernel(
    vel_hbm, slot_hbm, class_hbm,
    brick_ref, part_ref, far_ref, near_ref, class_out,
    vel_ref, slot_ref, class_ref, sems,
):
    copies = [
        pltpu.make_async_copy(src, dst, sems.at[k])
        for k, (src, dst) in enumerate(
            ((slot_hbm, slot_ref), (class_hbm, class_ref), (vel_hbm, vel_ref))
        )
    ]
    for copy in copies:
        copy.start()
    rolls = span_rolls()
    brick_ref[:, :, :, 7:8, :] = jnp.zeros((3, 7, 7, 1, LANES), F32)
    copies[0].wait()
    copies[1].wait()
    one_hot = permutation(slot_ref)
    nt = (((1,), (1,)), ((), ()))
    class_out[...] = lax.dot_general(
        jnp.broadcast_to(class_ref[...].astype(F32), (8, LANES)), one_hot, nt, precision=HIGH
    )
    copies[2].wait()
    for i in range(3):
        moved = lax.dot_general(vel_ref[i], one_hot, nt, precision=HIGH, preferred_element_type=F32)
        for a in range(7):
            for b in range(7):
                row = 7 * (7 * a + b)
                brick_ref[i, a, b, 0:7, :] = moved[row : row + 7]

    def component(i, carry):
        sheets = [brick_ref[i, a] for a in range(7)]
        for a in range(7):
            along_a = derive_sheets(sheets, a)
            sheet = sheets[a]
            along_b = jnp.stack(
                [derive_sheets([sheet[b] for b in range(7)], target) for target in range(7)], axis=0
            )
            along_c = derive_span(rolls, sheet)
            advect = (
                brick_ref[0, a] * along_a + brick_ref[1, a] * along_b + brick_ref[2, a] * along_c
            )
            part_ref[i, a] = join_local(advect)
        emit_faces(part_ref, far_ref, near_ref, i)
        return carry

    lax.fori_loop(0, 3, component, 0)


def side_kernel(part_ref, far_x_ref, near_x_ref, far_ref, near_ref):
    for i in range(part_ref.shape[0]):
        low_x, high_x = lower_upper("slab", near_x_ref[i], far_x_ref[i])
        for a in range(7):
            first, last = part_ref[i, a, 0], part_ref[i, a, 6]
            if a == 0:
                first, last = first + low_x[0], last + low_x[6]
            if a == 6:
                first, last = first + high_x[0], last + high_x[6]
            down, up = pltpu.roll(first, LANES - BZ, 1), pltpu.roll(last, BZ, 1)
            even = even_place("dom", up)
            far_ref[i, a] = jnp.where(even, down, up)
            near_ref[i, a] = jnp.where(even, up, down)


def source_kernel(
    part_ref, far_x_ref, near_x_ref, far_y_ref, near_y_ref, brick_ref,
    out_ref, far_ref, near_ref, middle_ref,
):
    rolls = span_rolls()
    weights = span_vector(WEIGHTS)
    inverse = span_vector(1.0 / FACTOR)
    for i in range(3):
        for a in range(7):
            sheet = add_received(
                a, part_ref[i, a], far_x_ref[i], near_x_ref[i], far_y_ref[i, a], near_y_ref[i, a]
            )
            scaled = [
                sheet[b] * (inverse * float(DELTA_T / (FACTOR[a] * FACTOR[b]))) for b in range(7)
            ]
            middle_ref[i, a] = brick_ref[i, a] - jnp.stack(scaled, axis=0)
    sheets = [middle_ref[0, a] for a in range(7)]
    for a in range(7):
        along_a = derive_sheets(sheets, a)
        second = middle_ref[1, a]
        along_b = jnp.stack(
            [derive_sheets([second[b] for b in range(7)], target) for target in range(7)], axis=0
        )
        diverge = along_a + along_b + derive_span(rolls, middle_ref[2, a])
        source = [
            diverge[b] * (weights * float(-1.0 / DELTA_T * WEIGHTS[a] * WEIGHTS[b]))
            for b in range(7)
        ]
        out_ref[0, a] = join_local(jnp.stack(source, axis=0))
    emit_faces(out_ref, far_ref, near_ref, 0)


def gather_modes(part_ref, far_x_ref, near_x_ref, far_y_ref, near_y_ref, full_ref, modes_ref):
    for a in range(7):
        sheet = add_received(
            a, part_ref[0, a], far_x_ref[0], near_x_ref[0], far_y_ref[0, a], near_y_ref[0, a]
        )
        full_ref[56 * a : 56 * a + 56] = sheet.reshape(56, LANES)
    modes_ref[216:224] = jnp.zeros((8, LANES), F32)
    for compact, padded, rows in RUNS:
        modes_ref[compact : compact + rows] = full_ref[padded : padded + rows]


STARTS = tuple(range(0, MODES, 32))


def block_copy(schur_hbm, schur_ref, sems, start):
    rows = pl.ds(CLASSES * start, CLASSES * min(32, MODES - start))
    return pltpu.make_async_copy(schur_hbm.at[rows], schur_ref.at[rows], sems.at[start // 32])


def start_blocks(schur_hbm, schur_ref, sems):
    for start in STARTS:
        block_copy(schur_hbm, schur_ref, sems, start).start()


def multiply_blocks(schur_hbm, schur_ref, sems, class_ref, modes_ref, image_ref):
    modes = modes_ref[0:MODES]
    row = lax.broadcasted_iota(jnp.int32, (CLASSES, LANES), 0).astype(F32)
    mine = jnp.where(jnp.abs(class_ref[0:1, :] - row) < 0.5, 1.0, 0.0)
    image_ref[216:224] = jnp.zeros((8, LANES), F32)
    for start in STARTS:
        count = min(32, MODES - start)
        block_copy(schur_hbm, schur_ref, sems, start).wait()
        block = schur_ref[CLASSES * start : CLASSES * (start + count)]
        every = jnp.dot(block, modes, precision=HIGH, preferred_element_type=F32)
        every = every.reshape(count, 2, 8, LANES) * mine.reshape(2, 8, LANES)
        image_ref[start : start + count] = jnp.sum(every[:, 0] + every[:, 1], axis=1)


def scatter_modes(image_ref, full_ref, out_ref, far_ref, near_ref):
    full_ref[...] = jnp.zeros((392, LANES), F32)
    for compact, padded, rows in RUNS:
        full_ref[padded : padded + rows] = image_ref[compact : compact + rows]
    for a in range(7):
        out_ref[0, a] = join_local(full_ref[56 * a : 56 * a + 56].reshape(7, 8, LANES))
    emit_faces(out_ref, far_ref, near_ref, 0)


def total_of(values):
    return jnp.sum(jnp.sum(values, axis=0, keepdims=True), axis=1, keepdims=True)


def first_apply_kernel(
    part_ref, far_x_ref, near_x_ref, far_y_ref, near_y_ref, schur_hbm, class_ref,
    load_ref, image_ref, out_ref, far_ref, near_ref, full_ref, schur_ref, sems,
):
    start_blocks(schur_hbm, schur_ref, sems)
    gather_modes(part_ref, far_x_ref, near_x_ref, far_y_ref, near_y_ref, full_ref, load_ref)
    multiply_blocks(schur_hbm, schur_ref, sems, class_ref, load_ref, image_ref)
    scatter_modes(image_ref, full_ref, out_ref, far_ref, near_ref)


def second_apply_kernel(
    part_ref, far_x_ref, near_x_ref, far_y_ref, near_y_ref, schur_hbm, class_ref, load_ref,
    first_ref, shell_ref, power_ref, dots_ref, out_ref, far_ref, near_ref, image_ref, full_ref, schur_ref,
    sems,
):
    start_blocks(schur_hbm, schur_ref, sems)
    gather_modes(part_ref, far_x_ref, near_x_ref, far_y_ref, near_y_ref, full_ref, power_ref)
    multiply_blocks(schur_hbm, schur_ref, sems, class_ref, power_ref, image_ref)
    scatter_modes(image_ref, full_ref, out_ref, far_ref, near_ref)
    load, power, shell = load_ref[...], power_ref[...], shell_ref[...]
    first, image = first_ref[...], image_ref[...]
    lane = lax.broadcasted_iota(jnp.int32, (1, LANES), 1)
    dots = jnp.zeros((1, LANES), F32)
    values = (
        load * load * shell, load * first, power * power * shell, load * image, power * image
    )
    for k, value in enumerate(values):
        dots = dots + jnp.where(lane == k, total_of(value), 0.0)
    dots_ref[...] = dots


def finish_kernel(
    part_ref, far_x_ref, near_x_ref, far_y_ref, near_y_ref, load_ref, power_ref, dots_ref, slot_ref,
    pressure_ref, residual_ref, full_ref, modes_ref,
):
    gather_modes(part_ref, far_x_ref, near_x_ref, far_y_ref, near_y_ref, full_ref, modes_ref)
    dots = jnp.sum(dots_ref[...], axis=0, keepdims=True)
    square, energy, power_square, cross, power_energy = (dots[:, k : k + 1] for k in range(5))
    step = square / energy
    fresh = square - 2.0 * step * energy + step * step * power_square
    ratio = fresh / square
    grow = 1.0 + ratio
    curvature = (
        grow * grow * energy
        - step * grow * (cross + power_square)
        + step * step * power_energy
    )
    second = fresh / curvature
    load, power, twice = load_ref[...], power_ref[...], modes_ref[...]
    pressure = step * load + second * (grow * load - step * power)
    residual = load - step * power - second * (grow * power - step * twice)
    one_hot = permutation(slot_ref)
    pressure_ref[...] = jnp.dot(pressure, one_hot, precision=HIGH, preferred_element_type=F32)[:MODES]
    residual_ref[...] = jnp.dot(residual, one_hot, precision=HIGH, preferred_element_type=F32)[:MODES]


def call(kernel, outs, args, scratch=(), name=None, hbm=()):
    vmem = pl.BlockSpec(memory_space=pltpu.VMEM)
    places = [pl.BlockSpec(memory_space=pltpu.HBM) if k in hbm else vmem for k in range(len(args))]
    args = [
        pltpu.with_memory_space_constraint(x, pltpu.HBM) if k in hbm else x
        for k, x in enumerate(args)
    ]
    return pl.pallas_call(
        kernel,
        out_shape=tuple(jax.ShapeDtypeStruct(shape, F32) for shape in outs),
        in_specs=places,
        out_specs=tuple([vmem] * len(outs)),
        scratch_shapes=[pltpu.VMEM(s, F32) if isinstance(s, tuple) else s for s in scratch],
        compiler_params=pltpu.CompilerParams(vmem_limit_bytes=48 << 20),
        name=name,
    )(*args)


def partners(axis):
    count = lax.axis_size(axis)
    far = [(i, (i + 1) % count if i % 2 else (i - 1) % count) for i in range(count)]
    near = [(i, i ^ 1) for i in range(count)]
    return far, near


def swap(axis, far, near):
    far_pairs, near_pairs = partners(axis)
    return lax.ppermute(far, axis, far_pairs), lax.ppermute(near, axis, near_pairs)


def exchange(part, far, near, dots=None):
    far_x, near_x = swap("slab", far, near)
    k = part.shape[0]
    if dots is not None:
        inner, outer = reduction_groups()
        rows = gather_parts(dots, inner)
        far_x, near_x, rows = lax.optimization_barrier((far_x, near_x, rows))
        rows = gather_parts(rows.sum(axis=0), outer).reshape(-1, LANES)
    far, near = call(side_kernel, [(k, 7, 8, LANES)] * 2, (part, far_x, near_x), name="side")
    received = part, far_x, near_x, *swap("dom", far, near)
    return received if dots is None else (received, rows)


def gather_parts(row, groups):
    count = len(groups[0])
    spread = jnp.broadcast_to(row.reshape(1, 1, LANES), (count, 1, LANES))
    return lax.all_to_all(spread, ("slab", "dom"), 0, 0, axis_index_groups=groups)


def reduction_groups():
    slabs, doms = lax.axis_size("slab"), lax.axis_size("dom")
    run = min(8, doms)
    total = slabs * doms
    inner = [list(range(i, i + run)) for i in range(0, total, run)]
    outer = [list(range(k, total, run)) for k in range(run)]
    return inner, outer


def per_device(velocity, slot_map, class_index, schur_blocks):
    slots = slot_map.reshape(1, LANES)
    shell = jnp.asarray(SHELL)
    schur = schur_blocks.transpose(1, 0, 2).reshape(MODES * CLASSES, MODES)
    face = (7, 8, LANES)
    whole = (7, 7, 8, LANES)
    modes = (224, LANES)
    blocks = [(MODES * CLASSES, MODES), pltpu.SemaphoreType.DMA((len(STARTS),))]
    brick, part, far, near, classes = call(
        advect_kernel,
        [(3, *whole), (3, *whole), (3, *face), (3, *face), (8, LANES)],
        (velocity, slots, class_index.reshape(1, LANES)),
        [
            (3, NODES, LANES),
            pltpu.VMEM((1, LANES), jnp.int32),
            pltpu.VMEM((1, LANES), jnp.int32),
            pltpu.SemaphoreType.DMA((3,)),
        ],
        name="advect",
        hbm=(0, 1, 2),
    )
    part, far, near = call(
        source_kernel,
        [(1, *whole), (1, *face), (1, *face)],
        (*exchange(part, far, near), brick),
        [(3, *whole)],
        name="source",
    )
    load, first, part, far, near = call(
        first_apply_kernel,
        [modes, modes, (1, *whole), (1, *face), (1, *face)],
        (*exchange(part, far, near), schur, classes),
        [(392, LANES), *blocks],
        name="first",
        hbm=(5,),
    )
    power, dots, part, far, near = call(
        second_apply_kernel,
        [modes, (1, LANES), (1, *whole), (1, *face), (1, *face)],
        (*exchange(part, far, near), schur, classes, load, first, shell),
        [modes, (392, LANES), *blocks],
        name="second",
        hbm=(5,),
    )
    received, rows = exchange(part, far, near, dots)
    return call(
        finish_kernel,
        [(MODES, LANES), (MODES, LANES)],
        (*received, load, power, rows, slots),
        [(392, LANES), modes],
        name="finish",
    )


def solution(mesh):
    return jax.shard_map(
        per_device,
        mesh=mesh,
        in_specs=(
            P(None, None, ("slab", "dom")),
            P("slab", "dom", None),
            P("slab", "dom", None),
            P(),
        ),
        out_specs=(P(None, ("slab", "dom")), P(None, ("slab", "dom"))),
        check_vma=False,
    )
```

```python
import jax
import jax.numpy as jnp
import numpy as np
from jax import lax
from jax.experimental import pallas as pl
from jax.experimental.pallas import tpu as pltpu
from jax.sharding import PartitionSpec as P

CLASSES = 16
MODES = 218
NODES = 343
LANES = 128
BZ = 16
BY = 8
DELTA_T = 0.05
F32 = jnp.float32
BF16 = jnp.bfloat16


def gll_tables():
    degree = 6
    outer_point = 0.830223896278567
    inner_point = 0.46884879347071423
    points = np.array([-1.0, -outer_point, -inner_point, 0.0, inner_point, outer_point, 1.0])
    values = (231.0 * points**6 - 315.0 * points**4 + 105.0 * points**2 - 5.0) / 16.0
    weights = 2.0 / (degree * (degree + 1) * values**2)
    derivative = np.zeros((7, 7))
    for target in range(7):
        for source in range(7):
            if target != source:
                derivative[target, source] = values[target] / (
                    values[source] * (points[target] - points[source])
                )
    derivative[0, 0] = -degree * (degree + 1) / 4.0
    derivative[6, 6] = degree * (degree + 1) / 4.0
    return derivative, weights


DERIV, WEIGHTS = gll_tables()
FACTOR = np.where((np.arange(7) == 0) | (np.arange(7) == 6), 2.0, 1.0)


def shell_runs():
    runs, offset = [], 0
    for a in range(7):
        for b in range(7):
            base = 8 * (7 * a + b)
            if a in (0, 6) or b in (0, 6):
                runs.append((offset, base, 7))
                offset += 7
            else:
                runs.append((offset, base, 1))
                runs.append((offset + 1, base + 6, 1))
                offset += 2
    return runs


RUNS = shell_runs()


def shell_table():
    multiple = (FACTOR[:, None, None] * FACTOR[None, :, None] * FACTOR[None, None, :]).reshape(-1)
    surface = [
        i for i in range(NODES) if i // 49 in (0, 6) or i // 7 % 7 in (0, 6) or i % 7 in (0, 6)
    ]
    shell = np.zeros((224, LANES))
    shell[:MODES] = (1.0 / multiple[surface])[:, None]
    return shell.astype(np.float32)


SHELL = shell_table()


def span_vector(values):
    node = lax.broadcasted_iota(jnp.int32, (8, LANES), 0)
    table = jnp.zeros((8, LANES), F32)
    for c in range(7):
        table = jnp.where(node == c, float(values[c]), table)
    return table


def span_rolls():
    tables = []
    for shift in range(8):
        sources = [(target - shift) % 8 for target in range(7)]
        tables.append(
            span_vector([DERIV[t, c] if c < 7 else 0.0 for t, c in zip(range(7), sources)])
        )
    return tables


def even_place(axis, like):
    return jnp.full(like.shape, lax.axis_index(axis) % 2, jnp.int32) == 0


def lower_upper(axis, near, far):
    even = even_place(axis, near)
    return jnp.where(even, far, near), jnp.where(even, near, far)


def iotas(shape):
    lane = lax.broadcasted_iota(jnp.int32, shape, len(shape) - 1)
    node = lax.broadcasted_iota(jnp.int32, shape, len(shape) - 2)
    return lane % BZ, lane // BZ, node


def join_local(sheet):
    bz, by, node = iotas(sheet.shape)
    low = pltpu.roll(sheet, 2, 1)
    low = jnp.where(bz == 0, pltpu.roll(low, LANES - 15, 2), pltpu.roll(low, 1, 2))
    high = pltpu.roll(sheet, 6, 1)
    high = jnp.where(bz == BZ - 1, pltpu.roll(high, 15, 2), pltpu.roll(high, LANES - 1, 2))
    sheet = sheet + jnp.where(node == 0, low, jnp.where(node == 6, high, 0.0))
    first, last = sheet[0], sheet[6]
    first_by = by[0]
    new_first = first + jnp.where(first_by > 0, pltpu.roll(last, BZ, 1), 0.0)
    new_last = last + jnp.where(first_by < BY - 1, pltpu.roll(first, LANES - BZ, 1), 0.0)
    return jnp.concatenate([new_first[None], sheet[1:6], new_last[None]], axis=0)


def add_received(a, sheet, far_x, near_x, far_y, near_y):
    if a == 0:
        sheet = sheet + lower_upper("slab", near_x, far_x)[0]
    if a == 6:
        sheet = sheet + lower_upper("slab", near_x, far_x)[1]
    low_y, high_y = lower_upper("dom", near_y, far_y)
    _, by, _ = iotas(sheet.shape[1:])
    first = sheet[0] + jnp.where(by == 0, low_y, 0.0)
    last = sheet[6] + jnp.where(by == BY - 1, high_y, 0.0)
    return jnp.concatenate([first[None], sheet[1:6], last[None]], axis=0)


def derive_sheets(sheets, target):
    total = float(DERIV[target, 0]) * sheets[0]
    for source in range(1, 7):
        total = total + float(DERIV[target, source]) * sheets[source]
    return total


def derive_span(rolls, sheet):
    total = rolls[0] * sheet
    for shift in range(1, 8):
        total = total + rolls[shift] * pltpu.roll(sheet, shift, 1)
    return total


def permutation(slot_ref):
    position = lax.broadcasted_iota(jnp.int32, (LANES, LANES), 0)
    return jnp.where(position == slot_ref[...], 1.0, 0.0).astype(BF16)


def moved(values, one_hot, dims):
    return sum(
        lax.dot_general(term, one_hot, (dims, ((), ())), preferred_element_type=F32)
        for term in terms(values)
    )


TO_BRICK = ((1,), (1,))
TO_STORED = ((1,), (0,))


def emit_faces(part_ref, far_ref, near_ref, index):
    low, high = part_ref[index, 0], part_ref[index, 6]
    even = even_place("slab", low)
    far_ref[index] = jnp.where(even, low, high)
    near_ref[index] = jnp.where(even, high, low)


def advect_kernel(
    vel_hbm, slot_hbm, class_hbm,
    brick_ref, part_ref, far_ref, near_ref, class_out,
    vel_ref, slot_ref, class_ref, sems,
):
    copies = [
        pltpu.make_async_copy(src, dst, sems.at[k])
        for k, (src, dst) in enumerate(
            (
                (slot_hbm, slot_ref), (class_hbm, class_ref),
                *((vel_hbm.at[i], vel_ref.at[i]) for i in range(3)),
            )
        )
    ]
    for copy in copies:
        copy.start()
    rolls = span_rolls()
    brick_ref[:, :, :, 7:8, :] = jnp.zeros((3, 7, 7, 1, LANES), F32)
    copies[0].wait()
    copies[1].wait()
    one_hot = permutation(slot_ref)
    class_out[...] = moved(
        jnp.broadcast_to(class_ref[...].astype(F32), (8, LANES)), one_hot, TO_BRICK
    )
    for i in range(3):
        copies[2 + i].wait()
        stored = moved(vel_ref[i], one_hot, TO_BRICK)
        for a in range(7):
            for b in range(7):
                row = 7 * (7 * a + b)
                brick_ref[i, a, b, 0:7, :] = stored[row : row + 7]

    def component(i, carry):
        sheets = [brick_ref[i, a] for a in range(7)]
        for a in range(7):
            along_a = derive_sheets(sheets, a)
            sheet = sheets[a]
            along_b = jnp.stack(
                [derive_sheets([sheet[b] for b in range(7)], target) for target in range(7)], axis=0
            )
            along_c = derive_span(rolls, sheet)
            advect = (
                brick_ref[0, a] * along_a + brick_ref[1, a] * along_b + brick_ref[2, a] * along_c
            )
            part_ref[i, a] = join_local(advect)
        emit_faces(part_ref, far_ref, near_ref, i)
        return carry

    lax.fori_loop(0, 3, component, 0)


def side_kernel(part_ref, far_x_ref, near_x_ref, far_ref, near_ref):
    for i in range(part_ref.shape[0]):
        low_x, high_x = lower_upper("slab", near_x_ref[i], far_x_ref[i])
        for a in range(7):
            first, last = part_ref[i, a, 0], part_ref[i, a, 6]
            if a == 0:
                first, last = first + low_x[0], last + low_x[6]
            if a == 6:
                first, last = first + high_x[0], last + high_x[6]
            down, up = pltpu.roll(first, LANES - BZ, 1), pltpu.roll(last, BZ, 1)
            even = even_place("dom", up)
            far_ref[i, a] = jnp.where(even, down, up)
            near_ref[i, a] = jnp.where(even, up, down)


def source_kernel(
    part_ref, far_x_ref, near_x_ref, far_y_ref, near_y_ref, brick_ref,
    out_ref, far_ref, near_ref, middle_ref,
):
    rolls = span_rolls()
    weights = span_vector(WEIGHTS)
    inverse = span_vector(1.0 / FACTOR)
    for i in range(3):
        for a in range(7):
            sheet = add_received(
                a, part_ref[i, a], far_x_ref[i], near_x_ref[i], far_y_ref[i, a], near_y_ref[i, a]
            )
            scaled = [
                sheet[b] * (inverse * float(DELTA_T / (FACTOR[a] * FACTOR[b]))) for b in range(7)
            ]
            middle_ref[i, a] = brick_ref[i, a] - jnp.stack(scaled, axis=0)
    sheets = [middle_ref[0, a] for a in range(7)]
    for a in range(7):
        along_a = derive_sheets(sheets, a)
        second = middle_ref[1, a]
        along_b = jnp.stack(
            [derive_sheets([second[b] for b in range(7)], target) for target in range(7)], axis=0
        )
        diverge = along_a + along_b + derive_span(rolls, middle_ref[2, a])
        source = [
            diverge[b] * (weights * float(-1.0 / DELTA_T * WEIGHTS[a] * WEIGHTS[b]))
            for b in range(7)
        ]
        out_ref[0, a] = join_local(jnp.stack(source, axis=0))
    emit_faces(out_ref, far_ref, near_ref, 0)


def gather_modes(part_ref, far_x_ref, near_x_ref, far_y_ref, near_y_ref, full_ref, modes_ref):
    for a in range(7):
        sheet = add_received(
            a, part_ref[0, a], far_x_ref[0], near_x_ref[0], far_y_ref[0, a], near_y_ref[0, a]
        )
        full_ref[56 * a : 56 * a + 56] = sheet.reshape(56, LANES)
    modes_ref[216:224] = jnp.zeros((8, LANES), F32)
    for compact, padded, rows in RUNS:
        modes_ref[compact : compact + rows] = full_ref[padded : padded + rows]


def terms(values):
    high = values.astype(BF16)
    rest = values - high.astype(F32)
    middle = rest.astype(BF16)
    return high, middle, (rest - middle.astype(F32)).astype(BF16)


def split_kernel(schur_hbm, split_ref, schur_ref, left_ref, right_ref, sems):
    parts = 2
    size = MODES * CLASSES // parts
    copies = [
        pltpu.make_async_copy(
            schur_hbm.at[pl.ds(size * k, size)], schur_ref.at[pl.ds(size * k, size)], sems.at[k]
        )
        for k in range(parts)
    ]
    for copy in copies:
        copy.start()
    for k in range(3):
        split_ref[224 * k + 208 : 224 * k + 224] = jnp.zeros((16, 256 * CLASSES), BF16)
    right_ref[...] = jnp.zeros(right_ref.shape, F32)
    for copy in copies:
        copy.wait()
    left_ref[...] = schur_ref[:, :LANES]
    right_ref[:, : MODES - LANES] = schur_ref[:, LANES:]
    for c in range(CLASSES):
        for half, half_ref in enumerate((left_ref, right_ref)):
            block = half_ref[pl.ds(c, MODES, stride=CLASSES), :]
            place = LANES * (2 * c + half)
            for k, term in enumerate(terms(block)):
                split_ref[224 * k : 224 * k + MODES, place : place + LANES] = term


def multiply_blocks(split_ref, class_ref, modes_ref, image_ref, right_ref, last_ref):
    high, middle, low = terms(modes_ref[...])
    pair = jnp.concatenate([high, middle], axis=1)
    zeros = jnp.zeros((32, 2 * LANES), BF16)
    mine = class_ref[0:1, :]
    for c in range(CLASSES):
        chosen = jnp.where(jnp.abs(mine - float(c)) < 0.5, 1.0, 0.0).astype(BF16)
        right_ref[256 * c : 256 * c + 224] = pair * jnp.concatenate([chosen, chosen], axis=1)
        right_ref[256 * c + 224 : 256 * c + 256] = zeros
        last_ref[256 * c : 256 * c + 224] = low * chosen
        last_ref[256 * c + 224 : 256 * c + 256] = zeros[:, :LANES]
    total = jnp.dot(split_ref[...], right_ref[...], preferred_element_type=F32)
    total = total[:, :LANES] + total[:, LANES:]
    small = jnp.dot(split_ref[0:224], last_ref[...], preferred_element_type=F32)
    image_ref[...] = total[0:224] + (total[224:448] + (total[448:672] + small))


def scatter_modes(image_ref, full_ref, out_ref, far_ref, near_ref):
    full_ref[...] = jnp.zeros((392, LANES), F32)
    for compact, padded, rows in RUNS:
        full_ref[padded : padded + rows] = image_ref[compact : compact + rows]
    for a in range(7):
        out_ref[0, a] = join_local(full_ref[56 * a : 56 * a + 56].reshape(7, 8, LANES))
    emit_faces(out_ref, far_ref, near_ref, 0)


def total_of(values):
    return jnp.sum(jnp.sum(values, axis=0, keepdims=True), axis=1, keepdims=True)


def first_apply_kernel(
    part_ref, far_x_ref, near_x_ref, far_y_ref, near_y_ref, split_ref, class_ref,
    load_ref, image_ref, out_ref, far_ref, near_ref, full_ref, right_ref, last_ref,
):
    gather_modes(part_ref, far_x_ref, near_x_ref, far_y_ref, near_y_ref, full_ref, load_ref)
    multiply_blocks(split_ref, class_ref, load_ref, image_ref, right_ref, last_ref)
    scatter_modes(image_ref, full_ref, out_ref, far_ref, near_ref)


def second_apply_kernel(
    part_ref, far_x_ref, near_x_ref, far_y_ref, near_y_ref, split_ref, class_ref, load_ref,
    first_ref, shell_ref, power_ref, dots_ref, out_ref, far_ref, near_ref, image_ref, full_ref, right_ref,
    last_ref,
):
    gather_modes(part_ref, far_x_ref, near_x_ref, far_y_ref, near_y_ref, full_ref, power_ref)
    multiply_blocks(split_ref, class_ref, power_ref, image_ref, right_ref, last_ref)
    scatter_modes(image_ref, full_ref, out_ref, far_ref, near_ref)
    load, power, shell = load_ref[...], power_ref[...], shell_ref[...]
    first, image = first_ref[...], image_ref[...]
    lane = lax.broadcasted_iota(jnp.int32, (1, LANES), 1)
    dots = jnp.zeros((1, LANES), F32)
    values = (
        load * load * shell, load * first, power * power * shell, load * image, power * image
    )
    for k, value in enumerate(values):
        dots = dots + jnp.where(lane == k, total_of(value), 0.0)
    dots_ref[...] = dots


def finish_kernel(
    part_ref, far_x_ref, near_x_ref, far_y_ref, near_y_ref, load_ref, power_ref, dots_ref, slot_ref,
    pressure_ref, residual_ref, full_ref, modes_ref,
):
    gather_modes(part_ref, far_x_ref, near_x_ref, far_y_ref, near_y_ref, full_ref, modes_ref)
    dots = jnp.sum(dots_ref[...], axis=0, keepdims=True)
    square, energy, power_square, cross, power_energy = (dots[:, k : k + 1] for k in range(5))
    step = square / energy
    fresh = square - 2.0 * step * energy + step * step * power_square
    ratio = fresh / square
    grow = 1.0 + ratio
    curvature = (
        grow * grow * energy
        - step * grow * (cross + power_square)
        + step * step * power_energy
    )
    second = fresh / curvature
    load, power, twice = load_ref[...], power_ref[...], modes_ref[...]
    pressure = step * load + second * (grow * load - step * power)
    residual = load - step * power - second * (grow * power - step * twice)
    one_hot = permutation(slot_ref)
    pressure_ref[...] = moved(pressure, one_hot, TO_STORED)[:MODES]
    residual_ref[...] = moved(residual, one_hot, TO_STORED)[:MODES]


def call(kernel, outs, args, scratch=(), name=None, hbm=()):
    vmem = pl.BlockSpec(memory_space=pltpu.VMEM)
    places = [pl.BlockSpec(memory_space=pltpu.HBM) if k in hbm else vmem for k in range(len(args))]
    args = [
        pltpu.with_memory_space_constraint(x, pltpu.HBM) if k in hbm else x
        for k, x in enumerate(args)
    ]
    return pl.pallas_call(
        kernel,
        out_shape=tuple(
            jax.ShapeDtypeStruct(*(o if isinstance(o[0], tuple) else (o, F32))) for o in outs
        ),
        in_specs=places,
        out_specs=tuple([vmem] * len(outs)),
        scratch_shapes=[pltpu.VMEM(s, F32) if isinstance(s, tuple) else s for s in scratch],
        compiler_params=pltpu.CompilerParams(vmem_limit_bytes=24 << 20),
        name=name,
    )(*args)


def partners(axis):
    count = lax.axis_size(axis)
    far = [(i, (i + 1) % count if i % 2 else (i - 1) % count) for i in range(count)]
    near = [(i, i ^ 1) for i in range(count)]
    return far, near


def swap(axis, far, near):
    far_pairs, near_pairs = partners(axis)
    return lax.ppermute(far, axis, far_pairs), lax.ppermute(near, axis, near_pairs)


def exchange(part, far, near, dots=None, beside=None):
    far_x, near_x = swap("slab", far, near)
    k = part.shape[0]
    if beside is not None:
        part, beside = lax.optimization_barrier((part, beside))
    if dots is not None:
        cores, chips = reduction_groups()
        dots = lax.psum(dots, ("slab", "dom"), axis_index_groups=cores)
        rows = gather_parts(dots, chips).reshape(-1, LANES)
    far, near = call(side_kernel, [(k, 7, 8, LANES)] * 2, (part, far_x, near_x), name="side")
    received = part, far_x, near_x, *swap("dom", far, near)
    if beside is not None:
        return received, beside
    return received if dots is None else (received, rows)


def gather_parts(row, groups):
    count = len(groups[0])
    spread = jnp.broadcast_to(row.reshape(1, 1, LANES), (count, 1, LANES))
    return lax.all_to_all(spread, ("slab", "dom"), 0, 0, axis_index_groups=groups)


def reduction_groups():
    total = lax.axis_size("slab") * lax.axis_size("dom")
    pairs = [[i, i + 1] for i in range(0, total, 2)]
    return pairs, [list(range(k, total, 2)) for k in range(2)]


def per_device(velocity, slot_map, class_index, schur_blocks):
    slots = slot_map.reshape(1, LANES)
    shell = jnp.asarray(SHELL)
    schur = schur_blocks.transpose(1, 0, 2).reshape(MODES * CLASSES, MODES)
    face = (7, 8, LANES)
    whole = (7, 7, 8, LANES)
    modes = (224, LANES)
    rights = [pltpu.VMEM((256 * CLASSES, n), BF16) for n in (2 * LANES, LANES)]
    brick, part, far, near, classes = call(
        advect_kernel,
        [(3, *whole), (3, *whole), (3, *face), (3, *face), (8, LANES)],
        (velocity, slots, class_index.reshape(1, LANES)),
        [
            (3, NODES, LANES),
            pltpu.VMEM((1, LANES), jnp.int32),
            pltpu.VMEM((1, LANES), jnp.int32),
            pltpu.SemaphoreType.DMA((5,)),
        ],
        name="advect",
        hbm=(0, 1, 2),
    )
    split = call(
        split_kernel,
        [((672, 256 * CLASSES), BF16)],
        (schur,),
        [(MODES * CLASSES, MODES), *[(MODES * CLASSES, LANES)] * 2, pltpu.SemaphoreType.DMA((2,))],
        name="split",
        hbm=(0,),
    )[0]
    received, split = exchange(part, far, near, beside=split)
    part, far, near = call(
        source_kernel,
        [(1, *whole), (1, *face), (1, *face)],
        (*received, brick),
        [(3, *whole)],
        name="source",
    )
    load, first, part, far, near = call(
        first_apply_kernel,
        [modes, modes, (1, *whole), (1, *face), (1, *face)],
        (*exchange(part, far, near), split, classes),
        [(392, LANES), *rights],
        name="first",
    )
    power, dots, part, far, near = call(
        second_apply_kernel,
        [modes, (1, LANES), (1, *whole), (1, *face), (1, *face)],
        (*exchange(part, far, near), split, classes, load, first, shell),
        [modes, (392, LANES), *rights],
        name="second",
    )
    received, rows = exchange(part, far, near, dots)
    return call(
        finish_kernel,
        [(MODES, LANES), (MODES, LANES)],
        (*received, load, power, rows, slots),
        [(392, LANES), modes],
        name="finish",
    )


def solution(mesh):
    return jax.shard_map(
        per_device,
        mesh=mesh,
        in_specs=(
            P(None, None, ("slab", "dom")),
            P("slab", "dom", None),
            P("slab", "dom", None),
            P(),
        ),
        out_specs=(P(None, ("slab", "dom")), P(None, ("slab", "dom"))),
        check_vma=False,
    )
```

```python
import functools

import jax
import jax.numpy as jnp
import numpy as np
from jax import lax
from jax.experimental import pallas as pl
from jax.experimental.pallas import tpu as pltpu
from jax.sharding import PartitionSpec as P

CLASSES = 16
MODES = 218
NODES = 343
LANES = 128
BZ = 16
BY = 8
DELTA_T = 0.05
F32 = jnp.float32
BF16 = jnp.bfloat16


def gll_tables():
    degree = 6
    outer_point = 0.830223896278567
    inner_point = 0.46884879347071423
    points = np.array([-1.0, -outer_point, -inner_point, 0.0, inner_point, outer_point, 1.0])
    values = (231.0 * points**6 - 315.0 * points**4 + 105.0 * points**2 - 5.0) / 16.0
    weights = 2.0 / (degree * (degree + 1) * values**2)
    derivative = np.zeros((7, 7))
    for target in range(7):
        for source in range(7):
            if target != source:
                derivative[target, source] = values[target] / (
                    values[source] * (points[target] - points[source])
                )
    derivative[0, 0] = -degree * (degree + 1) / 4.0
    derivative[6, 6] = degree * (degree + 1) / 4.0
    return derivative, weights


DERIV, WEIGHTS = gll_tables()
FACTOR = np.where((np.arange(7) == 0) | (np.arange(7) == 6), 2.0, 1.0)


def shell_runs():
    runs, offset = [], 0
    for a in range(7):
        for b in range(7):
            base = 8 * (7 * a + b)
            if a in (0, 6) or b in (0, 6):
                runs.append((offset, base, 7))
                offset += 7
            else:
                runs.append((offset, base, 1))
                runs.append((offset + 1, base + 6, 1))
                offset += 2
    return runs


RUNS = shell_runs()


def shell_table():
    multiple = (FACTOR[:, None, None] * FACTOR[None, :, None] * FACTOR[None, None, :]).reshape(-1)
    surface = [
        i for i in range(NODES) if i // 49 in (0, 6) or i // 7 % 7 in (0, 6) or i % 7 in (0, 6)
    ]
    shell = np.zeros((224, LANES))
    shell[:MODES] = (1.0 / multiple[surface])[:, None]
    return shell.astype(np.float32)


SHELL = shell_table()


def span_vector(values):
    node = lax.broadcasted_iota(jnp.int32, (8, LANES), 0)
    table = jnp.zeros((8, LANES), F32)
    for c in range(7):
        table = jnp.where(node == c, float(values[c]), table)
    return table


def span_rolls():
    tables = []
    for shift in range(8):
        sources = [(target - shift) % 8 for target in range(7)]
        tables.append(
            span_vector([DERIV[t, c] if c < 7 else 0.0 for t, c in zip(range(7), sources)])
        )
    return tables


def even_place(axis, like):
    return jnp.full(like.shape, lax.axis_index(axis) % 2, jnp.int32) == 0


def lower_upper(axis, near, far):
    even = even_place(axis, near)
    return jnp.where(even, far, near), jnp.where(even, near, far)


def iotas(shape):
    lane = lax.broadcasted_iota(jnp.int32, shape, len(shape) - 1)
    node = lax.broadcasted_iota(jnp.int32, shape, len(shape) - 2)
    return lane % BZ, lane // BZ, node


def join_local(sheet):
    bz, by, node = iotas(sheet.shape)
    low = pltpu.roll(sheet, 2, 1)
    low = jnp.where(bz == 0, pltpu.roll(low, LANES - 15, 2), pltpu.roll(low, 1, 2))
    high = pltpu.roll(sheet, 6, 1)
    high = jnp.where(bz == BZ - 1, pltpu.roll(high, 15, 2), pltpu.roll(high, LANES - 1, 2))
    sheet = sheet + jnp.where(node == 0, low, jnp.where(node == 6, high, 0.0))
    first, last = sheet[0], sheet[6]
    first_by = by[0]
    new_first = first + jnp.where(first_by > 0, pltpu.roll(last, BZ, 1), 0.0)
    new_last = last + jnp.where(first_by < BY - 1, pltpu.roll(first, LANES - BZ, 1), 0.0)
    return jnp.concatenate([new_first[None], sheet[1:6], new_last[None]], axis=0)


def add_received(a, sheet, far_x, near_x, far_y, near_y):
    if a == 0:
        sheet = sheet + lower_upper("slab", near_x, far_x)[0]
    if a == 6:
        sheet = sheet + lower_upper("slab", near_x, far_x)[1]
    low_y, high_y = lower_upper("dom", near_y, far_y)
    _, by, _ = iotas(sheet.shape[1:])
    first = sheet[0] + jnp.where(by == 0, low_y, 0.0)
    last = sheet[6] + jnp.where(by == BY - 1, high_y, 0.0)
    return jnp.concatenate([first[None], sheet[1:6], last[None]], axis=0)


def derive_sheets(sheets, target):
    total = float(DERIV[target, 0]) * sheets[0]
    for source in range(1, 7):
        total = total + float(DERIV[target, source]) * sheets[source]
    return total


def derive_span(rolls, sheet):
    total = rolls[0] * sheet
    for shift in range(1, 8):
        total = total + rolls[shift] * pltpu.roll(sheet, shift, 1)
    return total


def permutation(slot_ref):
    position = lax.broadcasted_iota(jnp.int32, (LANES, LANES), 0)
    return jnp.where(position == slot_ref[...], 1.0, 0.0).astype(BF16)


def moved(values, one_hot, dims):
    return sum(
        lax.dot_general(term, one_hot, (dims, ((), ())), preferred_element_type=F32)
        for term in terms(values)
    )


TO_BRICK = ((1,), (1,))
TO_STORED = ((1,), (0,))


def emit_faces(part_ref, far_ref, near_ref, index):
    low, high = part_ref[index, 0], part_ref[index, 6]
    even = even_place("slab", low)
    far_ref[index] = jnp.where(even, low, high)
    near_ref[index] = jnp.where(even, high, low)


def advect_kernel(
    vel_hbm, slot_hbm, class_hbm,
    brick_ref, part_ref, far_ref, near_ref, class_out,
    vel_ref, slot_ref, class_ref, sems,
):
    copies = [
        pltpu.make_async_copy(src, dst, sems.at[k])
        for k, (src, dst) in enumerate(
            (
                (slot_hbm, slot_ref), (class_hbm, class_ref),
                *((vel_hbm.at[i], vel_ref.at[i]) for i in range(3)),
            )
        )
    ]
    for copy in copies:
        copy.start()
    rolls = span_rolls()
    brick_ref[:, :, :, 7:8, :] = jnp.zeros((3, 7, 7, 1, LANES), F32)
    copies[0].wait()
    copies[1].wait()
    one_hot = permutation(slot_ref)
    class_out[...] = moved(
        jnp.broadcast_to(class_ref[...].astype(F32), (8, LANES)), one_hot, TO_BRICK
    )
    for i in range(3):
        copies[2 + i].wait()
        stored = moved(vel_ref[i], one_hot, TO_BRICK)
        for a in range(7):
            for b in range(7):
                row = 7 * (7 * a + b)
                brick_ref[i, a, b, 0:7, :] = stored[row : row + 7]

    def component(i, carry):
        sheets = [brick_ref[i, a] for a in range(7)]
        for a in range(7):
            along_a = derive_sheets(sheets, a)
            sheet = sheets[a]
            along_b = jnp.stack(
                [derive_sheets([sheet[b] for b in range(7)], target) for target in range(7)], axis=0
            )
            along_c = derive_span(rolls, sheet)
            advect = (
                brick_ref[0, a] * along_a + brick_ref[1, a] * along_b + brick_ref[2, a] * along_c
            )
            part_ref[i, a] = join_local(advect)
        emit_faces(part_ref, far_ref, near_ref, i)
        return carry

    lax.fori_loop(0, 3, component, 0)


def side_kernel(part_ref, far_x_ref, near_x_ref, far_ref, near_ref):
    for i in range(part_ref.shape[0]):
        low_x, high_x = lower_upper("slab", near_x_ref[i], far_x_ref[i])
        for a in range(7):
            first, last = part_ref[i, a, 0], part_ref[i, a, 6]
            if a == 0:
                first, last = first + low_x[0], last + low_x[6]
            if a == 6:
                first, last = first + high_x[0], last + high_x[6]
            down, up = pltpu.roll(first, LANES - BZ, 1), pltpu.roll(last, BZ, 1)
            even = even_place("dom", up)
            far_ref[i, a] = jnp.where(even, down, up)
            near_ref[i, a] = jnp.where(even, up, down)


def source_kernel(
    part_ref, far_x_ref, near_x_ref, far_y_ref, near_y_ref, brick_ref,
    out_ref, far_ref, near_ref, middle_ref,
):
    rolls = span_rolls()
    weights = span_vector(WEIGHTS)
    inverse = span_vector(1.0 / FACTOR)
    for i in range(3):
        for a in range(7):
            sheet = add_received(
                a, part_ref[i, a], far_x_ref[i], near_x_ref[i], far_y_ref[i, a], near_y_ref[i, a]
            )
            scaled = [
                sheet[b] * (inverse * float(DELTA_T / (FACTOR[a] * FACTOR[b]))) for b in range(7)
            ]
            middle_ref[i, a] = brick_ref[i, a] - jnp.stack(scaled, axis=0)
    sheets = [middle_ref[0, a] for a in range(7)]
    for a in range(7):
        along_a = derive_sheets(sheets, a)
        second = middle_ref[1, a]
        along_b = jnp.stack(
            [derive_sheets([second[b] for b in range(7)], target) for target in range(7)], axis=0
        )
        diverge = along_a + along_b + derive_span(rolls, middle_ref[2, a])
        source = [
            diverge[b] * (weights * float(-1.0 / DELTA_T * WEIGHTS[a] * WEIGHTS[b]))
            for b in range(7)
        ]
        out_ref[0, a] = join_local(jnp.stack(source, axis=0))
    emit_faces(out_ref, far_ref, near_ref, 0)


def gather_modes(part_ref, far_x_ref, near_x_ref, far_y_ref, near_y_ref, full_ref, modes_ref):
    for a in range(7):
        sheet = add_received(
            a, part_ref[0, a], far_x_ref[0], near_x_ref[0], far_y_ref[0, a], near_y_ref[0, a]
        )
        full_ref[56 * a : 56 * a + 56] = sheet.reshape(56, LANES)
    modes_ref[216:224] = jnp.zeros((8, LANES), F32)
    for compact, padded, rows in RUNS:
        modes_ref[compact : compact + rows] = full_ref[padded : padded + rows]


def terms(values):
    high = values.astype(BF16)
    rest = values - high.astype(F32)
    middle = rest.astype(BF16)
    return high, middle, (rest - middle.astype(F32)).astype(BF16)


HALF = 8


def split_kernel(half, schur_hbm, split_ref, schur_ref, left_ref, right_ref, sems):
    copies = [
        pltpu.make_async_copy(
            schur_hbm.at[pl.ds(109 * k, 109), pl.ds(HALF * half, HALF)],
            schur_ref.at[pl.ds(109 * k, 109)],
            sems.at[k],
        )
        for k in range(2)
    ]
    for copy in copies:
        copy.start()
    for k in range(3):
        split_ref[224 * k + 208 : 224 * k + 224] = jnp.zeros((16, 256 * HALF), BF16)
    right_ref[...] = jnp.zeros(right_ref.shape, F32)
    for copy in copies:
        copy.wait()
    left_ref[...] = schur_ref[:, :, :LANES].reshape(MODES * HALF, LANES)
    right_ref[:, : MODES - LANES] = schur_ref[:, :, LANES:].reshape(MODES * HALF, MODES - LANES)
    for c in range(HALF):
        for side, side_ref in enumerate((left_ref, right_ref)):
            block = side_ref[pl.ds(c, MODES, stride=HALF), :]
            place = LANES * (2 * c + side)
            for k, term in enumerate(terms(block)):
                split_ref[224 * k : 224 * k + MODES, place : place + LANES] = term


def split_half(schur, half):
    return call(
        functools.partial(split_kernel, half),
        [((672, 256 * HALF), BF16)],
        (schur,),
        [
            (MODES, HALF, MODES),
            *[(MODES * HALF, LANES)] * 2,
            pltpu.SemaphoreType.DMA((2,)),
        ],
        name="split",
        hbm=(0,),
    )[0]


def multiply_blocks(split_refs, class_ref, modes_ref, image_ref, right_ref, last_ref):
    high, middle, low = terms(modes_ref[...])
    pair = jnp.concatenate([high, middle], axis=1)
    zeros = jnp.zeros((32, 2 * LANES), BF16)
    mine = class_ref[0:1, :]
    for c in range(CLASSES):
        chosen = jnp.where(jnp.abs(mine - float(c)) < 0.5, 1.0, 0.0).astype(BF16)
        right_ref[256 * c : 256 * c + 224] = pair * jnp.concatenate([chosen, chosen], axis=1)
        right_ref[256 * c + 224 : 256 * c + 256] = zeros
        last_ref[256 * c : 256 * c + 224] = low * chosen
        last_ref[256 * c + 224 : 256 * c + 256] = zeros[:, :LANES]
    total, small = 0.0, 0.0
    for half, split_ref in enumerate(split_refs):
        rows = pl.ds(256 * HALF * half, 256 * HALF)
        total = total + jnp.dot(split_ref[...], right_ref[rows], preferred_element_type=F32)
        small = small + jnp.dot(split_ref[0:224], last_ref[rows], preferred_element_type=F32)
    total = total[:, :LANES] + total[:, LANES:]
    image_ref[...] = total[0:224] + (total[224:448] + (total[448:672] + small))


def scatter_modes(image_ref, full_ref, out_ref, far_ref, near_ref):
    full_ref[...] = jnp.zeros((392, LANES), F32)
    for compact, padded, rows in RUNS:
        full_ref[padded : padded + rows] = image_ref[compact : compact + rows]
    for a in range(7):
        out_ref[0, a] = join_local(full_ref[56 * a : 56 * a + 56].reshape(7, 8, LANES))
    emit_faces(out_ref, far_ref, near_ref, 0)


def total_of(values):
    return jnp.sum(jnp.sum(values, axis=0, keepdims=True), axis=1, keepdims=True)


def first_apply_kernel(
    part_ref, far_x_ref, near_x_ref, far_y_ref, near_y_ref, split_0, split_1, class_ref,
    load_ref, image_ref, out_ref, far_ref, near_ref, full_ref, right_ref, last_ref,
):
    gather_modes(part_ref, far_x_ref, near_x_ref, far_y_ref, near_y_ref, full_ref, load_ref)
    multiply_blocks((split_0, split_1), class_ref, load_ref, image_ref, right_ref, last_ref)
    scatter_modes(image_ref, full_ref, out_ref, far_ref, near_ref)


def second_apply_kernel(
    part_ref, far_x_ref, near_x_ref, far_y_ref, near_y_ref, split_0, split_1, class_ref, load_ref,
    first_ref, shell_ref, power_ref, dots_ref, out_ref, far_ref, near_ref, image_ref, full_ref, right_ref,
    last_ref,
):
    gather_modes(part_ref, far_x_ref, near_x_ref, far_y_ref, near_y_ref, full_ref, power_ref)
    multiply_blocks((split_0, split_1), class_ref, power_ref, image_ref, right_ref, last_ref)
    scatter_modes(image_ref, full_ref, out_ref, far_ref, near_ref)
    load, power, shell = load_ref[...], power_ref[...], shell_ref[...]
    first, image = first_ref[...], image_ref[...]
    lane = lax.broadcasted_iota(jnp.int32, (1, LANES), 1)
    dots = jnp.zeros((1, LANES), F32)
    values = (
        load * load * shell, load * first, power * power * shell, load * image, power * image
    )
    for k, value in enumerate(values):
        dots = dots + jnp.where(lane == k, total_of(value), 0.0)
    dots_ref[...] = dots


def finish_kernel(
    part_ref, far_x_ref, near_x_ref, far_y_ref, near_y_ref, load_ref, power_ref, dots_ref, slot_ref,
    pressure_ref, residual_ref, full_ref, modes_ref,
):
    gather_modes(part_ref, far_x_ref, near_x_ref, far_y_ref, near_y_ref, full_ref, modes_ref)
    dots = jnp.sum(dots_ref[...], axis=0)[0:1]
    square, energy, power_square, cross, power_energy = (dots[:, k : k + 1] for k in range(5))
    step = square / energy
    fresh = square - 2.0 * step * energy + step * step * power_square
    ratio = fresh / square
    grow = 1.0 + ratio
    curvature = (
        grow * grow * energy
        - step * grow * (cross + power_square)
        + step * step * power_energy
    )
    second = fresh / curvature
    load, power, twice = load_ref[...], power_ref[...], modes_ref[...]
    pressure = step * load + second * (grow * load - step * power)
    residual = load - step * power - second * (grow * power - step * twice)
    one_hot = permutation(slot_ref)
    pressure_ref[...] = moved(pressure, one_hot, TO_STORED)[:MODES]
    residual_ref[...] = moved(residual, one_hot, TO_STORED)[:MODES]


def call(kernel, outs, args, scratch=(), name=None, hbm=()):
    vmem = pl.BlockSpec(memory_space=pltpu.VMEM)
    places = [pl.BlockSpec(memory_space=pltpu.HBM) if k in hbm else vmem for k in range(len(args))]
    args = [
        pltpu.with_memory_space_constraint(x, pltpu.HBM) if k in hbm else x
        for k, x in enumerate(args)
    ]
    return pl.pallas_call(
        kernel,
        out_shape=tuple(
            jax.ShapeDtypeStruct(*(o if isinstance(o[0], tuple) else (o, F32))) for o in outs
        ),
        in_specs=places,
        out_specs=tuple([vmem] * len(outs)),
        scratch_shapes=[pltpu.VMEM(s, F32) if isinstance(s, tuple) else s for s in scratch],
        compiler_params=pltpu.CompilerParams(vmem_limit_bytes=24 << 20),
        name=name,
    )(*args)


def partners(axis):
    count = lax.axis_size(axis)
    far = [(i, (i + 1) % count if i % 2 else (i - 1) % count) for i in range(count)]
    near = [(i, i ^ 1) for i in range(count)]
    return far, near


def swap(axis, far, near):
    far_pairs, near_pairs = partners(axis)
    return lax.ppermute(far, axis, far_pairs), lax.ppermute(near, axis, near_pairs)


def exchange(part, far, near, dots=None, beside=None):
    far_x, near_x = swap("slab", far, near)
    k = part.shape[0]
    if beside is not None:
        part, beside = lax.optimization_barrier((part, beside))
    if dots is not None:
        rows = gather_parts(dots, "dom")
        far_x, near_x, rows = lax.optimization_barrier((far_x, near_x, rows))
        rows = gather_parts(rows.sum(axis=0), "slab", 4)
    far, near = call(side_kernel, [(k, 7, 8, LANES)] * 2, (part, far_x, near_x), name="side")
    received = part, far_x, near_x, *swap("dom", far, near)
    if beside is not None:
        return received, beside
    return received if dots is None else (received, rows)


def gather_parts(row, axis, copies=1):
    spread = jnp.broadcast_to(row[None], (lax.axis_size(axis), copies, LANES))
    return lax.all_to_all(spread, axis, 0, 0)


def per_device(velocity, slot_map, class_index, schur_blocks):
    slots = slot_map.reshape(1, LANES)
    shell = jnp.asarray(SHELL)
    schur = schur_blocks.transpose(1, 0, 2)
    face = (7, 8, LANES)
    whole = (7, 7, 8, LANES)
    modes = (224, LANES)
    rights = [pltpu.VMEM((256 * CLASSES, n), BF16) for n in (2 * LANES, LANES)]
    brick, part, far, near, classes = call(
        advect_kernel,
        [(3, *whole), (3, *whole), (3, *face), (3, *face), (8, LANES)],
        (velocity, slots, class_index.reshape(1, LANES)),
        [
            (3, NODES, LANES),
            pltpu.VMEM((1, LANES), jnp.int32),
            pltpu.VMEM((1, LANES), jnp.int32),
            pltpu.SemaphoreType.DMA((5,)),
        ],
        name="advect",
        hbm=(0, 1, 2),
    )
    received, split_0 = exchange(part, far, near, beside=split_half(schur, 0))
    part, far, near = call(
        source_kernel,
        [(1, *whole), (1, *face), (1, *face)],
        (*received, brick),
        [(3, *whole)],
        name="source",
    )
    received, split_1 = exchange(part, far, near, beside=split_half(schur, 1))
    load, first, part, far, near = call(
        first_apply_kernel,
        [modes, modes, (1, *whole), (1, *face), (1, *face)],
        (*received, split_0, split_1, classes),
        [(392, LANES), *rights],
        name="first",
    )
    power, dots, part, far, near = call(
        second_apply_kernel,
        [modes, (1, LANES), (1, *whole), (1, *face), (1, *face)],
        (*exchange(part, far, near), split_0, split_1, classes, load, first, shell),
        [modes, (392, LANES), *rights],
        name="second",
    )
    received, rows = exchange(part, far, near, dots)
    return call(
        finish_kernel,
        [(MODES, LANES), (MODES, LANES)],
        (*received, load, power, rows, slots),
        [(392, LANES), modes],
        name="finish",
    )


def solution(mesh):
    return jax.shard_map(
        per_device,
        mesh=mesh,
        in_specs=(
            P(None, None, ("slab", "dom")),
            P("slab", "dom", None),
            P("slab", "dom", None),
            P(),
        ),
        out_specs=(P(None, ("slab", "dom")), P(None, ("slab", "dom"))),
        check_vma=False,
    )
```

```python
import functools

import jax
import jax.numpy as jnp
import numpy as np
from jax import lax
from jax.experimental import pallas as pl
from jax.experimental.pallas import tpu as pltpu
from jax.sharding import PartitionSpec as P

CLASSES = 16
MODES = 218
NODES = 343
LANES = 128
BZ = 16
BY = 8
DELTA_T = 0.05
F32 = jnp.float32
BF16 = jnp.bfloat16


def gll_tables():
    degree = 6
    outer_point = 0.830223896278567
    inner_point = 0.46884879347071423
    points = np.array([-1.0, -outer_point, -inner_point, 0.0, inner_point, outer_point, 1.0])
    values = (231.0 * points**6 - 315.0 * points**4 + 105.0 * points**2 - 5.0) / 16.0
    weights = 2.0 / (degree * (degree + 1) * values**2)
    derivative = np.zeros((7, 7))
    for target in range(7):
        for source in range(7):
            if target != source:
                derivative[target, source] = values[target] / (
                    values[source] * (points[target] - points[source])
                )
    derivative[0, 0] = -degree * (degree + 1) / 4.0
    derivative[6, 6] = degree * (degree + 1) / 4.0
    return derivative, weights


DERIV, WEIGHTS = gll_tables()
FACTOR = np.where((np.arange(7) == 0) | (np.arange(7) == 6), 2.0, 1.0)


def shell_runs():
    runs, offset = [], 0
    for a in range(7):
        for b in range(7):
            base = 8 * (7 * a + b)
            if a in (0, 6) or b in (0, 6):
                runs.append((offset, base, 7))
                offset += 7
            else:
                runs.append((offset, base, 1))
                runs.append((offset + 1, base + 6, 1))
                offset += 2
    return runs


RUNS = shell_runs()
FACE_ROWS = {padded // 8: compact for compact, padded, rows in RUNS if rows == 7}


def shell_table():
    multiple = (FACTOR[:, None, None] * FACTOR[None, :, None] * FACTOR[None, None, :]).reshape(-1)
    surface = [
        i for i in range(NODES) if i // 49 in (0, 6) or i // 7 % 7 in (0, 6) or i % 7 in (0, 6)
    ]
    shell = np.zeros((224, LANES))
    shell[:MODES] = (1.0 / multiple[surface])[:, None]
    return shell.astype(np.float32)


SHELL = shell_table()


def span_vector(values):
    node = lax.broadcasted_iota(jnp.int32, (8, LANES), 0)
    table = jnp.zeros((8, LANES), F32)
    for c in range(7):
        table = jnp.where(node == c, float(values[c]), table)
    return table


def span_rolls():
    tables = []
    for shift in range(8):
        sources = [(target - shift) % 8 for target in range(7)]
        tables.append(
            span_vector([DERIV[t, c] if c < 7 else 0.0 for t, c in zip(range(7), sources)])
        )
    return tables


def even_place(axis, like):
    return jnp.full(like.shape, lax.axis_index(axis) % 2, jnp.int32) == 0


def lower_upper(axis, near, far):
    even = even_place(axis, near)
    return jnp.where(even, far, near), jnp.where(even, near, far)


def iotas(shape):
    lane = lax.broadcasted_iota(jnp.int32, shape, len(shape) - 1)
    node = lax.broadcasted_iota(jnp.int32, shape, len(shape) - 2)
    return lane % BZ, lane // BZ, node


def join_span(sheet):
    bz, _, node = iotas(sheet.shape)
    low = pltpu.roll(sheet, 2, 1)
    low = jnp.where(bz == 0, pltpu.roll(low, LANES - 15, 2), pltpu.roll(low, 1, 2))
    high = pltpu.roll(sheet, 6, 1)
    high = jnp.where(bz == BZ - 1, pltpu.roll(high, 15, 2), pltpu.roll(high, LANES - 1, 2))
    return sheet + jnp.where(node == 0, low, jnp.where(node == 6, high, 0.0))


def join_local(sheet):
    sheet = join_span(sheet)
    _, by, _ = iotas(sheet.shape[1:])
    first, last = sheet[0], sheet[6]
    new_first = first + jnp.where(by > 0, pltpu.roll(last, BZ, 1), 0.0)
    new_last = last + jnp.where(by < BY - 1, pltpu.roll(first, LANES - BZ, 1), 0.0)
    return jnp.concatenate([new_first[None], sheet[1:6], new_last[None]], axis=0)


def add_streamwise(a, sheet, far_x, near_x):
    if a == 0:
        sheet = sheet + lower_upper("slab", near_x, far_x)[0]
    if a == 6:
        sheet = sheet + lower_upper("slab", near_x, far_x)[1]
    return sheet


def add_second(sheet, low_y, high_y):
    _, by, _ = iotas(sheet.shape[1:])
    first = sheet[0] + jnp.where(by == 0, low_y, 0.0)
    last = sheet[6] + jnp.where(by == BY - 1, high_y, 0.0)
    return jnp.concatenate([first[None], sheet[1:6], last[None]], axis=0)


def pack_groups(blocks, start):
    _, group, _ = iotas(blocks[0].shape)
    total = jnp.zeros(blocks[0].shape, F32)
    for k, block in enumerate(blocks):
        shift = (BZ * k - start) % LANES
        total = jnp.where(group == k, pltpu.roll(block, shift, 1) if shift else block, total)
    return total


def lanes_from(packed, group, start):
    shift = (start - BZ * group) % LANES
    return pltpu.roll(packed, shift, 1) if shift else packed


def derive_sheets(sheets, target):
    total = float(DERIV[target, 0]) * sheets[0]
    for source in range(1, 7):
        total = total + float(DERIV[target, source]) * sheets[source]
    return total


def derive_span(rolls, sheet):
    total = rolls[0] * sheet
    for shift in range(1, 8):
        total = total + rolls[shift] * pltpu.roll(sheet, shift, 1)
    return total


def permutation(slot_ref):
    position = lax.broadcasted_iota(jnp.int32, (LANES, LANES), 0)
    return jnp.where(position == slot_ref[...], 1.0, 0.0).astype(BF16)


def moved(values, one_hot, dims):
    return sum(
        lax.dot_general(term, one_hot, (dims, ((), ())), preferred_element_type=F32)
        for term in terms(values)
    )


TO_BRICK = ((1,), (1,))
TO_STORED = ((1,), (0,))


def emit_faces(part_ref, far_ref, near_ref, index):
    low, high = part_ref[index, 0], part_ref[index, 6]
    even = even_place("slab", low)
    far_ref[index] = jnp.where(even, low, high)
    near_ref[index] = jnp.where(even, high, low)


def advect_kernel(
    vel_hbm, slot_hbm, class_hbm,
    brick_ref, part_ref, far_ref, near_ref, class_out,
    vel_ref, slot_ref, class_ref, sems,
):
    copies = [
        pltpu.make_async_copy(src, dst, sems.at[k])
        for k, (src, dst) in enumerate(
            (
                (slot_hbm, slot_ref), (class_hbm, class_ref),
                *((vel_hbm.at[i], vel_ref.at[i]) for i in range(3)),
            )
        )
    ]
    for copy in copies:
        copy.start()
    rolls = span_rolls()
    brick_ref[:, :, :, 7:8, :] = jnp.zeros((3, 7, 7, 1, LANES), F32)
    copies[0].wait()
    copies[1].wait()
    one_hot = permutation(slot_ref)
    class_out[...] = moved(
        jnp.broadcast_to(class_ref[...].astype(F32), (8, LANES)), one_hot, TO_BRICK
    )
    for i in range(3):
        copies[2 + i].wait()
        stored = moved(vel_ref[i], one_hot, TO_BRICK)
        for a in range(7):
            for b in range(7):
                row = 7 * (7 * a + b)
                brick_ref[i, a, b, 0:7, :] = stored[row : row + 7]

    def component(i, carry):
        sheets = [brick_ref[i, a] for a in range(7)]
        for a in range(7):
            along_a = derive_sheets(sheets, a)
            sheet = sheets[a]
            along_b = jnp.stack(
                [derive_sheets([sheet[b] for b in range(7)], target) for target in range(7)], axis=0
            )
            along_c = derive_span(rolls, sheet)
            advect = (
                brick_ref[0, a] * along_a + brick_ref[1, a] * along_b + brick_ref[2, a] * along_c
            )
            part_ref[i, a] = join_local(advect)
        emit_faces(part_ref, far_ref, near_ref, i)
        return carry

    lax.fori_loop(0, 3, component, 0)


def side_kernel(part_ref, far_x_ref, near_x_ref, far_ref, near_ref):
    for i in range(part_ref.shape[0]):
        low_x, high_x = lower_upper("slab", near_x_ref[i], far_x_ref[i])
        for a in range(7):
            first, last = part_ref[i, a, 0], part_ref[i, a, 6]
            if a == 0:
                first, last = first + low_x[0], last + low_x[6]
            if a == 6:
                first, last = first + high_x[0], last + high_x[6]
            down, up = pltpu.roll(first, LANES - BZ, 1), pltpu.roll(last, BZ, 1)
            even = even_place("dom", up)
            far_ref[i, a] = jnp.where(even, down, up)
            near_ref[i, a] = jnp.where(even, up, down)


def row_kernel(part_ref, far_x_ref, near_x_ref, class_ref, far_ref, near_ref):
    classes = class_ref[...]
    for a in range(7):
        sheet = add_streamwise(a, part_ref[0, a], far_x_ref[0], near_x_ref[0])
        blocks = [*(sheet[b] for b in range(7)), classes]
        down, up = pack_groups(blocks, 0), pack_groups(blocks, LANES - BZ)
        even = even_place("dom", up)
        far_ref[0, a] = jnp.where(even, down, up)
        near_ref[0, a] = jnp.where(even, up, down)


def source_kernel(
    part_ref, far_x_ref, near_x_ref, far_y_ref, near_y_ref, brick_ref,
    out_ref, far_ref, near_ref, middle_ref,
):
    rolls = span_rolls()
    weights = span_vector(WEIGHTS)
    inverse = span_vector(1.0 / FACTOR)
    for i in range(3):
        for a in range(7):
            sheet = add_streamwise(a, part_ref[i, a], far_x_ref[i], near_x_ref[i])
            sheet = add_second(sheet, *lower_upper("dom", near_y_ref[i, a], far_y_ref[i, a]))
            scaled = [
                sheet[b] * (inverse * float(DELTA_T / (FACTOR[a] * FACTOR[b]))) for b in range(7)
            ]
            middle_ref[i, a] = brick_ref[i, a] - jnp.stack(scaled, axis=0)
    sheets = [middle_ref[0, a] for a in range(7)]
    for a in range(7):
        along_a = derive_sheets(sheets, a)
        second = middle_ref[1, a]
        along_b = jnp.stack(
            [derive_sheets([second[b] for b in range(7)], target) for target in range(7)], axis=0
        )
        diverge = along_a + along_b + derive_span(rolls, middle_ref[2, a])
        source = [
            diverge[b] * (weights * float(-1.0 / DELTA_T * WEIGHTS[a] * WEIGHTS[b]))
            for b in range(7)
        ]
        out_ref[0, a] = join_local(jnp.stack(source, axis=0))
    emit_faces(out_ref, far_ref, near_ref, 0)


def gather_modes(full_ref, modes_ref):
    modes_ref[216:224] = jnp.zeros((8, LANES), F32)
    for compact, padded, rows in RUNS:
        modes_ref[compact : compact + rows] = full_ref[padded : padded + rows]


def terms(values):
    high = values.astype(BF16)
    rest = values - high.astype(F32)
    middle = rest.astype(BF16)
    return high, middle, (rest - middle.astype(F32)).astype(BF16)


HALF = 8


def split_kernel(half, schur_hbm, split_ref, schur_ref, left_ref, right_ref, sems):
    copies = [
        pltpu.make_async_copy(
            schur_hbm.at[pl.ds(109 * k, 109), pl.ds(HALF * half, HALF)],
            schur_ref.at[pl.ds(109 * k, 109)],
            sems.at[k],
        )
        for k in range(2)
    ]
    for copy in copies:
        copy.start()
    for k in range(3):
        split_ref[224 * k + 208 : 224 * k + 224] = jnp.zeros((16, 256 * HALF), BF16)
    right_ref[...] = jnp.zeros(right_ref.shape, F32)
    for copy in copies:
        copy.wait()
    left_ref[...] = schur_ref[:, :, :LANES].reshape(MODES * HALF, LANES)
    right_ref[:, : MODES - LANES] = schur_ref[:, :, LANES:].reshape(MODES * HALF, MODES - LANES)
    for c in range(HALF):
        for side, side_ref in enumerate((left_ref, right_ref)):
            block = side_ref[pl.ds(c, MODES, stride=HALF), :]
            place = LANES * (2 * c + side)
            for k, term in enumerate(terms(block)):
                split_ref[224 * k : 224 * k + MODES, place : place + LANES] = term


def split_half(schur, half):
    return call(
        functools.partial(split_kernel, half),
        [((672, 256 * HALF), BF16)],
        (schur,),
        [
            (MODES, HALF, MODES),
            *[(MODES * HALF, LANES)] * 2,
            pltpu.SemaphoreType.DMA((2,)),
        ],
        name="split",
        hbm=(0,),
    )[0]


def multiply_blocks(splits, class_ref, modes_ref, image_ref, right_ref, last_ref, ghost=None):
    high, middle, low = terms(modes_ref[...])
    pair = jnp.concatenate([high, middle], axis=1)
    mine = class_ref[0:1, :]
    both, last_both, rows = jnp.concatenate([mine, mine], axis=1), mine, 224
    if ghost is not None:
        modes, classes = (
            x + pltpu.roll(x, 32, 1) + pltpu.roll(x, 64, 1) for x in (ghost[0], ghost[1])
        )
        lane = lax.broadcasted_iota(jnp.int32, modes.shape, 1)
        three = [
            jnp.where((lane >= 32 * k) & (lane < 32 * k + 32), term.astype(F32), 0.0)
            for k, term in enumerate(terms(modes))
        ]
        low = jnp.concatenate([low, (three[0] + three[1] + three[2]).astype(BF16)], axis=1)
        last_both, rows = jnp.concatenate([mine, classes[0:1]], axis=1), 672
    zeros = jnp.zeros((32, 2 * LANES), BF16)
    for c in range(CLASSES):
        chosen, last_chosen = (
            jnp.where(jnp.abs(x - float(c)) < 0.5, 1.0, 0.0).astype(BF16) for x in (both, last_both)
        )
        right_ref[256 * c : 256 * c + 224] = pair * chosen
        right_ref[256 * c + 224 : 256 * c + 256] = zeros
        last_ref[256 * c : 256 * c + 224] = low * last_chosen
        last_ref[256 * c + 224 : 256 * c + 256] = zeros[:, : low.shape[1]]
    total, small = 0.0, 0.0
    for half, split_ref in enumerate(splits):
        part = pl.ds(256 * HALF * half, 256 * HALF)
        total = total + jnp.dot(split_ref[...], right_ref[part], preferred_element_type=F32)
        small = small + jnp.dot(split_ref[0:rows], last_ref[part], preferred_element_type=F32)
    total = total[:, :LANES] + total[:, LANES:]
    image_ref[...] = total[0:224] + (total[224:448] + (total[448:672] + small[0:224, :LANES]))
    if ghost is None:
        return None
    extra = small[:, LANES:]
    extra = extra[0:224] + (extra[224:448] + extra[448:672])
    return extra + (pltpu.roll(extra, LANES - 32, 1) + pltpu.roll(extra, LANES - 64, 1))


def scatter_modes(image_ref, full_ref, out_ref):
    full_ref[...] = jnp.zeros((392, LANES), F32)
    for compact, padded, rows in RUNS:
        full_ref[padded : padded + rows] = image_ref[compact : compact + rows]
    for a in range(7):
        out_ref[0, a] = join_local(full_ref[56 * a : 56 * a + 56].reshape(7, 8, LANES))


def total_of(values):
    return jnp.sum(jnp.sum(values, axis=0, keepdims=True), axis=1, keepdims=True)


def first_apply_kernel(
    part_ref, far_x_ref, near_x_ref, far_y_ref, near_y_ref, split_0, split_1, class_ref,
    load_ref, image_ref, out_ref, far_ref, near_ref,
    full_ref, ghost_ref, ghost_modes_ref, side_ref, right_ref, last_ref,
):
    _, by, _ = iotas((8, LANES))
    for a in range(7):
        sheet = add_streamwise(a, part_ref[0, a], far_x_ref[0], near_x_ref[0])
        low, high = lower_upper("dom", near_y_ref[0, a], far_y_ref[0, a])
        for b in range(7):
            block = jnp.where(by == 0, lanes_from(low, b, 0), 0.0)
            block = jnp.where(by == 1, lanes_from(high, b, BZ), block)
            if b == 6:
                block = block + jnp.where(by == 0, sheet[0], 0.0)
            if b == 0:
                block = block + jnp.where(by == 1, pltpu.roll(sheet[6], 2 * BZ, 1), 0.0)
            ghost_ref[56 * a + 8 * b : 56 * a + 8 * b + 8] = block
        sheet = add_second(sheet, lanes_from(low, 6, 0), lanes_from(high, 0, LANES - BZ))
        full_ref[56 * a : 56 * a + 56] = sheet.reshape(56, LANES)
    low, high = lower_upper("dom", near_y_ref[0, 0], far_y_ref[0, 0])
    ghost_class = jnp.where(by == 0, lanes_from(low, 7, 0), 0.0)
    ghost_class = jnp.where(by == 1, lanes_from(high, 7, BZ), ghost_class)
    gather_modes(full_ref, load_ref)
    gather_modes(ghost_ref, ghost_modes_ref)
    ghost_image = multiply_blocks(
        (split_0, split_1), class_ref, load_ref, image_ref, right_ref, last_ref,
        (ghost_modes_ref[...], ghost_class),
    )
    scatter_modes(image_ref, full_ref, out_ref)
    ghost_modes_ref[...] = ghost_image
    side_ref[...] = jnp.zeros(side_ref.shape, F32)
    for k, b in enumerate((6, 0)):
        for a in range(7):
            row = FACE_ROWS[7 * a + b]
            side_ref[k, a, 0:7] = ghost_modes_ref[row : row + 7]
    below, above = join_span(side_ref[0]), join_span(side_ref[1])
    for a in range(7):
        out_ref[0, a, 0] += jnp.where(by == 0, below[a], 0.0)
        out_ref[0, a, 6] += jnp.where(by == BY - 1, pltpu.roll(above[a], LANES - 2 * BZ, 1), 0.0)
    emit_faces(out_ref, far_ref, near_ref, 0)


def second_apply_kernel(
    part_ref, far_x_ref, near_x_ref, split_0, split_1, class_ref, load_ref, first_ref, shell_ref,
    power_ref, send_ref, out_ref, image_ref, full_ref, right_ref, last_ref,
):
    for a in range(7):
        sheet = add_streamwise(a, part_ref[0, a], far_x_ref[0], near_x_ref[0])
        full_ref[56 * a : 56 * a + 56] = sheet.reshape(56, LANES)
    gather_modes(full_ref, power_ref)
    multiply_blocks((split_0, split_1), class_ref, power_ref, image_ref, right_ref, last_ref)
    scatter_modes(image_ref, full_ref, out_ref)
    load, power, shell = load_ref[...], power_ref[...], shell_ref[...]
    first, image = first_ref[...], image_ref[...]
    lane = lax.broadcasted_iota(jnp.int32, (1, LANES), 1)
    dots = jnp.zeros((1, LANES), F32)
    values = (
        load * load * shell, load * first, power * power * shell, load * image, power * image
    )
    for k, value in enumerate(values):
        dots = dots + jnp.where(lane == k, total_of(value), 0.0)
    node = lax.broadcasted_iota(jnp.int32, (8, LANES), 0)
    count = send_ref.shape[0]
    mine = lax.axis_index("dom")
    alone = jnp.where(node == 7, dots, 0.0)
    send_ref[...] = jnp.broadcast_to(alone[None], send_ref.shape)
    up = pack_groups([out_ref[0, a, 6] for a in range(7)], LANES - BZ)
    down = pack_groups([out_ref[0, a, 0] for a in range(7)], 0)
    send_ref[lax.rem(mine + 1, count)] = jnp.where(node == 7, dots, up)
    send_ref[lax.rem(mine + count - 1, count)] = jnp.where(node == 7, dots, down)


def middle_kernel(part_ref, got_ref, far_ref, near_ref, low_ref, high_ref, sums_ref):
    node = lax.broadcasted_iota(jnp.int32, (8, LANES), 0)
    count = got_ref.shape[0]
    mine = lax.axis_index("dom")
    low = jnp.where(node < 7, got_ref[lax.rem(mine + count - 1, count)], 0.0)
    high = jnp.where(node < 7, got_ref[lax.rem(mine + 1, count)], 0.0)
    faces = []
    for a in range(7):
        low_ref[a], high_ref[a] = lanes_from(low, a, 0), lanes_from(high, a, LANES - BZ)
        if a in (0, 6):
            faces.append(add_second(part_ref[0, a], low_ref[a], high_ref[a]))
    even = even_place("slab", faces[0])
    far_ref[0] = jnp.where(even, faces[0], faces[1])
    near_ref[0] = jnp.where(even, faces[1], faces[0])
    total = jnp.sum(got_ref[...], axis=0)[7:8]
    sums_ref[...] = jnp.broadcast_to(total[None], sums_ref.shape)


def finish_kernel(
    part_ref, far_x_ref, near_x_ref, low_ref, high_ref, load_ref, power_ref, dots_ref, slot_ref,
    pressure_ref, residual_ref, full_ref, modes_ref,
):
    for a in range(7):
        sheet = add_streamwise(a, part_ref[0, a], far_x_ref[0], near_x_ref[0])
        sheet = add_second(sheet, low_ref[a], high_ref[a])
        full_ref[56 * a : 56 * a + 56] = sheet.reshape(56, LANES)
    gather_modes(full_ref, modes_ref)
    dots = jnp.sum(dots_ref[...], axis=0)[0:1]
    square, energy, power_square, cross, power_energy = (dots[:, k : k + 1] for k in range(5))
    step = square / energy
    fresh = square - 2.0 * step * energy + step * step * power_square
    ratio = fresh / square
    grow = 1.0 + ratio
    curvature = (
        grow * grow * energy
        - step * grow * (cross + power_square)
        + step * step * power_energy
    )
    second = fresh / curvature
    load, power, twice = load_ref[...], power_ref[...], modes_ref[...]
    pressure = step * load + second * (grow * load - step * power)
    residual = load - step * power - second * (grow * power - step * twice)
    one_hot = permutation(slot_ref)
    pressure_ref[...] = moved(pressure, one_hot, TO_STORED)[:MODES]
    residual_ref[...] = moved(residual, one_hot, TO_STORED)[:MODES]


def call(kernel, outs, args, scratch=(), name=None, hbm=()):
    vmem = pl.BlockSpec(memory_space=pltpu.VMEM)
    places = [pl.BlockSpec(memory_space=pltpu.HBM) if k in hbm else vmem for k in range(len(args))]
    args = [
        pltpu.with_memory_space_constraint(x, pltpu.HBM) if k in hbm else x
        for k, x in enumerate(args)
    ]
    return pl.pallas_call(
        kernel,
        out_shape=tuple(
            jax.ShapeDtypeStruct(*(o if isinstance(o[0], tuple) else (o, F32))) for o in outs
        ),
        in_specs=places,
        out_specs=tuple([vmem] * len(outs)),
        scratch_shapes=[pltpu.VMEM(s, F32) if isinstance(s, tuple) else s for s in scratch],
        compiler_params=pltpu.CompilerParams(vmem_limit_bytes=24 << 20),
        name=name,
    )(*args)


def partners(axis):
    count = lax.axis_size(axis)
    far = [(i, (i + 1) % count if i % 2 else (i - 1) % count) for i in range(count)]
    near = [(i, i ^ 1) for i in range(count)]
    return far, near


def swap(axis, far, near):
    far_pairs, near_pairs = partners(axis)
    return lax.ppermute(far, axis, far_pairs), lax.ppermute(near, axis, near_pairs)


def exchange(part, far, near, beside, rows=None):
    far_x, near_x = swap("slab", far, near)
    part, beside = lax.optimization_barrier((part, beside))
    outs = [(part.shape[0], 7, 8, LANES)] * 2
    args = (part, far_x, near_x)
    if rows is None:
        far, near = call(side_kernel, outs, args, name="side")
    else:
        far, near = call(row_kernel, outs, (*args, rows), name="rows")
    return (part, far_x, near_x, *swap("dom", far, near)), beside


def per_device(velocity, slot_map, class_index, schur_blocks):
    slots = slot_map.reshape(1, LANES)
    shell = jnp.asarray(SHELL)
    schur = schur_blocks.transpose(1, 0, 2)
    face = (7, 8, LANES)
    whole = (7, 7, 8, LANES)
    modes = (224, LANES)
    rights = [pltpu.VMEM((256 * CLASSES, n), BF16) for n in (2 * LANES, LANES)]
    brick, part, far, near, classes = call(
        advect_kernel,
        [(3, *whole), (3, *whole), (3, *face), (3, *face), (8, LANES)],
        (velocity, slots, class_index.reshape(1, LANES)),
        [
            (3, NODES, LANES),
            pltpu.VMEM((1, LANES), jnp.int32),
            pltpu.VMEM((1, LANES), jnp.int32),
            pltpu.SemaphoreType.DMA((5,)),
        ],
        name="advect",
        hbm=(0, 1, 2),
    )
    received, split_0 = exchange(part, far, near, split_half(schur, 0))
    part, far, near = call(
        source_kernel,
        [(1, *whole), (1, *face), (1, *face)],
        (*received, brick),
        [(3, *whole)],
        name="source",
    )
    received, split_1 = exchange(part, far, near, split_half(schur, 1), classes)
    load, first, part, far, near = call(
        first_apply_kernel,
        [modes, modes, (1, *whole), (1, *face), (1, *face)],
        (*received, split_0, split_1, classes),
        [(392, LANES), (392, LANES), modes, (2, *face), rights[0], rights[0]],
        name="first",
    )
    slabs, doms = lax.axis_size("slab"), lax.axis_size("dom")
    power, send, part = call(
        second_apply_kernel,
        [modes, (doms, 8, LANES), (1, *whole)],
        (part, *swap("slab", far, near), split_0, split_1, classes, load, first, shell),
        [modes, (392, LANES), *rights],
        name="second",
    )
    far, near, low, high, sums = call(
        middle_kernel,
        [(1, *face), (1, *face), face, face, (slabs, 4, LANES)],
        (part, lax.all_to_all(send, "dom", 0, 0)),
        name="middle",
    )
    dots = lax.all_to_all(sums, "slab", 0, 0)
    return call(
        finish_kernel,
        [(MODES, LANES), (MODES, LANES)],
        (part, *swap("slab", far, near), low, high, load, power, dots, slots),
        [(392, LANES), modes],
        name="finish",
    )


def solution(mesh):
    return jax.shard_map(
        per_device,
        mesh=mesh,
        in_specs=(
            P(None, None, ("slab", "dom")),
            P("slab", "dom", None),
            P("slab", "dom", None),
            P(),
        ),
        out_specs=(P(None, ("slab", "dom")), P(None, ("slab", "dom"))),
        check_vma=False,
    )
```

```python
import functools

import jax
import jax.numpy as jnp
import numpy as np
from jax import lax
from jax.experimental import pallas as pl
from jax.experimental.pallas import tpu as pltpu
from jax.sharding import PartitionSpec as P

CLASSES = 16
MODES = 218
NODES = 343
LANES = 128
BZ = 16
BY = 8
DELTA_T = 0.05
F32 = jnp.float32
BF16 = jnp.bfloat16


def gll_tables():
    degree = 6
    outer_point = 0.830223896278567
    inner_point = 0.46884879347071423
    points = np.array([-1.0, -outer_point, -inner_point, 0.0, inner_point, outer_point, 1.0])
    values = (231.0 * points**6 - 315.0 * points**4 + 105.0 * points**2 - 5.0) / 16.0
    weights = 2.0 / (degree * (degree + 1) * values**2)
    derivative = np.zeros((7, 7))
    for target in range(7):
        for source in range(7):
            if target != source:
                derivative[target, source] = values[target] / (
                    values[source] * (points[target] - points[source])
                )
    derivative[0, 0] = -degree * (degree + 1) / 4.0
    derivative[6, 6] = degree * (degree + 1) / 4.0
    return derivative, weights


DERIV, WEIGHTS = gll_tables()
FACTOR = np.where((np.arange(7) == 0) | (np.arange(7) == 6), 2.0, 1.0)


def shell_runs():
    runs, offset = [], 0
    for a in range(7):
        for b in range(7):
            base = 8 * (7 * a + b)
            if a in (0, 6) or b in (0, 6):
                runs.append((offset, base, 7))
                offset += 7
            else:
                runs.append((offset, base, 1))
                runs.append((offset + 1, base + 6, 1))
                offset += 2
    return runs


RUNS = shell_runs()
FACE_ROWS = {padded // 8: compact for compact, padded, rows in RUNS if rows == 7}


def shell_table():
    multiple = (FACTOR[:, None, None] * FACTOR[None, :, None] * FACTOR[None, None, :]).reshape(-1)
    surface = [
        i for i in range(NODES) if i // 49 in (0, 6) or i // 7 % 7 in (0, 6) or i % 7 in (0, 6)
    ]
    shell = np.zeros((224, LANES))
    shell[:MODES] = (1.0 / multiple[surface])[:, None]
    return shell.astype(np.float32)


SHELL = shell_table()


def span_vector(values):
    node = lax.broadcasted_iota(jnp.int32, (8, LANES), 0)
    table = jnp.zeros((8, LANES), F32)
    for c in range(7):
        table = jnp.where(node == c, float(values[c]), table)
    return table


def span_rolls():
    tables = []
    for shift in range(8):
        sources = [(target - shift) % 8 for target in range(7)]
        tables.append(
            span_vector([DERIV[t, c] if c < 7 else 0.0 for t, c in zip(range(7), sources)])
        )
    return tables


def even_place(axis, like):
    return jnp.full(like.shape, lax.axis_index(axis) % 2, jnp.int32) == 0


def lower_upper(axis, near, far):
    even = even_place(axis, near)
    return jnp.where(even, far, near), jnp.where(even, near, far)


def iotas(shape):
    lane = lax.broadcasted_iota(jnp.int32, shape, len(shape) - 1)
    node = lax.broadcasted_iota(jnp.int32, shape, len(shape) - 2)
    return lane % BZ, lane // BZ, node


def join_span(sheet):
    bz, _, node = iotas(sheet.shape)
    low = pltpu.roll(sheet, 2, 1)
    low = jnp.where(bz == 0, pltpu.roll(low, LANES - 15, 2), pltpu.roll(low, 1, 2))
    high = pltpu.roll(sheet, 6, 1)
    high = jnp.where(bz == BZ - 1, pltpu.roll(high, 15, 2), pltpu.roll(high, LANES - 1, 2))
    return sheet + jnp.where(node == 0, low, jnp.where(node == 6, high, 0.0))


def join_local(sheet):
    sheet = join_span(sheet)
    _, by, _ = iotas(sheet.shape[1:])
    first, last = sheet[0], sheet[6]
    new_first = first + jnp.where(by > 0, pltpu.roll(last, BZ, 1), 0.0)
    new_last = last + jnp.where(by < BY - 1, pltpu.roll(first, LANES - BZ, 1), 0.0)
    return jnp.concatenate([new_first[None], sheet[1:6], new_last[None]], axis=0)


def add_streamwise(a, sheet, far_x, near_x):
    if a == 0:
        sheet = sheet + lower_upper("slab", near_x, far_x)[0]
    if a == 6:
        sheet = sheet + lower_upper("slab", near_x, far_x)[1]
    return sheet


def add_second(sheet, low_y, high_y):
    _, by, _ = iotas(sheet.shape[1:])
    first = sheet[0] + jnp.where(by == 0, low_y, 0.0)
    last = sheet[6] + jnp.where(by == BY - 1, high_y, 0.0)
    return jnp.concatenate([first[None], sheet[1:6], last[None]], axis=0)


def pack_groups(blocks, start):
    _, group, _ = iotas(blocks[0].shape)
    total = jnp.zeros(blocks[0].shape, F32)
    for k, block in enumerate(blocks):
        shift = (BZ * k - start) % LANES
        total = jnp.where(group == k, pltpu.roll(block, shift, 1) if shift else block, total)
    return total


def lanes_from(packed, group, start):
    shift = (start - BZ * group) % LANES
    return pltpu.roll(packed, shift, 1) if shift else packed


def derive_sheets(sheets, target):
    total = float(DERIV[target, 0]) * sheets[0]
    for source in range(1, 7):
        total = total + float(DERIV[target, source]) * sheets[source]
    return total


def derive_span(rolls, sheet):
    total = rolls[0] * sheet
    for shift in range(1, 8):
        total = total + rolls[shift] * pltpu.roll(sheet, shift, 1)
    return total


def permutation(slot_ref):
    position = lax.broadcasted_iota(jnp.int32, (LANES, LANES), 0)
    return jnp.where(position == slot_ref[...], 1.0, 0.0).astype(BF16)


def moved(values, one_hot, dims):
    return sum(
        lax.dot_general(term, one_hot, (dims, ((), ())), preferred_element_type=F32)
        for term in terms(values)
    )


TO_BRICK = ((1,), (1,))
TO_STORED = ((1,), (0,))


def emit_faces(part_ref, far_ref, near_ref, index):
    low, high = part_ref[index, 0], part_ref[index, 6]
    even = even_place("slab", low)
    far_ref[index] = jnp.where(even, low, high)
    near_ref[index] = jnp.where(even, high, low)


def advect_kernel(
    vel_hbm, slot_hbm, class_hbm,
    brick_ref, part_ref, far_ref, near_ref, class_out,
    vel_ref, slot_ref, class_ref, sems,
):
    copies = [
        pltpu.make_async_copy(src, dst, sems.at[k])
        for k, (src, dst) in enumerate(
            (
                (slot_hbm, slot_ref), (class_hbm, class_ref),
                *((vel_hbm.at[i], vel_ref.at[i]) for i in range(3)),
            )
        )
    ]
    for copy in copies:
        copy.start()
    rolls = span_rolls()
    brick_ref[:, :, :, 7:8, :] = jnp.zeros((3, 7, 7, 1, LANES), F32)
    copies[0].wait()
    copies[1].wait()
    one_hot = permutation(slot_ref)
    class_out[...] = moved(
        jnp.broadcast_to(class_ref[...].astype(F32), (8, LANES)), one_hot, TO_BRICK
    )
    for i in range(3):
        copies[2 + i].wait()
        stored = moved(vel_ref[i], one_hot, TO_BRICK)
        for a in range(7):
            for b in range(7):
                row = 7 * (7 * a + b)
                brick_ref[i, a, b, 0:7, :] = stored[row : row + 7]

    def component(i, carry):
        sheets = [brick_ref[i, a] for a in range(7)]
        for a in range(7):
            along_a = derive_sheets(sheets, a)
            sheet = sheets[a]
            along_b = jnp.stack(
                [derive_sheets([sheet[b] for b in range(7)], target) for target in range(7)], axis=0
            )
            along_c = derive_span(rolls, sheet)
            advect = (
                brick_ref[0, a] * along_a + brick_ref[1, a] * along_b + brick_ref[2, a] * along_c
            )
            part_ref[i, a] = join_local(advect)
        emit_faces(part_ref, far_ref, near_ref, i)
        return carry

    lax.fori_loop(0, 3, component, 0)


def source_kernel(
    part_ref, far_x_ref, near_x_ref, brick_ref, class_ref,
    out_ref, far_ref, near_ref, first_ref, last_ref, middle_ref,
):
    rolls = span_rolls()
    weights = span_vector(WEIGHTS)
    inverse = span_vector(1.0 / FACTOR)
    for i in range(3):
        for a in range(7):
            sheet = add_streamwise(a, part_ref[i, a], far_x_ref[i], near_x_ref[i])
            first_ref[i, a], last_ref[i, a] = sheet[0], sheet[6]
            scaled = [
                sheet[b] * (inverse * float(DELTA_T / (FACTOR[a] * FACTOR[b]))) for b in range(7)
            ]
            middle_ref[i, a] = brick_ref[i, a] - jnp.stack(scaled, axis=0)
    sheets = [middle_ref[0, a] for a in range(7)]
    for a in range(7):
        along_a = derive_sheets(sheets, a)
        second = middle_ref[1, a]
        along_b = jnp.stack(
            [derive_sheets([second[b] for b in range(7)], target) for target in range(7)], axis=0
        )
        diverge = along_a + along_b + derive_span(rolls, middle_ref[2, a])
        source = [
            diverge[b] * (weights * float(-1.0 / DELTA_T * WEIGHTS[a] * WEIGHTS[b]))
            for b in range(7)
        ]
        out_ref[0, a] = join_local(jnp.stack(source, axis=0))
    classes = class_ref[...]
    even = even_place("dom", classes)
    for a in range(7):
        rows = [*(out_ref[0, a, b] for b in range(7)), classes]
        pairs = (
            (pack_groups(rows, 0), pack_groups(rows, LANES - BZ)),
            (
                pack_groups([first_ref[i, a] for i in range(3)], 0),
                pack_groups([last_ref[i, a] for i in range(3)], LANES - BZ),
            ),
        )
        for k, (down, up) in enumerate(pairs):
            far_ref[k, a] = jnp.where(even, down, up)
            near_ref[k, a] = jnp.where(even, up, down)


def face_source(rolls, weights, inverse, low, high):
    across = []
    for face in (low, high):
        for i in range(3):
            for a in range(7):
                face[i][a] = face[i][a] * (inverse * float(-DELTA_T / (2.0 * FACTOR[a])))
        across.append(
            [derive_sheets(face[0], a) + derive_span(rolls, face[2][a][None])[0] for a in range(7)]
        )
    sheets = []
    for a in range(7):
        rows = []
        for b in range(7):
            total = float(DERIV[b, 0]) * low[1][a] + float(DERIV[b, 6]) * high[1][a]
            if b == 0:
                total = total + across[0][a]
            if b == 6:
                total = total + across[1][a]
            rows.append(total * (weights * float(-1.0 / DELTA_T * WEIGHTS[a] * WEIGHTS[b])))
        sheets.append(jnp.stack(rows, axis=0))
    return sheets


def correct_kernel(
    part_ref, far_y_ref, near_y_ref, first_ref, last_ref, out_ref, far_ref, near_ref, class_out
):
    rolls = span_rolls()
    weights = span_vector(WEIGHTS)
    inverse = span_vector(1.0 / FACTOR)
    _, by, _ = iotas((8, LANES))
    received = [
        [lower_upper("dom", near_y_ref[k, a], far_y_ref[k, a]) for a in range(7)] for k in range(2)
    ]

    def chosen(place, values):
        return jnp.where(by == place, values, 0.0)

    each = [(i, range(7)) for i in range(3)]
    own = face_source(
        rolls, weights, inverse,
        [[chosen(0, lanes_from(received[1][a][0], i, 0)) for a in r] for i, r in each],
        [[chosen(BY - 1, lanes_from(received[1][a][1], i, LANES - BZ)) for a in r] for i, r in each],
    )
    other = face_source(
        rolls, weights, inverse,
        [[chosen(1, pltpu.roll(last_ref[i, a], 2 * BZ, 1)) for a in r] for i, r in each],
        [[chosen(0, first_ref[i, a]) for a in r] for i, r in each],
    )
    for a in range(7):
        mine = part_ref[0, a] + join_local(own[a])
        low, high = received[0][a]
        theirs = join_span(other[a]) + jnp.stack(
            [
                chosen(0, lanes_from(low, b, 0)) + chosen(1, lanes_from(high, b, BZ))
                for b in range(7)
            ],
            axis=0,
        )
        out_ref[0, a], out_ref[1, a] = mine, theirs
        out_ref[0, a, 0] = mine[0] + chosen(0, theirs[6])
        out_ref[0, a, 6] = mine[6] + chosen(BY - 1, pltpu.roll(theirs[0], LANES - 2 * BZ, 1))
        out_ref[1, a, 6] = theirs[6] + chosen(0, mine[0])
        out_ref[1, a, 0] = theirs[0] + chosen(1, pltpu.roll(mine[6], 2 * BZ, 1))
    for k in range(2):
        emit_faces(out_ref, far_ref, near_ref, k)
    low, high = received[0][0]
    class_out[...] = chosen(0, lanes_from(low, 7, 0)) + chosen(1, lanes_from(high, 7, BZ))


def gather_modes(full_ref, modes_ref):
    modes_ref[216:224] = jnp.zeros((8, LANES), F32)
    for compact, padded, rows in RUNS:
        modes_ref[compact : compact + rows] = full_ref[padded : padded + rows]


def terms(values):
    high = values.astype(BF16)
    rest = values - high.astype(F32)
    middle = rest.astype(BF16)
    return high, middle, (rest - middle.astype(F32)).astype(BF16)


HALF = 8


def split_kernel(half, schur_hbm, split_ref, schur_ref, left_ref, right_ref, sems):
    copies = [
        pltpu.make_async_copy(
            schur_hbm.at[pl.ds(109 * k, 109), pl.ds(HALF * half, HALF)],
            schur_ref.at[pl.ds(109 * k, 109)],
            sems.at[k],
        )
        for k in range(2)
    ]
    for copy in copies:
        copy.start()
    for k in range(3):
        split_ref[224 * k + 208 : 224 * k + 224] = jnp.zeros((16, 256 * HALF), BF16)
    right_ref[...] = jnp.zeros(right_ref.shape, F32)
    for copy in copies:
        copy.wait()
    left_ref[...] = schur_ref[:, :, :LANES].reshape(MODES * HALF, LANES)
    right_ref[:, : MODES - LANES] = schur_ref[:, :, LANES:].reshape(MODES * HALF, MODES - LANES)
    for c in range(HALF):
        for side, side_ref in enumerate((left_ref, right_ref)):
            block = side_ref[pl.ds(c, MODES, stride=HALF), :]
            place = LANES * (2 * c + side)
            for k, term in enumerate(terms(block)):
                split_ref[224 * k : 224 * k + MODES, place : place + LANES] = term


def split_half(schur, half):
    return call(
        functools.partial(split_kernel, half),
        [((672, 256 * HALF), BF16)],
        (schur,),
        [
            (MODES, HALF, MODES),
            *[(MODES * HALF, LANES)] * 2,
            pltpu.SemaphoreType.DMA((2,)),
        ],
        name="split",
        hbm=(0,),
    )[0]


def multiply_blocks(splits, class_ref, modes_ref, image_ref, right_ref, last_ref, ghost=None):
    high, middle, low = terms(modes_ref[...])
    pair = jnp.concatenate([high, middle], axis=1)
    mine = class_ref[0:1, :]
    both, last_both, rows = jnp.concatenate([mine, mine], axis=1), mine, 224
    if ghost is not None:
        modes, classes = (
            x + pltpu.roll(x, 32, 1) + pltpu.roll(x, 64, 1) for x in (ghost[0], ghost[1])
        )
        lane = lax.broadcasted_iota(jnp.int32, modes.shape, 1)
        three = [
            jnp.where((lane >= 32 * k) & (lane < 32 * k + 32), term.astype(F32), 0.0)
            for k, term in enumerate(terms(modes))
        ]
        low = jnp.concatenate([low, (three[0] + three[1] + three[2]).astype(BF16)], axis=1)
        last_both, rows = jnp.concatenate([mine, classes[0:1]], axis=1), 672
    zeros = jnp.zeros((32, 2 * LANES), BF16)
    for c in range(CLASSES):
        chosen, last_chosen = (
            jnp.where(jnp.abs(x - float(c)) < 0.5, 1.0, 0.0).astype(BF16) for x in (both, last_both)
        )
        right_ref[256 * c : 256 * c + 224] = pair * chosen
        right_ref[256 * c + 224 : 256 * c + 256] = zeros
        last_ref[256 * c : 256 * c + 224] = low * last_chosen
        last_ref[256 * c + 224 : 256 * c + 256] = zeros[:, : low.shape[1]]
    total, small = 0.0, 0.0
    for half, split_ref in enumerate(splits):
        part = pl.ds(256 * HALF * half, 256 * HALF)
        total = total + jnp.dot(split_ref[...], right_ref[part], preferred_element_type=F32)
        small = small + jnp.dot(split_ref[0:rows], last_ref[part], preferred_element_type=F32)
    total = total[:, :LANES] + total[:, LANES:]
    image_ref[...] = total[0:224] + (total[224:448] + (total[448:672] + small[0:224, :LANES]))
    if ghost is None:
        return None
    extra = small[:, LANES:]
    extra = extra[0:224] + (extra[224:448] + extra[448:672])
    return extra + (pltpu.roll(extra, LANES - 32, 1) + pltpu.roll(extra, LANES - 64, 1))


def scatter_modes(image_ref, full_ref, out_ref):
    full_ref[...] = jnp.zeros((392, LANES), F32)
    for compact, padded, rows in RUNS:
        full_ref[padded : padded + rows] = image_ref[compact : compact + rows]
    for a in range(7):
        out_ref[0, a] = join_local(full_ref[56 * a : 56 * a + 56].reshape(7, 8, LANES))


def total_of(values):
    return jnp.sum(jnp.sum(values, axis=0, keepdims=True), axis=1, keepdims=True)


def first_apply_kernel(
    part_ref, far_x_ref, near_x_ref, split_0, split_1, class_ref, ghost_class_ref,
    load_ref, image_ref, out_ref, far_ref, near_ref,
    full_ref, ghost_ref, ghost_modes_ref, side_ref, right_ref, last_ref,
):
    _, by, _ = iotas((8, LANES))
    for k, padded_ref in enumerate((full_ref, ghost_ref)):
        for a in range(7):
            sheet = add_streamwise(a, part_ref[k, a], far_x_ref[k], near_x_ref[k])
            padded_ref[56 * a : 56 * a + 56] = sheet.reshape(56, LANES)
    gather_modes(full_ref, load_ref)
    gather_modes(ghost_ref, ghost_modes_ref)
    ghost_image = multiply_blocks(
        (split_0, split_1), class_ref, load_ref, image_ref, right_ref, last_ref,
        (ghost_modes_ref[...], ghost_class_ref[...]),
    )
    scatter_modes(image_ref, full_ref, out_ref)
    ghost_modes_ref[...] = ghost_image
    side_ref[...] = jnp.zeros(side_ref.shape, F32)
    for k, b in enumerate((6, 0)):
        for a in range(7):
            row = FACE_ROWS[7 * a + b]
            side_ref[k, a, 0:7] = ghost_modes_ref[row : row + 7]
    below, above = join_span(side_ref[0]), join_span(side_ref[1])
    for a in range(7):
        out_ref[0, a, 0] += jnp.where(by == 0, below[a], 0.0)
        out_ref[0, a, 6] += jnp.where(by == BY - 1, pltpu.roll(above[a], LANES - 2 * BZ, 1), 0.0)
    emit_faces(out_ref, far_ref, near_ref, 0)


def second_apply_kernel(
    part_ref, far_x_ref, near_x_ref, split_0, split_1, class_ref, load_ref, first_ref, shell_ref,
    power_ref, send_ref, out_ref, image_ref, full_ref, right_ref, last_ref,
):
    for a in range(7):
        sheet = add_streamwise(a, part_ref[0, a], far_x_ref[0], near_x_ref[0])
        full_ref[56 * a : 56 * a + 56] = sheet.reshape(56, LANES)
    gather_modes(full_ref, power_ref)
    multiply_blocks((split_0, split_1), class_ref, power_ref, image_ref, right_ref, last_ref)
    scatter_modes(image_ref, full_ref, out_ref)
    load, power, shell = load_ref[...], power_ref[...], shell_ref[...]
    first, image = first_ref[...], image_ref[...]
    lane = lax.broadcasted_iota(jnp.int32, (1, LANES), 1)
    dots = jnp.zeros((1, LANES), F32)
    values = (
        load * load * shell, load * first, power * power * shell, load * image, power * image
    )
    for k, value in enumerate(values):
        dots = dots + jnp.where(lane == k, total_of(value), 0.0)
    node = lax.broadcasted_iota(jnp.int32, (8, LANES), 0)
    count = send_ref.shape[0]
    mine = lax.axis_index("dom")
    alone = jnp.where(node == 7, dots, 0.0)
    send_ref[...] = jnp.broadcast_to(alone[None], send_ref.shape)
    up = pack_groups([out_ref[0, a, 6] for a in range(7)], LANES - BZ)
    down = pack_groups([out_ref[0, a, 0] for a in range(7)], 0)
    send_ref[lax.rem(mine + 1, count)] = jnp.where(node == 7, dots, up)
    send_ref[lax.rem(mine + count - 1, count)] = jnp.where(node == 7, dots, down)


def middle_kernel(part_ref, got_ref, far_ref, near_ref, low_ref, high_ref, sums_ref):
    node = lax.broadcasted_iota(jnp.int32, (8, LANES), 0)
    count = got_ref.shape[0]
    mine = lax.axis_index("dom")
    low = jnp.where(node < 7, got_ref[lax.rem(mine + count - 1, count)], 0.0)
    high = jnp.where(node < 7, got_ref[lax.rem(mine + 1, count)], 0.0)
    faces = []
    for a in range(7):
        low_ref[a], high_ref[a] = lanes_from(low, a, 0), lanes_from(high, a, LANES - BZ)
        if a in (0, 6):
            faces.append(add_second(part_ref[0, a], low_ref[a], high_ref[a]))
    even = even_place("slab", faces[0])
    far_ref[0] = jnp.where(even, faces[0], faces[1])
    near_ref[0] = jnp.where(even, faces[1], faces[0])
    total = jnp.sum(got_ref[...], axis=0)[7:8]
    sums_ref[...] = jnp.broadcast_to(total[None], sums_ref.shape)


def finish_kernel(
    part_ref, far_x_ref, near_x_ref, low_ref, high_ref, load_ref, power_ref, dots_ref, slot_ref,
    pressure_ref, residual_ref, full_ref, modes_ref,
):
    for a in range(7):
        sheet = add_streamwise(a, part_ref[0, a], far_x_ref[0], near_x_ref[0])
        sheet = add_second(sheet, low_ref[a], high_ref[a])
        full_ref[56 * a : 56 * a + 56] = sheet.reshape(56, LANES)
    gather_modes(full_ref, modes_ref)
    dots = jnp.sum(dots_ref[...], axis=0)[0:1]
    square, energy, power_square, cross, power_energy = (dots[:, k : k + 1] for k in range(5))
    step = square / energy
    fresh = square - 2.0 * step * energy + step * step * power_square
    ratio = fresh / square
    grow = 1.0 + ratio
    curvature = (
        grow * grow * energy
        - step * grow * (cross + power_square)
        + step * step * power_energy
    )
    second = fresh / curvature
    load, power, twice = load_ref[...], power_ref[...], modes_ref[...]
    pressure = step * load + second * (grow * load - step * power)
    residual = load - step * power - second * (grow * power - step * twice)
    one_hot = permutation(slot_ref)
    pressure_ref[...] = moved(pressure, one_hot, TO_STORED)[:MODES]
    residual_ref[...] = moved(residual, one_hot, TO_STORED)[:MODES]


def call(kernel, outs, args, scratch=(), name=None, hbm=()):
    vmem = pl.BlockSpec(memory_space=pltpu.VMEM)
    places = [pl.BlockSpec(memory_space=pltpu.HBM) if k in hbm else vmem for k in range(len(args))]
    args = [
        pltpu.with_memory_space_constraint(x, pltpu.HBM) if k in hbm else x
        for k, x in enumerate(args)
    ]
    return pl.pallas_call(
        kernel,
        out_shape=tuple(
            jax.ShapeDtypeStruct(*(o if isinstance(o[0], tuple) else (o, F32))) for o in outs
        ),
        in_specs=places,
        out_specs=tuple([vmem] * len(outs)),
        scratch_shapes=[pltpu.VMEM(s, F32) if isinstance(s, tuple) else s for s in scratch],
        compiler_params=pltpu.CompilerParams(vmem_limit_bytes=24 << 20),
        name=name,
    )(*args)


def partners(axis):
    count = lax.axis_size(axis)
    far = [(i, (i + 1) % count if i % 2 else (i - 1) % count) for i in range(count)]
    near = [(i, i ^ 1) for i in range(count)]
    return far, near


def swap(axis, far, near):
    far_pairs, near_pairs = partners(axis)
    return lax.ppermute(far, axis, far_pairs), lax.ppermute(near, axis, near_pairs)


def per_device(velocity, slot_map, class_index, schur_blocks):
    slots = slot_map.reshape(1, LANES)
    shell = jnp.asarray(SHELL)
    schur = schur_blocks.transpose(1, 0, 2)
    face = (7, 8, LANES)
    whole = (7, 7, 8, LANES)
    modes = (224, LANES)
    rights = [pltpu.VMEM((256 * CLASSES, n), BF16) for n in (2 * LANES, LANES)]
    brick, part, far, near, classes = call(
        advect_kernel,
        [(3, *whole), (3, *whole), (3, *face), (3, *face), (8, LANES)],
        (velocity, slots, class_index.reshape(1, LANES)),
        [
            (3, NODES, LANES),
            pltpu.VMEM((1, LANES), jnp.int32),
            pltpu.VMEM((1, LANES), jnp.int32),
            pltpu.SemaphoreType.DMA((5,)),
        ],
        name="advect",
        hbm=(0, 1, 2),
    )
    swapped = swap("slab", far, near)
    part, split_0 = lax.optimization_barrier((part, split_half(schur, 0)))
    part, far, near, first_side, last_side = call(
        source_kernel,
        [(1, *whole), (2, *face), (2, *face), (3, *face), (3, *face)],
        (part, *swapped, brick, classes),
        [(3, *whole)],
        name="source",
    )
    part, far, near, ghost_classes = call(
        correct_kernel,
        [(2, *whole), (2, *face), (2, *face), (8, LANES)],
        (part, *swap("dom", far, near), first_side, last_side),
        name="correct",
    )
    swapped = swap("slab", far, near)
    part, split_1 = lax.optimization_barrier((part, split_half(schur, 1)))
    load, first, part, far, near = call(
        first_apply_kernel,
        [modes, modes, (1, *whole), (1, *face), (1, *face)],
        (part, *swapped, split_0, split_1, classes, ghost_classes),
        [(392, LANES), (392, LANES), modes, (2, *face), rights[0], rights[0]],
        name="first",
    )
    slabs, doms = lax.axis_size("slab"), lax.axis_size("dom")
    power, send, part = call(
        second_apply_kernel,
        [modes, (doms, 8, LANES), (1, *whole)],
        (part, *swap("slab", far, near), split_0, split_1, classes, load, first, shell),
        [modes, (392, LANES), *rights],
        name="second",
    )
    far, near, low, high, sums = call(
        middle_kernel,
        [(1, *face), (1, *face), face, face, (slabs, 4, LANES)],
        (part, lax.all_to_all(send, "dom", 0, 0)),
        name="middle",
    )
    dots = lax.all_to_all(sums, "slab", 0, 0)
    return call(
        finish_kernel,
        [(MODES, LANES), (MODES, LANES)],
        (part, *swap("slab", far, near), low, high, load, power, dots, slots),
        [(392, LANES), modes],
        name="finish",
    )


def solution(mesh):
    return jax.shard_map(
        per_device,
        mesh=mesh,
        in_specs=(
            P(None, None, ("slab", "dom")),
            P("slab", "dom", None),
            P("slab", "dom", None),
            P(),
        ),
        out_specs=(P(None, ("slab", "dom")), P(None, ("slab", "dom"))),
        check_vma=False,
    )
```

```python
import functools

import jax
import jax.numpy as jnp
import numpy as np
from jax import lax
from jax.experimental import pallas as pl
from jax.experimental.pallas import tpu as pltpu
from jax.sharding import PartitionSpec as P

CLASSES = 16
MODES = 218
NODES = 343
LANES = 128
BZ = 16
BY = 8
DELTA_T = 0.05
F32 = jnp.float32
BF16 = jnp.bfloat16


def gll_tables():
    degree = 6
    outer_point = 0.830223896278567
    inner_point = 0.46884879347071423
    points = np.array([-1.0, -outer_point, -inner_point, 0.0, inner_point, outer_point, 1.0])
    values = (231.0 * points**6 - 315.0 * points**4 + 105.0 * points**2 - 5.0) / 16.0
    weights = 2.0 / (degree * (degree + 1) * values**2)
    derivative = np.zeros((7, 7))
    for target in range(7):
        for source in range(7):
            if target != source:
                derivative[target, source] = values[target] / (
                    values[source] * (points[target] - points[source])
                )
    derivative[0, 0] = -degree * (degree + 1) / 4.0
    derivative[6, 6] = degree * (degree + 1) / 4.0
    return derivative, weights


DERIV, WEIGHTS = gll_tables()
FACTOR = np.where((np.arange(7) == 0) | (np.arange(7) == 6), 2.0, 1.0)


def shell_runs():
    runs, offset = [], 0
    for a in range(7):
        for b in range(7):
            base = 8 * (7 * a + b)
            if a in (0, 6) or b in (0, 6):
                runs.append((offset, base, 7))
                offset += 7
            else:
                runs.append((offset, base, 1))
                runs.append((offset + 1, base + 6, 1))
                offset += 2
    return runs


RUNS = shell_runs()
FACE_ROWS = {padded // 8: compact for compact, padded, rows in RUNS if rows == 7}


def shell_table():
    multiple = (FACTOR[:, None, None] * FACTOR[None, :, None] * FACTOR[None, None, :]).reshape(-1)
    surface = [
        i for i in range(NODES) if i // 49 in (0, 6) or i // 7 % 7 in (0, 6) or i % 7 in (0, 6)
    ]
    shell = np.zeros((224, LANES))
    shell[:MODES] = (1.0 / multiple[surface])[:, None]
    return shell.astype(np.float32)


SHELL = shell_table()


def span_vector(values):
    node = lax.broadcasted_iota(jnp.int32, (8, LANES), 0)
    table = jnp.zeros((8, LANES), F32)
    for c in range(7):
        table = jnp.where(node == c, float(values[c]), table)
    return table


def span_rolls():
    tables = []
    for shift in range(8):
        sources = [(target - shift) % 8 for target in range(7)]
        tables.append(
            span_vector([DERIV[t, c] if c < 7 else 0.0 for t, c in zip(range(7), sources)])
        )
    return tables


def even_place(axis, like):
    return jnp.full(like.shape, lax.axis_index(axis) % 2, jnp.int32) == 0


def lower_upper(axis, near, far):
    even = even_place(axis, near)
    return jnp.where(even, far, near), jnp.where(even, near, far)


def iotas(shape):
    lane = lax.broadcasted_iota(jnp.int32, shape, len(shape) - 1)
    node = lax.broadcasted_iota(jnp.int32, shape, len(shape) - 2)
    return lane % BZ, lane // BZ, node


def join_span(sheet):
    bz, _, node = iotas(sheet.shape)
    low = pltpu.roll(sheet, 2, 1)
    low = jnp.where(bz == 0, pltpu.roll(low, LANES - 15, 2), pltpu.roll(low, 1, 2))
    high = pltpu.roll(sheet, 6, 1)
    high = jnp.where(bz == BZ - 1, pltpu.roll(high, 15, 2), pltpu.roll(high, LANES - 1, 2))
    return sheet + jnp.where(node == 0, low, jnp.where(node == 6, high, 0.0))


def join_local(sheet):
    sheet = join_span(sheet)
    _, by, _ = iotas(sheet.shape[1:])
    first, last = sheet[0], sheet[6]
    new_first = first + jnp.where(by > 0, pltpu.roll(last, BZ, 1), 0.0)
    new_last = last + jnp.where(by < BY - 1, pltpu.roll(first, LANES - BZ, 1), 0.0)
    return jnp.concatenate([new_first[None], sheet[1:6], new_last[None]], axis=0)


def add_streamwise(a, sheet, far_x, near_x):
    if a == 0:
        sheet = sheet + lower_upper("slab", near_x, far_x)[0]
    if a == 6:
        sheet = sheet + lower_upper("slab", near_x, far_x)[1]
    return sheet


def add_second(sheet, low_y, high_y):
    _, by, _ = iotas(sheet.shape[1:])
    first = sheet[0] + jnp.where(by == 0, low_y, 0.0)
    last = sheet[6] + jnp.where(by == BY - 1, high_y, 0.0)
    return jnp.concatenate([first[None], sheet[1:6], last[None]], axis=0)


def pack_groups(blocks, start):
    _, group, _ = iotas(blocks[0].shape)
    total = jnp.zeros(blocks[0].shape, F32)
    for k, block in enumerate(blocks):
        shift = (BZ * k - start) % LANES
        total = jnp.where(group == k, pltpu.roll(block, shift, 1) if shift else block, total)
    return total


def lanes_from(packed, group, start):
    shift = (start - BZ * group) % LANES
    return pltpu.roll(packed, shift, 1) if shift else packed


def derive_sheets(sheets, target):
    total = float(DERIV[target, 0]) * sheets[0]
    for source in range(1, 7):
        total = total + float(DERIV[target, source]) * sheets[source]
    return total


def derive_span(rolls, sheet):
    total = rolls[0] * sheet
    for shift in range(1, 8):
        total = total + rolls[shift] * pltpu.roll(sheet, shift, 1)
    return total


def permutation(slot_ref):
    position = lax.broadcasted_iota(jnp.int32, (LANES, LANES), 0)
    return jnp.where(position == slot_ref[...], 1.0, 0.0).astype(BF16)


def moved(values, one_hot, dims):
    return sum(
        lax.dot_general(term, one_hot, (dims, ((), ())), preferred_element_type=F32)
        for term in terms(values)
    )


TO_BRICK = ((1,), (1,))
TO_STORED = ((1,), (0,))


def emit_faces(part_ref, far_ref, near_ref, index):
    low, high = part_ref[index, 0], part_ref[index, 6]
    even = even_place("slab", low)
    far_ref[index] = jnp.where(even, low, high)
    near_ref[index] = jnp.where(even, high, low)


def advect_kernel(
    vel_hbm, slot_hbm, class_hbm,
    brick_ref, part_ref, far_ref, near_ref, class_out,
    vel_ref, slot_ref, class_ref, sems,
):
    copies = [
        pltpu.make_async_copy(src, dst, sems.at[k])
        for k, (src, dst) in enumerate(
            (
                (slot_hbm, slot_ref), (class_hbm, class_ref),
                *((vel_hbm.at[i], vel_ref.at[i]) for i in range(3)),
            )
        )
    ]
    for copy in copies:
        copy.start()
    rolls = span_rolls()
    brick_ref[:, :, :, 7:8, :] = jnp.zeros((3, 7, 7, 1, LANES), F32)
    copies[0].wait()
    copies[1].wait()
    one_hot = permutation(slot_ref)
    class_out[...] = moved(
        jnp.broadcast_to(class_ref[...].astype(F32), (8, LANES)), one_hot, TO_BRICK
    )
    for i in range(3):
        copies[2 + i].wait()
        stored = moved(vel_ref[i], one_hot, TO_BRICK)
        for a in range(7):
            for b in range(7):
                row = 7 * (7 * a + b)
                brick_ref[i, a, b, 0:7, :] = stored[row : row + 7]

    def component(i, carry):
        sheets = [brick_ref[i, a] for a in range(7)]
        for a in range(7):
            along_a = derive_sheets(sheets, a)
            sheet = sheets[a]
            along_b = jnp.stack(
                [derive_sheets([sheet[b] for b in range(7)], target) for target in range(7)], axis=0
            )
            along_c = derive_span(rolls, sheet)
            advect = (
                brick_ref[0, a] * along_a + brick_ref[1, a] * along_b + brick_ref[2, a] * along_c
            )
            part_ref[i, a] = join_local(advect)
        emit_faces(part_ref, far_ref, near_ref, i)
        return carry

    lax.fori_loop(0, 3, component, 0)


def source_kernel(
    part_ref, far_x_ref, near_x_ref, brick_ref, class_ref,
    out_ref, far_ref, near_ref, first_ref, last_ref, middle_ref,
):
    rolls = span_rolls()
    weights = span_vector(WEIGHTS)
    inverse = span_vector(1.0 / FACTOR)
    for i in range(3):
        for a in range(7):
            sheet = add_streamwise(a, part_ref[i, a], far_x_ref[i], near_x_ref[i])
            first_ref[i, a], last_ref[i, a] = sheet[0], sheet[6]
            scaled = [
                sheet[b] * (inverse * float(DELTA_T / (FACTOR[a] * FACTOR[b]))) for b in range(7)
            ]
            middle_ref[i, a] = brick_ref[i, a] - jnp.stack(scaled, axis=0)
    sheets = [middle_ref[0, a] for a in range(7)]
    for a in range(7):
        along_a = derive_sheets(sheets, a)
        second = middle_ref[1, a]
        along_b = jnp.stack(
            [derive_sheets([second[b] for b in range(7)], target) for target in range(7)], axis=0
        )
        diverge = along_a + along_b + derive_span(rolls, middle_ref[2, a])
        source = [
            diverge[b] * (weights * float(-1.0 / DELTA_T * WEIGHTS[a] * WEIGHTS[b]))
            for b in range(7)
        ]
        out_ref[0, a] = join_local(jnp.stack(source, axis=0))
    classes = class_ref[...]
    even = even_place("dom", classes)
    for a in range(7):
        rows = [*(out_ref[0, a, b] for b in range(7)), classes]
        pairs = (
            (pack_groups(rows, 0), pack_groups(rows, LANES - BZ)),
            (
                pack_groups([first_ref[i, a] for i in range(3)], 0),
                pack_groups([last_ref[i, a] for i in range(3)], LANES - BZ),
            ),
        )
        for k, (down, up) in enumerate(pairs):
            far_ref[k, a] = jnp.where(even, down, up)
            near_ref[k, a] = jnp.where(even, up, down)


def face_source(rolls, weights, inverse, low, high):
    across = []
    for face in (low, high):
        for i in range(3):
            for a in range(7):
                face[i][a] = face[i][a] * (inverse * float(-DELTA_T / (2.0 * FACTOR[a])))
        across.append(
            [derive_sheets(face[0], a) + derive_span(rolls, face[2][a][None])[0] for a in range(7)]
        )
    sheets = []
    for a in range(7):
        rows = []
        for b in range(7):
            total = float(DERIV[b, 0]) * low[1][a] + float(DERIV[b, 6]) * high[1][a]
            if b == 0:
                total = total + across[0][a]
            if b == 6:
                total = total + across[1][a]
            rows.append(total * (weights * float(-1.0 / DELTA_T * WEIGHTS[a] * WEIGHTS[b])))
        sheets.append(jnp.stack(rows, axis=0))
    return sheets


def correct_kernel(
    part_ref, far_y_ref, near_y_ref, first_ref, last_ref, out_ref, far_ref, near_ref, class_out
):
    rolls = span_rolls()
    weights = span_vector(WEIGHTS)
    inverse = span_vector(1.0 / FACTOR)
    _, by, _ = iotas((8, LANES))
    received = [
        [lower_upper("dom", near_y_ref[k, a], far_y_ref[k, a]) for a in range(7)] for k in range(2)
    ]

    def chosen(place, values):
        return jnp.where(by == place, values, 0.0)

    each = [(i, range(7)) for i in range(3)]
    own = face_source(
        rolls, weights, inverse,
        [[chosen(0, lanes_from(received[1][a][0], i, 0)) for a in r] for i, r in each],
        [[chosen(BY - 1, lanes_from(received[1][a][1], i, LANES - BZ)) for a in r] for i, r in each],
    )
    other = face_source(
        rolls, weights, inverse,
        [[chosen(1, pltpu.roll(last_ref[i, a], 2 * BZ, 1)) for a in r] for i, r in each],
        [[chosen(0, first_ref[i, a]) for a in r] for i, r in each],
    )
    for a in range(7):
        mine = part_ref[0, a] + join_local(own[a])
        low, high = received[0][a]
        theirs = join_span(other[a]) + jnp.stack(
            [
                chosen(0, lanes_from(low, b, 0)) + chosen(1, lanes_from(high, b, BZ))
                for b in range(7)
            ],
            axis=0,
        )
        out_ref[0, a], out_ref[1, a] = mine, theirs
        out_ref[0, a, 0] = mine[0] + chosen(0, theirs[6])
        out_ref[0, a, 6] = mine[6] + chosen(BY - 1, pltpu.roll(theirs[0], LANES - 2 * BZ, 1))
        out_ref[1, a, 6] = theirs[6] + chosen(0, mine[0])
        out_ref[1, a, 0] = theirs[0] + chosen(1, pltpu.roll(mine[6], 2 * BZ, 1))
    for k in range(2):
        emit_faces(out_ref, far_ref, near_ref, k)
    low, high = received[0][0]
    class_out[...] = chosen(0, lanes_from(low, 7, 0)) + chosen(1, lanes_from(high, 7, BZ))


def gather_modes(full_ref, modes_ref):
    modes_ref[216:224] = jnp.zeros((8, LANES), F32)
    for compact, padded, rows in RUNS:
        modes_ref[compact : compact + rows] = full_ref[padded : padded + rows]


def terms(values):
    high = values.astype(BF16)
    rest = values - high.astype(F32)
    middle = rest.astype(BF16)
    return high, middle, (rest - middle.astype(F32)).astype(BF16)


HALF = 8


def split_kernel(half, schur_hbm, split_ref, schur_ref, left_ref, right_ref, sems):
    copies = [
        pltpu.make_async_copy(
            schur_hbm.at[pl.ds(109 * k, 109), pl.ds(HALF * half, HALF)],
            schur_ref.at[pl.ds(109 * k, 109)],
            sems.at[k],
        )
        for k in range(2)
    ]
    for copy in copies:
        copy.start()
    for k in range(2):
        split_ref[224 * k + 208 : 224 * k + 224] = jnp.zeros((16, 256 * HALF), BF16)
    right_ref[...] = jnp.zeros(right_ref.shape, F32)
    for copy in copies:
        copy.wait()
    left_ref[...] = schur_ref[:, :, :LANES].reshape(MODES * HALF, LANES)
    right_ref[:, : MODES - LANES] = schur_ref[:, :, LANES:].reshape(MODES * HALF, MODES - LANES)
    for c in range(HALF):
        for side, side_ref in enumerate((left_ref, right_ref)):
            block = side_ref[pl.ds(c, MODES, stride=HALF), :]
            place = LANES * (2 * c + side)
            for k, term in enumerate(terms(block)[:2]):
                split_ref[224 * k : 224 * k + MODES, place : place + LANES] = term


def split_half(schur, half):
    return call(
        functools.partial(split_kernel, half),
        [((448, 256 * HALF), BF16)],
        (schur,),
        [
            (MODES, HALF, MODES),
            *[(MODES * HALF, LANES)] * 2,
            pltpu.SemaphoreType.DMA((2,)),
        ],
        name="split",
        hbm=(0,),
    )[0]


def multiply_blocks(splits, class_ref, modes_ref, image_ref, right_ref, last_ref, ghost=None):
    high, middle, low = terms(modes_ref[...])
    pair = jnp.concatenate([high, middle], axis=1)
    mine = class_ref[0:1, :]
    both, last_both, rows = jnp.concatenate([mine, mine], axis=1), mine, 224
    if ghost is not None:
        modes, classes = (
            x + pltpu.roll(x, 32, 1) + pltpu.roll(x, 64, 1) for x in (ghost[0], ghost[1])
        )
        lane = lax.broadcasted_iota(jnp.int32, modes.shape, 1)
        three = [
            jnp.where((lane >= 32 * k) & (lane < 32 * k + 32), term.astype(F32), 0.0)
            for k, term in enumerate(terms(modes))
        ]
        low = jnp.concatenate([low, (three[0] + three[1] + three[2]).astype(BF16)], axis=1)
        last_both, rows = jnp.concatenate([mine, classes[0:1]], axis=1), 448
    zeros = jnp.zeros((32, 2 * LANES), BF16)
    for c in range(CLASSES):
        chosen, last_chosen = (
            jnp.where(jnp.abs(x - float(c)) < 0.5, 1.0, 0.0).astype(BF16) for x in (both, last_both)
        )
        right_ref[256 * c : 256 * c + 224] = pair * chosen
        right_ref[256 * c + 224 : 256 * c + 256] = zeros
        last_ref[256 * c : 256 * c + 224] = low * last_chosen
        last_ref[256 * c + 224 : 256 * c + 256] = zeros[:, : low.shape[1]]
    total, small = 0.0, 0.0
    for half, split_ref in enumerate(splits):
        part = pl.ds(256 * HALF * half, 256 * HALF)
        total = total + jnp.dot(split_ref[...], right_ref[part], preferred_element_type=F32)
        small = small + jnp.dot(split_ref[0:rows], last_ref[part], preferred_element_type=F32)
    total = total[:, :LANES] + total[:, LANES:]
    image_ref[...] = total[0:224] + (total[224:448] + small[0:224, :LANES])
    if ghost is None:
        return None
    extra = small[:, LANES:]
    extra = extra[0:224] + extra[224:448]
    return extra + (pltpu.roll(extra, LANES - 32, 1) + pltpu.roll(extra, LANES - 64, 1))


def scatter_modes(image_ref, full_ref, out_ref):
    full_ref[...] = jnp.zeros((392, LANES), F32)
    for compact, padded, rows in RUNS:
        full_ref[padded : padded + rows] = image_ref[compact : compact + rows]
    for a in range(7):
        out_ref[0, a] = join_local(full_ref[56 * a : 56 * a + 56].reshape(7, 8, LANES))


def total_of(values):
    return jnp.sum(jnp.sum(values, axis=0, keepdims=True), axis=1, keepdims=True)


def first_apply_kernel(
    part_ref, far_x_ref, near_x_ref, split_0, split_1, class_ref, ghost_class_ref,
    load_ref, image_ref, out_ref, far_ref, near_ref,
    full_ref, ghost_ref, ghost_modes_ref, side_ref, right_ref, last_ref,
):
    _, by, _ = iotas((8, LANES))
    for k, padded_ref in enumerate((full_ref, ghost_ref)):
        for a in range(7):
            sheet = add_streamwise(a, part_ref[k, a], far_x_ref[k], near_x_ref[k])
            padded_ref[56 * a : 56 * a + 56] = sheet.reshape(56, LANES)
    gather_modes(full_ref, load_ref)
    gather_modes(ghost_ref, ghost_modes_ref)
    ghost_image = multiply_blocks(
        (split_0, split_1), class_ref, load_ref, image_ref, right_ref, last_ref,
        (ghost_modes_ref[...], ghost_class_ref[...]),
    )
    scatter_modes(image_ref, full_ref, out_ref)
    ghost_modes_ref[...] = ghost_image
    side_ref[...] = jnp.zeros(side_ref.shape, F32)
    for k, b in enumerate((6, 0)):
        for a in range(7):
            row = FACE_ROWS[7 * a + b]
            side_ref[k, a, 0:7] = ghost_modes_ref[row : row + 7]
    below, above = join_span(side_ref[0]), join_span(side_ref[1])
    for a in range(7):
        out_ref[0, a, 0] += jnp.where(by == 0, below[a], 0.0)
        out_ref[0, a, 6] += jnp.where(by == BY - 1, pltpu.roll(above[a], LANES - 2 * BZ, 1), 0.0)
    emit_faces(out_ref, far_ref, near_ref, 0)


def second_apply_kernel(
    part_ref, far_x_ref, near_x_ref, split_0, split_1, class_ref, load_ref, first_ref, shell_ref,
    power_ref, send_ref, out_ref, far_ref, near_ref, image_ref, full_ref, right_ref, last_ref,
):
    for a in range(7):
        sheet = add_streamwise(a, part_ref[0, a], far_x_ref[0], near_x_ref[0])
        full_ref[56 * a : 56 * a + 56] = sheet.reshape(56, LANES)
    gather_modes(full_ref, power_ref)
    multiply_blocks((split_0, split_1), class_ref, power_ref, image_ref, right_ref, last_ref)
    scatter_modes(image_ref, full_ref, out_ref)
    emit_faces(out_ref, far_ref, near_ref, 0)
    load, power, shell = load_ref[...], power_ref[...], shell_ref[...]
    first, image = first_ref[...], image_ref[...]
    lane = lax.broadcasted_iota(jnp.int32, (1, LANES), 1)
    dots = jnp.zeros((1, LANES), F32)
    values = (
        load * load * shell, load * first, power * power * shell, load * image, power * image
    )
    for k, value in enumerate(values):
        dots = dots + jnp.where(lane == k, total_of(value), 0.0)
    node = lax.broadcasted_iota(jnp.int32, (8, LANES), 0)
    count = send_ref.shape[0]
    mine = lax.axis_index("dom")
    alone = jnp.where(node == 7, dots, 0.0)
    send_ref[...] = jnp.broadcast_to(alone[None], send_ref.shape)
    up = pack_groups([out_ref[0, a, 6] for a in range(7)], LANES - BZ)
    down = pack_groups([out_ref[0, a, 0] for a in range(7)], 0)
    send_ref[lax.rem(mine + 1, count)] = jnp.where(node == 7, dots, up)
    send_ref[lax.rem(mine + count - 1, count)] = jnp.where(node == 7, dots, down)


def middle_kernel(got_ref, low_ref, high_ref, send_ref):
    node = lax.broadcasted_iota(jnp.int32, (8, LANES), 0)
    _, by, _ = iotas((8, LANES))
    count = got_ref.shape[0]
    mine = lax.axis_index("dom")
    low = jnp.where(node < 7, got_ref[lax.rem(mine + count - 1, count)], 0.0)
    high = jnp.where(node < 7, got_ref[lax.rem(mine + 1, count)], 0.0)
    for a in range(7):
        low_ref[a], high_ref[a] = lanes_from(low, a, 0), lanes_from(high, a, LANES - BZ)
    total = jnp.sum(got_ref[...], axis=0)[7:8]
    send_ref[...] = jnp.broadcast_to(jnp.where(node == 7, total, 0.0)[None], send_ref.shape)
    slabs = send_ref.shape[0]
    place = lax.axis_index("slab")
    for a, step in ((6, 1), (0, slabs - 1)):
        edges = jnp.where(by == 0, low_ref[a], jnp.where(by == BY - 1, high_ref[a], 0.0))
        send_ref[lax.rem(place + step, slabs)] = jnp.where(node == 7, total, edges)


def finish_kernel(
    part_ref, far_x_ref, near_x_ref, low_ref, high_ref, load_ref, power_ref, dots_ref, slot_ref,
    pressure_ref, residual_ref, full_ref, modes_ref,
):
    node = lax.broadcasted_iota(jnp.int32, (8, LANES), 0)
    slabs = dots_ref.shape[0]
    place = lax.axis_index("slab")
    for a in range(7):
        sheet = add_streamwise(a, part_ref[0, a], far_x_ref[0], near_x_ref[0])
        sheet = add_second(sheet, low_ref[a], high_ref[a])
        if a in (0, 6):
            edges = dots_ref[lax.rem(place + (slabs - 1 if a == 0 else 1), slabs)]
            edges = jnp.where(node < 7, edges, 0.0)
            sheet = add_second(sheet, edges, edges)
        full_ref[56 * a : 56 * a + 56] = sheet.reshape(56, LANES)
    gather_modes(full_ref, modes_ref)
    dots = jnp.sum(dots_ref[...], axis=0)[7:8]
    square, energy, power_square, cross, power_energy = (dots[:, k : k + 1] for k in range(5))
    step = square / energy
    fresh = square - 2.0 * step * energy + step * step * power_square
    ratio = fresh / square
    grow = 1.0 + ratio
    curvature = (
        grow * grow * energy
        - step * grow * (cross + power_square)
        + step * step * power_energy
    )
    second = fresh / curvature
    load, power, twice = load_ref[...], power_ref[...], modes_ref[...]
    pressure = step * load + second * (grow * load - step * power)
    residual = load - step * power - second * (grow * power - step * twice)
    one_hot = permutation(slot_ref)
    pressure_ref[...] = moved(pressure, one_hot, TO_STORED)[:MODES]
    residual_ref[...] = moved(residual, one_hot, TO_STORED)[:MODES]


def call(kernel, outs, args, scratch=(), name=None, hbm=()):
    vmem = pl.BlockSpec(memory_space=pltpu.VMEM)
    places = [pl.BlockSpec(memory_space=pltpu.HBM) if k in hbm else vmem for k in range(len(args))]
    args = [
        pltpu.with_memory_space_constraint(x, pltpu.HBM) if k in hbm else x
        for k, x in enumerate(args)
    ]
    return pl.pallas_call(
        kernel,
        out_shape=tuple(
            jax.ShapeDtypeStruct(*(o if isinstance(o[0], tuple) else (o, F32))) for o in outs
        ),
        in_specs=places,
        out_specs=tuple([vmem] * len(outs)),
        scratch_shapes=[pltpu.VMEM(s, F32) if isinstance(s, tuple) else s for s in scratch],
        compiler_params=pltpu.CompilerParams(vmem_limit_bytes=24 << 20),
        name=name,
    )(*args)


def partners(axis):
    count = lax.axis_size(axis)
    far = [(i, (i + 1) % count if i % 2 else (i - 1) % count) for i in range(count)]
    near = [(i, i ^ 1) for i in range(count)]
    return far, near


def swap(axis, far, near):
    far_pairs, near_pairs = partners(axis)
    return lax.ppermute(far, axis, far_pairs), lax.ppermute(near, axis, near_pairs)


def per_device(velocity, slot_map, class_index, schur_blocks):
    slots = slot_map.reshape(1, LANES)
    shell = jnp.asarray(SHELL)
    schur = schur_blocks.transpose(1, 0, 2)
    face = (7, 8, LANES)
    whole = (7, 7, 8, LANES)
    modes = (224, LANES)
    rights = [pltpu.VMEM((256 * CLASSES, n), BF16) for n in (2 * LANES, LANES)]
    brick, part, far, near, classes = call(
        advect_kernel,
        [(3, *whole), (3, *whole), (3, *face), (3, *face), (8, LANES)],
        (velocity, slots, class_index.reshape(1, LANES)),
        [
            (3, NODES, LANES),
            pltpu.VMEM((1, LANES), jnp.int32),
            pltpu.VMEM((1, LANES), jnp.int32),
            pltpu.SemaphoreType.DMA((5,)),
        ],
        name="advect",
        hbm=(0, 1, 2),
    )
    swapped = swap("slab", far, near)
    part, split_0 = lax.optimization_barrier((part, split_half(schur, 0)))
    part, far, near, first_side, last_side = call(
        source_kernel,
        [(1, *whole), (2, *face), (2, *face), (3, *face), (3, *face)],
        (part, *swapped, brick, classes),
        [(3, *whole)],
        name="source",
    )
    part, far, near, ghost_classes = call(
        correct_kernel,
        [(2, *whole), (2, *face), (2, *face), (8, LANES)],
        (part, *swap("dom", far, near), first_side, last_side),
        name="correct",
    )
    swapped = swap("slab", far, near)
    part, split_1 = lax.optimization_barrier((part, split_half(schur, 1)))
    load, first, part, far, near = call(
        first_apply_kernel,
        [modes, modes, (1, *whole), (1, *face), (1, *face)],
        (part, *swapped, split_0, split_1, classes, ghost_classes),
        [(392, LANES), (392, LANES), modes, (2, *face), rights[0], rights[0]],
        name="first",
    )
    slabs, doms = lax.axis_size("slab"), lax.axis_size("dom")
    power, send, part, far, near = call(
        second_apply_kernel,
        [modes, (doms, 8, LANES), (1, *whole), (1, *face), (1, *face)],
        (part, *swap("slab", far, near), split_0, split_1, classes, load, first, shell),
        [modes, (392, LANES), *rights],
        name="second",
    )
    got = lax.all_to_all(send, "dom", 0, 0)
    far_x, near_x = swap("slab", far, near)
    got, near_x = lax.optimization_barrier((got, near_x))
    low, high, send = call(
        middle_kernel, [face, face, (slabs, 8, LANES)], (got,), name="middle"
    )
    dots = lax.all_to_all(send, "slab", 0, 0)
    return call(
        finish_kernel,
        [(MODES, LANES), (MODES, LANES)],
        (part, far_x, near_x, low, high, load, power, dots, slots),
        [(392, LANES), modes],
        name="finish",
    )


def solution(mesh):
    return jax.shard_map(
        per_device,
        mesh=mesh,
        in_specs=(
            P(None, None, ("slab", "dom")),
            P("slab", "dom", None),
            P("slab", "dom", None),
            P(),
        ),
        out_specs=(P(None, ("slab", "dom")), P(None, ("slab", "dom"))),
        check_vma=False,
    )
```

```python
import functools

import jax
import jax.numpy as jnp
import numpy as np
from jax import lax
from jax.experimental import pallas as pl
from jax.experimental.pallas import tpu as pltpu
from jax.sharding import PartitionSpec as P

CLASSES = 16
MODES = 218
NODES = 343
LANES = 128
BZ = 16
BY = 8
DELTA_T = 0.05
F32 = jnp.float32
BF16 = jnp.bfloat16


def gll_tables():
    degree = 6
    outer_point = 0.830223896278567
    inner_point = 0.46884879347071423
    points = np.array([-1.0, -outer_point, -inner_point, 0.0, inner_point, outer_point, 1.0])
    values = (231.0 * points**6 - 315.0 * points**4 + 105.0 * points**2 - 5.0) / 16.0
    weights = 2.0 / (degree * (degree + 1) * values**2)
    derivative = np.zeros((7, 7))
    for target in range(7):
        for source in range(7):
            if target != source:
                derivative[target, source] = values[target] / (
                    values[source] * (points[target] - points[source])
                )
    derivative[0, 0] = -degree * (degree + 1) / 4.0
    derivative[6, 6] = degree * (degree + 1) / 4.0
    return derivative, weights


DERIV, WEIGHTS = gll_tables()
FACTOR = np.where((np.arange(7) == 0) | (np.arange(7) == 6), 2.0, 1.0)


def shell_runs():
    runs, offset = [], 0
    for a in range(7):
        for b in range(7):
            base = 8 * (7 * a + b)
            if a in (0, 6) or b in (0, 6):
                runs.append((offset, base, 7))
                offset += 7
            else:
                runs.append((offset, base, 1))
                runs.append((offset + 1, base + 6, 1))
                offset += 2
    return runs


RUNS = shell_runs()
FACE_ROWS = {padded // 8: compact for compact, padded, rows in RUNS if rows == 7}


def shell_table():
    multiple = (FACTOR[:, None, None] * FACTOR[None, :, None] * FACTOR[None, None, :]).reshape(-1)
    surface = [
        i for i in range(NODES) if i // 49 in (0, 6) or i // 7 % 7 in (0, 6) or i % 7 in (0, 6)
    ]
    shell = np.zeros((224, LANES))
    shell[:MODES] = (1.0 / multiple[surface])[:, None]
    return shell.astype(np.float32)


SHELL = shell_table()


def span_vector(values):
    node = lax.broadcasted_iota(jnp.int32, (8, LANES), 0)
    table = jnp.zeros((8, LANES), F32)
    for c in range(7):
        table = jnp.where(node == c, float(values[c]), table)
    return table


def span_rolls():
    tables = []
    for shift in range(8):
        sources = [(target - shift) % 8 for target in range(7)]
        tables.append(
            span_vector([DERIV[t, c] if c < 7 else 0.0 for t, c in zip(range(7), sources)])
        )
    return tables


def even_place(axis, like):
    return jnp.full(like.shape, lax.axis_index(axis) % 2, jnp.int32) == 0


def lower_upper(axis, near, far):
    even = even_place(axis, near)
    return jnp.where(even, far, near), jnp.where(even, near, far)


def iotas(shape):
    lane = lax.broadcasted_iota(jnp.int32, shape, len(shape) - 1)
    node = lax.broadcasted_iota(jnp.int32, shape, len(shape) - 2)
    return lane % BZ, lane // BZ, node


def join_span(sheet):
    bz, _, node = iotas(sheet.shape)
    low = pltpu.roll(sheet, 2, 1)
    low = jnp.where(bz == 0, pltpu.roll(low, LANES - 15, 2), pltpu.roll(low, 1, 2))
    high = pltpu.roll(sheet, 6, 1)
    high = jnp.where(bz == BZ - 1, pltpu.roll(high, 15, 2), pltpu.roll(high, LANES - 1, 2))
    return sheet + jnp.where(node == 0, low, jnp.where(node == 6, high, 0.0))


def join_local(sheet):
    sheet = join_span(sheet)
    _, by, _ = iotas(sheet.shape[1:])
    first, last = sheet[0], sheet[6]
    new_first = first + jnp.where(by > 0, pltpu.roll(last, BZ, 1), 0.0)
    new_last = last + jnp.where(by < BY - 1, pltpu.roll(first, LANES - BZ, 1), 0.0)
    return jnp.concatenate([new_first[None], sheet[1:6], new_last[None]], axis=0)


def add_streamwise(a, sheet, far_x, near_x):
    if a == 0:
        sheet = sheet + lower_upper("slab", near_x, far_x)[0]
    if a == 6:
        sheet = sheet + lower_upper("slab", near_x, far_x)[1]
    return sheet


def add_second(sheet, low_y, high_y):
    _, by, _ = iotas(sheet.shape[1:])
    first = sheet[0] + jnp.where(by == 0, low_y, 0.0)
    last = sheet[6] + jnp.where(by == BY - 1, high_y, 0.0)
    return jnp.concatenate([first[None], sheet[1:6], last[None]], axis=0)


def pack_groups(blocks, start):
    _, group, _ = iotas(blocks[0].shape)
    total = jnp.zeros(blocks[0].shape, F32)
    for k, block in enumerate(blocks):
        shift = (BZ * k - start) % LANES
        total = jnp.where(group == k, pltpu.roll(block, shift, 1) if shift else block, total)
    return total


def lanes_from(packed, group, start):
    shift = (start - BZ * group) % LANES
    return pltpu.roll(packed, shift, 1) if shift else packed


def derive_sheets(sheets, target):
    total = float(DERIV[target, 0]) * sheets[0]
    for source in range(1, 7):
        total = total + float(DERIV[target, source]) * sheets[source]
    return total


def derive_span(rolls, sheet):
    total = rolls[0] * sheet
    for shift in range(1, 8):
        total = total + rolls[shift] * pltpu.roll(sheet, shift, 1)
    return total


def permutation(slot_ref):
    position = lax.broadcasted_iota(jnp.int32, (LANES, LANES), 0)
    return jnp.where(position == slot_ref[...], 1.0, 0.0).astype(BF16)


def moved(values, one_hot, dims):
    return sum(
        lax.dot_general(term, one_hot, (dims, ((), ())), preferred_element_type=F32)
        for term in terms(values)
    )


TO_BRICK = ((1,), (1,))
TO_STORED = ((1,), (0,))


def emit_faces(part_ref, far_ref, near_ref, index):
    low, high = part_ref[index, 0], part_ref[index, 6]
    even = even_place("slab", low)
    far_ref[index] = jnp.where(even, low, high)
    near_ref[index] = jnp.where(even, high, low)


def advect_kernel(
    vel_hbm, slot_hbm, class_hbm,
    brick_ref, part_ref, far_ref, near_ref, class_out,
    vel_ref, slot_ref, class_ref, sems,
):
    copies = [
        pltpu.make_async_copy(src, dst, sems.at[k])
        for k, (src, dst) in enumerate(
            (
                (slot_hbm, slot_ref), (class_hbm, class_ref),
                *((vel_hbm.at[i], vel_ref.at[i]) for i in range(3)),
            )
        )
    ]
    for copy in copies:
        copy.start()
    rolls = span_rolls()
    brick_ref[:, :, :, 7:8, :] = jnp.zeros((3, 7, 7, 1, LANES), F32)
    copies[0].wait()
    copies[1].wait()
    one_hot = permutation(slot_ref)
    class_out[...] = moved(
        jnp.broadcast_to(class_ref[...].astype(F32), (8, LANES)), one_hot, TO_BRICK
    )
    for i in range(3):
        copies[2 + i].wait()
        stored = moved(vel_ref[i], one_hot, TO_BRICK)
        for a in range(7):
            for b in range(7):
                row = 7 * (7 * a + b)
                brick_ref[i, a, b, 0:7, :] = stored[row : row + 7]

    def component(i, carry):
        sheets = [brick_ref[i, a] for a in range(7)]
        for a in range(7):
            along_a = derive_sheets(sheets, a)
            sheet = sheets[a]
            along_b = jnp.stack(
                [derive_sheets([sheet[b] for b in range(7)], target) for target in range(7)], axis=0
            )
            along_c = derive_span(rolls, sheet)
            advect = (
                brick_ref[0, a] * along_a + brick_ref[1, a] * along_b + brick_ref[2, a] * along_c
            )
            part_ref[i, a] = join_local(advect)
        emit_faces(part_ref, far_ref, near_ref, i)
        return carry

    lax.fori_loop(0, 3, component, 0)


def source_kernel(
    part_ref, far_x_ref, near_x_ref, brick_ref, class_ref,
    out_ref, far_ref, near_ref, first_ref, last_ref, middle_ref,
):
    rolls = span_rolls()
    weights = span_vector(WEIGHTS)
    inverse = span_vector(1.0 / FACTOR)
    for i in range(3):
        for a in range(7):
            sheet = add_streamwise(a, part_ref[i, a], far_x_ref[i], near_x_ref[i])
            first_ref[i, a], last_ref[i, a] = sheet[0], sheet[6]
            scaled = [
                sheet[b] * (inverse * float(DELTA_T / (FACTOR[a] * FACTOR[b]))) for b in range(7)
            ]
            middle_ref[i, a] = brick_ref[i, a] - jnp.stack(scaled, axis=0)
    sheets = [middle_ref[0, a] for a in range(7)]
    for a in range(7):
        along_a = derive_sheets(sheets, a)
        second = middle_ref[1, a]
        along_b = jnp.stack(
            [derive_sheets([second[b] for b in range(7)], target) for target in range(7)], axis=0
        )
        diverge = along_a + along_b + derive_span(rolls, middle_ref[2, a])
        source = [
            diverge[b] * (weights * float(-1.0 / DELTA_T * WEIGHTS[a] * WEIGHTS[b]))
            for b in range(7)
        ]
        out_ref[0, a] = join_local(jnp.stack(source, axis=0))
    classes = class_ref[...]
    even = even_place("dom", classes)
    for a in range(7):
        rows = [*(out_ref[0, a, b] for b in range(7)), classes]
        pairs = (
            (pack_groups(rows, 0), pack_groups(rows, LANES - BZ)),
            (
                pack_groups([first_ref[i, a] for i in range(3)], 0),
                pack_groups([last_ref[i, a] for i in range(3)], LANES - BZ),
            ),
        )
        for k, (down, up) in enumerate(pairs):
            far_ref[k, a] = jnp.where(even, down, up)
            near_ref[k, a] = jnp.where(even, up, down)


def face_source(rolls, weights, inverse, low, high):
    across = []
    for face in (low, high):
        for i in range(3):
            for a in range(7):
                face[i][a] = face[i][a] * (inverse * float(-DELTA_T / (2.0 * FACTOR[a])))
        across.append(
            [derive_sheets(face[0], a) + derive_span(rolls, face[2][a][None])[0] for a in range(7)]
        )
    sheets = []
    for a in range(7):
        rows = []
        for b in range(7):
            total = float(DERIV[b, 0]) * low[1][a] + float(DERIV[b, 6]) * high[1][a]
            if b == 0:
                total = total + across[0][a]
            if b == 6:
                total = total + across[1][a]
            rows.append(total * (weights * float(-1.0 / DELTA_T * WEIGHTS[a] * WEIGHTS[b])))
        sheets.append(jnp.stack(rows, axis=0))
    return sheets


def correct_kernel(
    part_ref, far_y_ref, near_y_ref, first_ref, last_ref, out_ref, far_ref, near_ref, class_out
):
    rolls = span_rolls()
    weights = span_vector(WEIGHTS)
    inverse = span_vector(1.0 / FACTOR)
    _, by, _ = iotas((8, LANES))
    received = [
        [lower_upper("dom", near_y_ref[k, a], far_y_ref[k, a]) for a in range(7)] for k in range(2)
    ]

    def chosen(place, values):
        return jnp.where(by == place, values, 0.0)

    each = [(i, range(7)) for i in range(3)]
    own = face_source(
        rolls, weights, inverse,
        [[chosen(0, lanes_from(received[1][a][0], i, 0)) for a in r] for i, r in each],
        [[chosen(BY - 1, lanes_from(received[1][a][1], i, LANES - BZ)) for a in r] for i, r in each],
    )
    other = face_source(
        rolls, weights, inverse,
        [[chosen(1, pltpu.roll(last_ref[i, a], 2 * BZ, 1)) for a in r] for i, r in each],
        [[chosen(0, first_ref[i, a]) for a in r] for i, r in each],
    )
    for a in range(7):
        mine = part_ref[0, a] + join_local(own[a])
        low, high = received[0][a]
        theirs = join_span(other[a]) + jnp.stack(
            [
                chosen(0, lanes_from(low, b, 0)) + chosen(1, lanes_from(high, b, BZ))
                for b in range(7)
            ],
            axis=0,
        )
        out_ref[0, a], out_ref[1, a] = mine, theirs
        out_ref[0, a, 0] = mine[0] + chosen(0, theirs[6])
        out_ref[0, a, 6] = mine[6] + chosen(BY - 1, pltpu.roll(theirs[0], LANES - 2 * BZ, 1))
        out_ref[1, a, 6] = theirs[6] + chosen(0, mine[0])
        out_ref[1, a, 0] = theirs[0] + chosen(1, pltpu.roll(mine[6], 2 * BZ, 1))
    for k in range(2):
        emit_faces(out_ref, far_ref, near_ref, k)
    low, high = received[0][0]
    class_out[...] = chosen(0, lanes_from(low, 7, 0)) + chosen(1, lanes_from(high, 7, BZ))


def gather_modes(full_ref, modes_ref):
    modes_ref[216:224] = jnp.zeros((8, LANES), F32)
    for compact, padded, rows in RUNS:
        modes_ref[compact : compact + rows] = full_ref[padded : padded + rows]


def terms(values):
    high = values.astype(BF16)
    rest = values - high.astype(F32)
    middle = rest.astype(BF16)
    return high, middle, (rest - middle.astype(F32)).astype(BF16)


HALF = 8


def split_kernel(half, schur_hbm, split_ref, schur_ref, left_ref, right_ref, sems):
    copies = [
        pltpu.make_async_copy(
            schur_hbm.at[pl.ds(109 * k, 109), pl.ds(HALF * half, HALF)],
            schur_ref.at[pl.ds(109 * k, 109)],
            sems.at[k],
        )
        for k in range(2)
    ]
    for copy in copies:
        copy.start()
    for k in range(2):
        split_ref[224 * k + 208 : 224 * k + 224] = jnp.zeros((16, 256 * HALF), BF16)
    right_ref[...] = jnp.zeros(right_ref.shape, F32)
    for copy in copies:
        copy.wait()
    left_ref[...] = schur_ref[:, :, :LANES].reshape(MODES * HALF, LANES)
    right_ref[:, : MODES - LANES] = schur_ref[:, :, LANES:].reshape(MODES * HALF, MODES - LANES)
    for c in range(HALF):
        for side, side_ref in enumerate((left_ref, right_ref)):
            block = side_ref[pl.ds(c, MODES, stride=HALF), :]
            place = LANES * (2 * c + side)
            for k, term in enumerate(terms(block)[:2]):
                split_ref[224 * k : 224 * k + MODES, place : place + LANES] = term


def split_half(schur, half):
    return call(
        functools.partial(split_kernel, half),
        [((448, 256 * HALF), BF16)],
        (schur,),
        [
            (MODES, HALF, MODES),
            *[(MODES * HALF, LANES)] * 2,
            pltpu.SemaphoreType.DMA((2,)),
        ],
        name="split",
        hbm=(0,),
    )[0]


def multiply_blocks(splits, class_ref, modes_ref, image_ref, right_ref, last_ref, ghost=None):
    high, middle, low = terms(modes_ref[...])
    pair = jnp.concatenate([high, middle], axis=1)
    mine = class_ref[0:1, :]
    both, last_both, rows = jnp.concatenate([mine, mine], axis=1), mine, 224
    if ghost is not None:
        modes, classes = (
            x + pltpu.roll(x, 32, 1) + pltpu.roll(x, 64, 1) for x in (ghost[0], ghost[1])
        )
        lane = lax.broadcasted_iota(jnp.int32, modes.shape, 1)
        three = [
            jnp.where((lane >= 32 * k) & (lane < 32 * k + 32), term.astype(F32), 0.0)
            for k, term in enumerate(terms(modes))
        ]
        low = jnp.concatenate([low, (three[0] + three[1] + three[2]).astype(BF16)], axis=1)
        last_both, rows = jnp.concatenate([mine, classes[0:1]], axis=1), 448
    zeros = jnp.zeros((32, 2 * LANES), BF16)
    for c in range(CLASSES):
        chosen, last_chosen = (
            jnp.where(jnp.abs(x - float(c)) < 0.5, 1.0, 0.0).astype(BF16) for x in (both, last_both)
        )
        right_ref[256 * c : 256 * c + 224] = pair * chosen
        right_ref[256 * c + 224 : 256 * c + 256] = zeros
        last_ref[256 * c : 256 * c + 224] = low * last_chosen
        last_ref[256 * c + 224 : 256 * c + 256] = zeros[:, : low.shape[1]]
    total, small = 0.0, 0.0
    for half, split_ref in enumerate(splits):
        part = pl.ds(256 * HALF * half, 256 * HALF)
        total = total + jnp.dot(split_ref[...], right_ref[part], preferred_element_type=F32)
        small = small + jnp.dot(split_ref[0:rows], last_ref[part], preferred_element_type=F32)
    total = total[:, :LANES] + total[:, LANES:]
    image_ref[...] = total[0:224] + (total[224:448] + small[0:224, :LANES])
    if ghost is None:
        return None
    extra = small[:, LANES:]
    extra = extra[0:224] + extra[224:448]
    return extra + (pltpu.roll(extra, LANES - 32, 1) + pltpu.roll(extra, LANES - 64, 1))


def scatter_modes(image_ref, full_ref, out_ref):
    full_ref[...] = jnp.zeros((392, LANES), F32)
    for compact, padded, rows in RUNS:
        full_ref[padded : padded + rows] = image_ref[compact : compact + rows]
    for a in range(7):
        out_ref[0, a] = join_local(full_ref[56 * a : 56 * a + 56].reshape(7, 8, LANES))


def total_of(values):
    return jnp.sum(jnp.sum(values, axis=0, keepdims=True), axis=1, keepdims=True)


def first_apply_kernel(
    part_ref, far_x_ref, near_x_ref, split_0, split_1, class_ref, ghost_class_ref,
    load_ref, image_ref, out_ref, far_ref, near_ref,
    full_ref, ghost_ref, ghost_modes_ref, side_ref, right_ref, last_ref,
):
    _, by, _ = iotas((8, LANES))
    for k, padded_ref in enumerate((full_ref, ghost_ref)):
        for a in range(7):
            sheet = add_streamwise(a, part_ref[k, a], far_x_ref[k], near_x_ref[k])
            padded_ref[56 * a : 56 * a + 56] = sheet.reshape(56, LANES)
    gather_modes(full_ref, load_ref)
    gather_modes(ghost_ref, ghost_modes_ref)
    ghost_image = multiply_blocks(
        (split_0, split_1), class_ref, load_ref, image_ref, right_ref, last_ref,
        (ghost_modes_ref[...], ghost_class_ref[...]),
    )
    scatter_modes(image_ref, full_ref, out_ref)
    ghost_modes_ref[...] = ghost_image
    side_ref[...] = jnp.zeros(side_ref.shape, F32)
    for k, b in enumerate((6, 0)):
        for a in range(7):
            row = FACE_ROWS[7 * a + b]
            side_ref[k, a, 0:7] = ghost_modes_ref[row : row + 7]
    below, above = join_span(side_ref[0]), join_span(side_ref[1])
    for a in range(7):
        out_ref[0, a, 0] += jnp.where(by == 0, below[a], 0.0)
        out_ref[0, a, 6] += jnp.where(by == BY - 1, pltpu.roll(above[a], LANES - 2 * BZ, 1), 0.0)
    emit_faces(out_ref, far_ref, near_ref, 0)


def second_apply_kernel(
    part_ref, far_x_ref, near_x_ref, split_0, split_1, class_ref, load_ref, first_ref, shell_ref,
    power_ref, send_ref, out_ref, far_ref, near_ref, image_ref, full_ref, right_ref, last_ref,
):
    for a in range(7):
        sheet = add_streamwise(a, part_ref[0, a], far_x_ref[0], near_x_ref[0])
        full_ref[56 * a : 56 * a + 56] = sheet.reshape(56, LANES)
    gather_modes(full_ref, power_ref)
    multiply_blocks((split_0, split_1), class_ref, power_ref, image_ref, right_ref, last_ref)
    scatter_modes(image_ref, full_ref, out_ref)
    emit_faces(out_ref, far_ref, near_ref, 0)
    load, power, shell = load_ref[...], power_ref[...], shell_ref[...]
    first, image = first_ref[...], image_ref[...]
    lane = lax.broadcasted_iota(jnp.int32, (1, LANES), 1)
    dots = jnp.zeros((1, LANES), F32)
    values = (
        load * load * shell, load * first, power * power * shell, load * image, power * image
    )
    for k, value in enumerate(values):
        dots = dots + jnp.where(lane == k, total_of(value), 0.0)
    node = lax.broadcasted_iota(jnp.int32, (8, LANES), 0)
    count = send_ref.shape[0] // 2
    mine = lax.axis_index("dom")
    alone = jnp.where(node == 7, dots, 0.0)
    send_ref[...] = jnp.broadcast_to(alone[None], send_ref.shape)
    up = pack_groups([out_ref[0, a, 6] for a in range(7)], LANES - BZ)
    down = pack_groups([out_ref[0, a, 0] for a in range(7)], 0)
    for half in range(2):
        send_ref[half * count + lax.rem(mine + 1, count)] = jnp.where(node == 7, dots, up)
        send_ref[half * count + lax.rem(mine + count - 1, count)] = jnp.where(node == 7, dots, down)


def middle_kernel(got_ref, low_ref, high_ref, send_ref):
    node = lax.broadcasted_iota(jnp.int32, (8, LANES), 0)
    _, by, _ = iotas((8, LANES))
    count, run = got_ref.shape[0] // 2, send_ref.shape[0]
    mine = lax.axis_index("dom")
    slab = lax.axis_index("slab")
    half, place = slab // run, lax.rem(slab, run)

    def faces(which):
        return tuple(
            jnp.where(node < 7, got_ref[which * count + lax.rem(mine + step, count)], 0.0)
            for step in (count - 1, 1)
        )

    low, high = faces(half)
    for a in range(7):
        low_ref[a], high_ref[a] = lanes_from(low, a, 0), lanes_from(high, a, LANES - BZ)
    total = jnp.sum(got_ref[...], axis=0)[7:8]
    send_ref[...] = jnp.broadcast_to(jnp.where(node == 7, total, 0.0)[None], send_ref.shape)
    for a, step, end in ((6, 1, run - 1), (0, run - 1, 0)):
        low, high = faces(jnp.where(place == end, 1 - half, half))
        low, high = lanes_from(low, a, 0), lanes_from(high, a, LANES - BZ)
        edges = jnp.where(by == 0, low, jnp.where(by == BY - 1, high, 0.0))
        send_ref[lax.rem(place + step, run)] = jnp.where(node == 7, total, edges)


def finish_kernel(
    part_ref, far_x_ref, near_x_ref, low_ref, high_ref, load_ref, power_ref, dots_ref, slot_ref,
    pressure_ref, residual_ref, full_ref, modes_ref,
):
    node = lax.broadcasted_iota(jnp.int32, (8, LANES), 0)
    run = dots_ref.shape[0]
    place = lax.rem(lax.axis_index("slab"), run)
    for a in range(7):
        sheet = add_streamwise(a, part_ref[0, a], far_x_ref[0], near_x_ref[0])
        sheet = add_second(sheet, low_ref[a], high_ref[a])
        if a in (0, 6):
            edges = dots_ref[lax.rem(place + (run - 1 if a == 0 else 1), run)]
            edges = jnp.where(node < 7, edges, 0.0)
            sheet = add_second(sheet, edges, edges)
        full_ref[56 * a : 56 * a + 56] = sheet.reshape(56, LANES)
    gather_modes(full_ref, modes_ref)
    dots = jnp.sum(dots_ref[...], axis=0)[7:8]
    square, energy, power_square, cross, power_energy = (dots[:, k : k + 1] for k in range(5))
    step = square / energy
    fresh = square - 2.0 * step * energy + step * step * power_square
    ratio = fresh / square
    grow = 1.0 + ratio
    curvature = (
        grow * grow * energy
        - step * grow * (cross + power_square)
        + step * step * power_energy
    )
    second = fresh / curvature
    load, power, twice = load_ref[...], power_ref[...], modes_ref[...]
    pressure = step * load + second * (grow * load - step * power)
    residual = load - step * power - second * (grow * power - step * twice)
    one_hot = permutation(slot_ref)
    pressure_ref[...] = moved(pressure, one_hot, TO_STORED)[:MODES]
    residual_ref[...] = moved(residual, one_hot, TO_STORED)[:MODES]


def call(kernel, outs, args, scratch=(), name=None, hbm=()):
    vmem = pl.BlockSpec(memory_space=pltpu.VMEM)
    places = [pl.BlockSpec(memory_space=pltpu.HBM) if k in hbm else vmem for k in range(len(args))]
    args = [
        pltpu.with_memory_space_constraint(x, pltpu.HBM) if k in hbm else x
        for k, x in enumerate(args)
    ]
    return pl.pallas_call(
        kernel,
        out_shape=tuple(
            jax.ShapeDtypeStruct(*(o if isinstance(o[0], tuple) else (o, F32))) for o in outs
        ),
        in_specs=places,
        out_specs=tuple([vmem] * len(outs)),
        scratch_shapes=[pltpu.VMEM(s, F32) if isinstance(s, tuple) else s for s in scratch],
        compiler_params=pltpu.CompilerParams(vmem_limit_bytes=24 << 20),
        name=name,
    )(*args)


def partners(axis):
    count = lax.axis_size(axis)
    far = [(i, (i + 1) % count if i % 2 else (i - 1) % count) for i in range(count)]
    near = [(i, i ^ 1) for i in range(count)]
    return far, near


def swap(axis, far, near):
    far_pairs, near_pairs = partners(axis)
    return lax.ppermute(far, axis, far_pairs), lax.ppermute(near, axis, near_pairs)


def per_device(velocity, slot_map, class_index, schur_blocks):
    slots = slot_map.reshape(1, LANES)
    shell = jnp.asarray(SHELL)
    schur = schur_blocks.transpose(1, 0, 2)
    face = (7, 8, LANES)
    whole = (7, 7, 8, LANES)
    modes = (224, LANES)
    rights = [pltpu.VMEM((256 * CLASSES, n), BF16) for n in (2 * LANES, LANES)]
    brick, part, far, near, classes = call(
        advect_kernel,
        [(3, *whole), (3, *whole), (3, *face), (3, *face), (8, LANES)],
        (velocity, slots, class_index.reshape(1, LANES)),
        [
            (3, NODES, LANES),
            pltpu.VMEM((1, LANES), jnp.int32),
            pltpu.VMEM((1, LANES), jnp.int32),
            pltpu.SemaphoreType.DMA((5,)),
        ],
        name="advect",
        hbm=(0, 1, 2),
    )
    swapped = swap("slab", far, near)
    part, split_0 = lax.optimization_barrier((part, split_half(schur, 0)))
    part, far, near, first_side, last_side = call(
        source_kernel,
        [(1, *whole), (2, *face), (2, *face), (3, *face), (3, *face)],
        (part, *swapped, brick, classes),
        [(3, *whole)],
        name="source",
    )
    part, far, near, ghost_classes = call(
        correct_kernel,
        [(2, *whole), (2, *face), (2, *face), (8, LANES)],
        (part, *swap("dom", far, near), first_side, last_side),
        name="correct",
    )
    swapped = swap("slab", far, near)
    part, split_1 = lax.optimization_barrier((part, split_half(schur, 1)))
    load, first, part, far, near = call(
        first_apply_kernel,
        [modes, modes, (1, *whole), (1, *face), (1, *face)],
        (part, *swapped, split_0, split_1, classes, ghost_classes),
        [(392, LANES), (392, LANES), modes, (2, *face), rights[0], rights[0]],
        name="first",
    )
    run, doms = lax.axis_size("slab") // 2, lax.axis_size("dom")
    rings = [[doms * run * half + doms * k + d for k in range(run)] for half in range(2) for d in range(doms)]
    sheets = [
        [doms * (run * half + k) + d for half in range(2) for d in range(doms)] for k in range(run)
    ]
    power, send, part, far, near = call(
        second_apply_kernel,
        [modes, (2 * doms, 8, LANES), (1, *whole), (1, *face), (1, *face)],
        (part, *swap("slab", far, near), split_0, split_1, classes, load, first, shell),
        [modes, (392, LANES), *rights],
        name="second",
    )
    got = lax.all_to_all(send, ("slab", "dom"), 0, 0, axis_index_groups=sheets)
    far_x, near_x = swap("slab", far, near)
    got, far_x = lax.optimization_barrier((got, far_x))
    low, high, send = call(
        middle_kernel, [face, face, (run, 8, LANES)], (got,), name="middle"
    )
    dots = lax.all_to_all(send, ("slab", "dom"), 0, 0, axis_index_groups=rings)
    return call(
        finish_kernel,
        [(MODES, LANES), (MODES, LANES)],
        (part, far_x, near_x, low, high, load, power, dots, slots),
        [(392, LANES), modes],
        name="finish",
    )


def solution(mesh):
    return jax.shard_map(
        per_device,
        mesh=mesh,
        in_specs=(
            P(None, None, ("slab", "dom")),
            P("slab", "dom", None),
            P("slab", "dom", None),
            P(),
        ),
        out_specs=(P(None, ("slab", "dom")), P(None, ("slab", "dom"))),
        check_vma=False,
    )
```

```python
import functools

import jax
import jax.numpy as jnp
import numpy as np
from jax import lax
from jax.experimental import pallas as pl
from jax.experimental.pallas import tpu as pltpu
from jax.sharding import PartitionSpec as P

CLASSES = 16
MODES = 218
NODES = 343
LANES = 128
BZ = 16
BY = 8
DELTA_T = 0.05
F32 = jnp.float32
BF16 = jnp.bfloat16


def gll_tables():
    degree = 6
    outer_point = 0.830223896278567
    inner_point = 0.46884879347071423
    points = np.array([-1.0, -outer_point, -inner_point, 0.0, inner_point, outer_point, 1.0])
    values = (231.0 * points**6 - 315.0 * points**4 + 105.0 * points**2 - 5.0) / 16.0
    weights = 2.0 / (degree * (degree + 1) * values**2)
    derivative = np.zeros((7, 7))
    for target in range(7):
        for source in range(7):
            if target != source:
                derivative[target, source] = values[target] / (
                    values[source] * (points[target] - points[source])
                )
    derivative[0, 0] = -degree * (degree + 1) / 4.0
    derivative[6, 6] = degree * (degree + 1) / 4.0
    return derivative, weights


DERIV, WEIGHTS = gll_tables()
FACTOR = np.where((np.arange(7) == 0) | (np.arange(7) == 6), 2.0, 1.0)


def shell_runs():
    runs, offset = [], 0
    for a in range(7):
        for b in range(7):
            base = 8 * (7 * a + b)
            if a in (0, 6) or b in (0, 6):
                runs.append((offset, base, 7))
                offset += 7
            else:
                runs.append((offset, base, 1))
                runs.append((offset + 1, base + 6, 1))
                offset += 2
    return runs


RUNS = shell_runs()
FACE_ROWS = {padded // 8: compact for compact, padded, rows in RUNS if rows == 7}


def shell_table():
    multiple = (FACTOR[:, None, None] * FACTOR[None, :, None] * FACTOR[None, None, :]).reshape(-1)
    surface = [
        i for i in range(NODES) if i // 49 in (0, 6) or i // 7 % 7 in (0, 6) or i % 7 in (0, 6)
    ]
    shell = np.zeros((224, LANES))
    shell[:MODES] = (1.0 / multiple[surface])[:, None]
    return shell.astype(np.float32)


SHELL = shell_table()


def span_vector(values):
    node = lax.broadcasted_iota(jnp.int32, (8, LANES), 0)
    table = jnp.zeros((8, LANES), F32)
    for c in range(7):
        table = jnp.where(node == c, float(values[c]), table)
    return table


def span_rolls():
    tables = []
    for shift in range(8):
        sources = [(target - shift) % 8 for target in range(7)]
        tables.append(
            span_vector([DERIV[t, c] if c < 7 else 0.0 for t, c in zip(range(7), sources)])
        )
    return tables


def even_place(axis, like):
    return jnp.full(like.shape, lax.axis_index(axis) % 2, jnp.int32) == 0


def lower_upper(axis, near, far):
    even = even_place(axis, near)
    return jnp.where(even, far, near), jnp.where(even, near, far)


def iotas(shape):
    lane = lax.broadcasted_iota(jnp.int32, shape, len(shape) - 1)
    node = lax.broadcasted_iota(jnp.int32, shape, len(shape) - 2)
    return lane % BZ, lane // BZ, node


def join_span(sheet):
    bz, _, node = iotas(sheet.shape)
    low = pltpu.roll(sheet, 2, 1)
    low = jnp.where(bz == 0, pltpu.roll(low, LANES - 15, 2), pltpu.roll(low, 1, 2))
    high = pltpu.roll(sheet, 6, 1)
    high = jnp.where(bz == BZ - 1, pltpu.roll(high, 15, 2), pltpu.roll(high, LANES - 1, 2))
    return sheet + jnp.where(node == 0, low, jnp.where(node == 6, high, 0.0))


def join_local(sheet):
    sheet = join_span(sheet)
    _, by, _ = iotas(sheet.shape[1:])
    first, last = sheet[0], sheet[6]
    new_first = first + jnp.where(by > 0, pltpu.roll(last, BZ, 1), 0.0)
    new_last = last + jnp.where(by < BY - 1, pltpu.roll(first, LANES - BZ, 1), 0.0)
    return jnp.concatenate([new_first[None], sheet[1:6], new_last[None]], axis=0)


def add_streamwise(a, sheet, far_x, near_x):
    if a == 0:
        sheet = sheet + lower_upper("slab", near_x, far_x)[0]
    if a == 6:
        sheet = sheet + lower_upper("slab", near_x, far_x)[1]
    return sheet


def add_second(sheet, low_y, high_y):
    _, by, _ = iotas(sheet.shape[1:])
    first = sheet[0] + jnp.where(by == 0, low_y, 0.0)
    last = sheet[6] + jnp.where(by == BY - 1, high_y, 0.0)
    return jnp.concatenate([first[None], sheet[1:6], last[None]], axis=0)


def pack_groups(blocks, start):
    _, group, _ = iotas(blocks[0].shape)
    total = jnp.zeros(blocks[0].shape, F32)
    for k, block in enumerate(blocks):
        shift = (BZ * k - start) % LANES
        total = jnp.where(group == k, pltpu.roll(block, shift, 1) if shift else block, total)
    return total


def lanes_from(packed, group, start):
    shift = (start - BZ * group) % LANES
    return pltpu.roll(packed, shift, 1) if shift else packed


def derive_sheets(sheets, target):
    total = float(DERIV[target, 0]) * sheets[0]
    for source in range(1, 7):
        total = total + float(DERIV[target, source]) * sheets[source]
    return total


def derive_span(rolls, sheet):
    total = rolls[0] * sheet
    for shift in range(1, 8):
        total = total + rolls[shift] * pltpu.roll(sheet, shift, 1)
    return total


def permutation(slot_ref):
    position = lax.broadcasted_iota(jnp.int32, (LANES, LANES), 0)
    return jnp.where(position == slot_ref[...], 1.0, 0.0).astype(BF16)


def moved(values, one_hot, dims):
    return sum(
        lax.dot_general(term, one_hot, (dims, ((), ())), preferred_element_type=F32)
        for term in terms(values)
    )


TO_BRICK = ((1,), (1,))
TO_STORED = ((1,), (0,))


def emit_faces(part_ref, far_ref, near_ref, index):
    low, high = part_ref[index, 0], part_ref[index, 6]
    even = even_place("slab", low)
    far_ref[index] = jnp.where(even, low, high)
    near_ref[index] = jnp.where(even, high, low)


def advect_kernel(
    vel_hbm, slot_hbm, class_hbm,
    brick_ref, part_ref, far_ref, near_ref, class_out,
    vel_ref, slot_ref, class_ref, sems,
):
    copies = [
        pltpu.make_async_copy(src, dst, sems.at[k])
        for k, (src, dst) in enumerate(
            (
                (slot_hbm, slot_ref), (class_hbm, class_ref),
                *((vel_hbm.at[i], vel_ref.at[i]) for i in range(3)),
            )
        )
    ]
    for copy in copies:
        copy.start()
    rolls = span_rolls()
    brick_ref[:, :, :, 7:8, :] = jnp.zeros((3, 7, 7, 1, LANES), F32)
    copies[0].wait()
    copies[1].wait()
    one_hot = permutation(slot_ref)
    class_out[...] = moved(
        jnp.broadcast_to(class_ref[...].astype(F32), (8, LANES)), one_hot, TO_BRICK
    )
    for i in range(3):
        copies[2 + i].wait()
        stored = moved(vel_ref[i], one_hot, TO_BRICK)
        for a in range(7):
            for b in range(7):
                row = 7 * (7 * a + b)
                brick_ref[i, a, b, 0:7, :] = stored[row : row + 7]

    def component(i, carry):
        sheets = [brick_ref[i, a] for a in range(7)]
        for a in range(7):
            along_a = derive_sheets(sheets, a)
            sheet = sheets[a]
            along_b = jnp.stack(
                [derive_sheets([sheet[b] for b in range(7)], target) for target in range(7)], axis=0
            )
            along_c = derive_span(rolls, sheet)
            advect = (
                brick_ref[0, a] * along_a + brick_ref[1, a] * along_b + brick_ref[2, a] * along_c
            )
            part_ref[i, a] = join_local(advect)
        emit_faces(part_ref, far_ref, near_ref, i)
        return carry

    lax.fori_loop(0, 3, component, 0)


def source_kernel(
    part_ref, far_x_ref, near_x_ref, brick_ref, class_ref,
    out_ref, far_ref, near_ref, first_ref, last_ref, middle_ref,
):
    rolls = span_rolls()
    weights = span_vector(WEIGHTS)
    inverse = span_vector(1.0 / FACTOR)
    for i in range(3):
        for a in range(7):
            sheet = add_streamwise(a, part_ref[i, a], far_x_ref[i], near_x_ref[i])
            first_ref[i, a], last_ref[i, a] = sheet[0], sheet[6]
            scaled = [
                sheet[b] * (inverse * float(DELTA_T / (FACTOR[a] * FACTOR[b]))) for b in range(7)
            ]
            middle_ref[i, a] = brick_ref[i, a] - jnp.stack(scaled, axis=0)
    sheets = [middle_ref[0, a] for a in range(7)]
    for a in range(7):
        along_a = derive_sheets(sheets, a)
        second = middle_ref[1, a]
        along_b = jnp.stack(
            [derive_sheets([second[b] for b in range(7)], target) for target in range(7)], axis=0
        )
        diverge = along_a + along_b + derive_span(rolls, middle_ref[2, a])
        source = [
            diverge[b] * (weights * float(-1.0 / DELTA_T * WEIGHTS[a] * WEIGHTS[b]))
            for b in range(7)
        ]
        out_ref[0, a] = join_local(jnp.stack(source, axis=0))
    classes = class_ref[...]
    even = even_place("dom", classes)
    for a in range(7):
        rows = [*(out_ref[0, a, b] for b in range(7)), classes]
        pairs = (
            (pack_groups(rows, 0), pack_groups(rows, LANES - BZ)),
            (
                pack_groups([first_ref[i, a] for i in range(3)], 0),
                pack_groups([last_ref[i, a] for i in range(3)], LANES - BZ),
            ),
        )
        for k, (down, up) in enumerate(pairs):
            far_ref[k, a] = jnp.where(even, down, up)
            near_ref[k, a] = jnp.where(even, up, down)


def face_source(rolls, weights, inverse, low, high):
    across = []
    for face in (low, high):
        for i in range(3):
            for a in range(7):
                face[i][a] = face[i][a] * (inverse * float(-DELTA_T / (2.0 * FACTOR[a])))
        across.append(
            [derive_sheets(face[0], a) + derive_span(rolls, face[2][a][None])[0] for a in range(7)]
        )
    sheets = []
    for a in range(7):
        rows = []
        for b in range(7):
            total = float(DERIV[b, 0]) * low[1][a] + float(DERIV[b, 6]) * high[1][a]
            if b == 0:
                total = total + across[0][a]
            if b == 6:
                total = total + across[1][a]
            rows.append(total * (weights * float(-1.0 / DELTA_T * WEIGHTS[a] * WEIGHTS[b])))
        sheets.append(jnp.stack(rows, axis=0))
    return sheets


def correct_kernel(
    part_ref, far_y_ref, near_y_ref, first_ref, last_ref, out_ref, far_ref, near_ref, class_out
):
    rolls = span_rolls()
    weights = span_vector(WEIGHTS)
    inverse = span_vector(1.0 / FACTOR)
    _, by, _ = iotas((8, LANES))
    received = [
        [lower_upper("dom", near_y_ref[k, a], far_y_ref[k, a]) for a in range(7)] for k in range(2)
    ]

    def chosen(place, values):
        return jnp.where(by == place, values, 0.0)

    each = [(i, range(7)) for i in range(3)]
    own = face_source(
        rolls, weights, inverse,
        [[chosen(0, lanes_from(received[1][a][0], i, 0)) for a in r] for i, r in each],
        [[chosen(BY - 1, lanes_from(received[1][a][1], i, LANES - BZ)) for a in r] for i, r in each],
    )
    other = face_source(
        rolls, weights, inverse,
        [[chosen(1, pltpu.roll(last_ref[i, a], 2 * BZ, 1)) for a in r] for i, r in each],
        [[chosen(0, first_ref[i, a]) for a in r] for i, r in each],
    )
    for a in range(7):
        mine = part_ref[0, a] + join_local(own[a])
        low, high = received[0][a]
        theirs = join_span(other[a]) + jnp.stack(
            [
                chosen(0, lanes_from(low, b, 0)) + chosen(1, lanes_from(high, b, BZ))
                for b in range(7)
            ],
            axis=0,
        )
        out_ref[0, a], out_ref[1, a] = mine, theirs
        out_ref[0, a, 0] = mine[0] + chosen(0, theirs[6])
        out_ref[0, a, 6] = mine[6] + chosen(BY - 1, pltpu.roll(theirs[0], LANES - 2 * BZ, 1))
        out_ref[1, a, 6] = theirs[6] + chosen(0, mine[0])
        out_ref[1, a, 0] = theirs[0] + chosen(1, pltpu.roll(mine[6], 2 * BZ, 1))
    for k in range(2):
        emit_faces(out_ref, far_ref, near_ref, k)
    low, high = received[0][0]
    class_out[...] = chosen(0, lanes_from(low, 7, 0)) + chosen(1, lanes_from(high, 7, BZ))


def gather_modes(full_ref, modes_ref):
    modes_ref[216:224] = jnp.zeros((8, LANES), F32)
    for compact, padded, rows in RUNS:
        modes_ref[compact : compact + rows] = full_ref[padded : padded + rows]


def terms(values):
    high = values.astype(BF16)
    rest = values - high.astype(F32)
    middle = rest.astype(BF16)
    return high, middle, (rest - middle.astype(F32)).astype(BF16)


HALF = 8


def split_kernel(half, schur_hbm, split_ref, schur_ref, left_ref, right_ref, sems):
    copies = [
        pltpu.make_async_copy(
            schur_hbm.at[pl.ds(109 * k, 109), pl.ds(HALF * half, HALF)],
            schur_ref.at[pl.ds(109 * k, 109)],
            sems.at[k],
        )
        for k in range(2)
    ]
    for copy in copies:
        copy.start()
    for k in range(2):
        split_ref[224 * k + 208 : 224 * k + 224] = jnp.zeros((16, 256 * HALF), BF16)
    right_ref[...] = jnp.zeros(right_ref.shape, F32)
    for copy in copies:
        copy.wait()
    left_ref[...] = schur_ref[:, :, :LANES].reshape(MODES * HALF, LANES)
    right_ref[:, : MODES - LANES] = schur_ref[:, :, LANES:].reshape(MODES * HALF, MODES - LANES)
    for c in range(HALF):
        for side, side_ref in enumerate((left_ref, right_ref)):
            block = side_ref[pl.ds(c, MODES, stride=HALF), :]
            place = LANES * (2 * c + side)
            for k, term in enumerate(terms(block)[:2]):
                split_ref[224 * k : 224 * k + MODES, place : place + LANES] = term


def split_half(schur, half):
    return call(
        functools.partial(split_kernel, half),
        [((448, 256 * HALF), BF16)],
        (schur,),
        [
            (MODES, HALF, MODES),
            *[(MODES * HALF, LANES)] * 2,
            pltpu.SemaphoreType.DMA((2,)),
        ],
        name="split",
        hbm=(0,),
    )[0]


def multiply_blocks(splits, class_ref, modes_ref, image_ref, right_ref, last_ref, ghost=None):
    high, middle, low = terms(modes_ref[...])
    pair = jnp.concatenate([high, middle], axis=1)
    mine = class_ref[0:1, :]
    both, last_both, rows = jnp.concatenate([mine, mine], axis=1), mine, 224
    if ghost is not None:
        modes, classes = (
            x + pltpu.roll(x, 32, 1) + pltpu.roll(x, 64, 1) for x in (ghost[0], ghost[1])
        )
        lane = lax.broadcasted_iota(jnp.int32, modes.shape, 1)
        three = [
            jnp.where((lane >= 32 * k) & (lane < 32 * k + 32), term.astype(F32), 0.0)
            for k, term in enumerate(terms(modes))
        ]
        low = jnp.concatenate([low, (three[0] + three[1] + three[2]).astype(BF16)], axis=1)
        last_both, rows = jnp.concatenate([mine, classes[0:1]], axis=1), 448
    zeros = jnp.zeros((32, 2 * LANES), BF16)
    for c in range(CLASSES):
        chosen, last_chosen = (
            jnp.where(jnp.abs(x - float(c)) < 0.5, 1.0, 0.0).astype(BF16) for x in (both, last_both)
        )
        right_ref[256 * c : 256 * c + 224] = pair * chosen
        right_ref[256 * c + 224 : 256 * c + 256] = zeros
        last_ref[256 * c : 256 * c + 224] = low * last_chosen
        last_ref[256 * c + 224 : 256 * c + 256] = zeros[:, : low.shape[1]]
    total, small = 0.0, 0.0
    for half, split_ref in enumerate(splits):
        part = pl.ds(256 * HALF * half, 256 * HALF)
        total = total + jnp.dot(split_ref[...], right_ref[part], preferred_element_type=F32)
        small = small + jnp.dot(split_ref[0:rows], last_ref[part], preferred_element_type=F32)
    total = total[:, :LANES] + total[:, LANES:]
    image_ref[...] = total[0:224] + (total[224:448] + small[0:224, :LANES])
    if ghost is None:
        return None
    extra = small[:, LANES:]
    extra = extra[0:224] + extra[224:448]
    return extra + (pltpu.roll(extra, LANES - 32, 1) + pltpu.roll(extra, LANES - 64, 1))


def scatter_modes(image_ref, full_ref, out_ref):
    full_ref[...] = jnp.zeros((392, LANES), F32)
    for compact, padded, rows in RUNS:
        full_ref[padded : padded + rows] = image_ref[compact : compact + rows]
    for a in range(7):
        out_ref[0, a] = join_local(full_ref[56 * a : 56 * a + 56].reshape(7, 8, LANES))


def total_of(values):
    return jnp.sum(jnp.sum(values, axis=0, keepdims=True), axis=1, keepdims=True)


def first_apply_kernel(
    part_ref, far_x_ref, near_x_ref, split_0, split_1, class_ref, ghost_class_ref,
    load_ref, image_ref, out_ref, far_ref, near_ref,
    full_ref, ghost_ref, ghost_modes_ref, side_ref, right_ref, last_ref,
):
    _, by, _ = iotas((8, LANES))
    for k, padded_ref in enumerate((full_ref, ghost_ref)):
        for a in range(7):
            sheet = add_streamwise(a, part_ref[k, a], far_x_ref[k], near_x_ref[k])
            padded_ref[56 * a : 56 * a + 56] = sheet.reshape(56, LANES)
    gather_modes(full_ref, load_ref)
    gather_modes(ghost_ref, ghost_modes_ref)
    ghost_image = multiply_blocks(
        (split_0, split_1), class_ref, load_ref, image_ref, right_ref, last_ref,
        (ghost_modes_ref[...], ghost_class_ref[...]),
    )
    scatter_modes(image_ref, full_ref, out_ref)
    ghost_modes_ref[...] = ghost_image
    side_ref[...] = jnp.zeros(side_ref.shape, F32)
    for k, b in enumerate((6, 0)):
        for a in range(7):
            row = FACE_ROWS[7 * a + b]
            side_ref[k, a, 0:7] = ghost_modes_ref[row : row + 7]
    below, above = join_span(side_ref[0]), join_span(side_ref[1])
    for a in range(7):
        out_ref[0, a, 0] += jnp.where(by == 0, below[a], 0.0)
        out_ref[0, a, 6] += jnp.where(by == BY - 1, pltpu.roll(above[a], LANES - 2 * BZ, 1), 0.0)
    emit_faces(out_ref, far_ref, near_ref, 0)


def second_apply_kernel(
    part_ref, far_x_ref, near_x_ref, split_0, split_1, class_ref, load_ref, first_ref, shell_ref,
    power_ref, send_ref, out_ref, far_ref, near_ref, image_ref, full_ref, right_ref, last_ref,
):
    for a in range(7):
        sheet = add_streamwise(a, part_ref[0, a], far_x_ref[0], near_x_ref[0])
        full_ref[56 * a : 56 * a + 56] = sheet.reshape(56, LANES)
    gather_modes(full_ref, power_ref)
    multiply_blocks((split_0, split_1), class_ref, power_ref, image_ref, right_ref, last_ref)
    scatter_modes(image_ref, full_ref, out_ref)
    emit_faces(out_ref, far_ref, near_ref, 0)
    load, power, shell = load_ref[...], power_ref[...], shell_ref[...]
    first, image = first_ref[...], image_ref[...]
    lane = lax.broadcasted_iota(jnp.int32, (1, LANES), 1)
    dots = jnp.zeros((1, LANES), F32)
    values = (
        load * load * shell, load * first, power * power * shell, load * image, power * image
    )
    for k, value in enumerate(values):
        dots = dots + jnp.where(lane == k, total_of(value), 0.0)
    node = lax.broadcasted_iota(jnp.int32, (8, LANES), 0)
    count = send_ref.shape[0] // 2
    mine = lax.axis_index("dom")
    alone = jnp.where(node == 7, dots, 0.0)
    send_ref[...] = jnp.broadcast_to(alone[None], send_ref.shape)
    up = pack_groups([out_ref[0, a, 6] for a in range(7)], LANES - BZ)
    down = pack_groups([out_ref[0, a, 0] for a in range(7)], 0)
    for half in range(2):
        send_ref[half * count + lax.rem(mine + 1, count)] = jnp.where(node == 7, dots, up)
        send_ref[half * count + lax.rem(mine + count - 1, count)] = jnp.where(node == 7, dots, down)


def middle_kernel(got_ref, low_ref, high_ref, send_ref):
    node = lax.broadcasted_iota(jnp.int32, (8, LANES), 0)
    _, by, _ = iotas((8, LANES))
    count, run = got_ref.shape[0] // 2, send_ref.shape[0]
    mine = lax.axis_index("dom")
    slab = lax.axis_index("slab")
    half, place = slab // run, lax.rem(slab, run)

    def faces(which):
        return tuple(
            jnp.where(node < 7, got_ref[which * count + lax.rem(mine + step, count)], 0.0)
            for step in (count - 1, 1)
        )

    low, high = faces(half)
    for a in range(7):
        low_ref[a], high_ref[a] = lanes_from(low, a, 0), lanes_from(high, a, LANES - BZ)
    total = jnp.sum(got_ref[...], axis=0)[7:8]
    send_ref[...] = jnp.broadcast_to(jnp.where(node == 7, total, 0.0)[None], send_ref.shape)
    for a, step, end in ((6, 1, run - 1), (0, run - 1, 0)):
        low, high = faces(jnp.where(place == end, 1 - half, half))
        low, high = lanes_from(low, a, 0), lanes_from(high, a, LANES - BZ)
        edges = jnp.where(by == 0, low, jnp.where(by == BY - 1, high, 0.0))
        send_ref[lax.rem(place + step, run)] = jnp.where(node == 7, total, edges)


def finish_kernel(
    part_ref, far_x_ref, near_x_ref, low_ref, high_ref, load_ref, power_ref, dots_ref, slot_ref,
    pressure_ref, residual_ref, full_ref, modes_ref,
):
    node = lax.broadcasted_iota(jnp.int32, (8, LANES), 0)
    run = dots_ref.shape[0]
    place = lax.rem(lax.axis_index("slab"), run)
    for a in range(7):
        sheet = add_streamwise(a, part_ref[0, a], far_x_ref[0], near_x_ref[0])
        sheet = add_second(sheet, low_ref[a], high_ref[a])
        if a in (0, 6):
            edges = dots_ref[lax.rem(place + (run - 1 if a == 0 else 1), run)]
            edges = jnp.where(node < 7, edges, 0.0)
            sheet = add_second(sheet, edges, edges)
        full_ref[56 * a : 56 * a + 56] = sheet.reshape(56, LANES)
    gather_modes(full_ref, modes_ref)
    dots = jnp.sum(dots_ref[...], axis=0)[7:8]
    square, energy, power_square, cross, power_energy = (dots[:, k : k + 1] for k in range(5))
    step = square / energy
    fresh = square - 2.0 * step * energy + step * step * power_square
    ratio = fresh / square
    grow = 1.0 + ratio
    curvature = (
        grow * grow * energy
        - step * grow * (cross + power_square)
        + step * step * power_energy
    )
    second = fresh / curvature
    load, power, twice = load_ref[...], power_ref[...], modes_ref[...]
    pressure = step * load + second * (grow * load - step * power)
    residual = load - step * power - second * (grow * power - step * twice)
    one_hot = permutation(slot_ref)
    pressure_ref[...] = moved(pressure, one_hot, TO_STORED)[:MODES]
    residual_ref[...] = moved(residual, one_hot, TO_STORED)[:MODES]


def call(kernel, outs, args, scratch=(), name=None, hbm=()):
    vmem = pl.BlockSpec(memory_space=pltpu.VMEM)
    places = [pl.BlockSpec(memory_space=pltpu.HBM) if k in hbm else vmem for k in range(len(args))]
    args = [
        pltpu.with_memory_space_constraint(x, pltpu.HBM) if k in hbm else x
        for k, x in enumerate(args)
    ]
    return pl.pallas_call(
        kernel,
        out_shape=tuple(
            jax.ShapeDtypeStruct(*(o if isinstance(o[0], tuple) else (o, F32))) for o in outs
        ),
        in_specs=places,
        out_specs=tuple([vmem] * len(outs)),
        scratch_shapes=[pltpu.VMEM(s, F32) if isinstance(s, tuple) else s for s in scratch],
        compiler_params=pltpu.CompilerParams(vmem_limit_bytes=24 << 20),
        name=name,
    )(*args)


def partners(axis):
    count = lax.axis_size(axis)
    far = [(i, (i + 1) % count if i % 2 else (i - 1) % count) for i in range(count)]
    near = [(i, i ^ 1) for i in range(count)]
    return far, near


def swap(axis, far, near):
    far_pairs, near_pairs = partners(axis)
    return lax.ppermute(far, axis, far_pairs), lax.ppermute(near, axis, near_pairs)


def per_device(velocity, slot_map, class_index, schur_blocks):
    slots = slot_map.reshape(1, LANES)
    shell = jnp.asarray(SHELL)
    schur = schur_blocks.transpose(1, 0, 2)
    face = (7, 8, LANES)
    whole = (7, 7, 8, LANES)
    modes = (224, LANES)
    rights = [pltpu.VMEM((256 * CLASSES, n), BF16) for n in (2 * LANES, LANES)]
    brick, part, far, near, classes = call(
        advect_kernel,
        [(3, *whole), (3, *whole), (3, *face), (3, *face), (8, LANES)],
        (velocity, slots, class_index.reshape(1, LANES)),
        [
            (3, NODES, LANES),
            pltpu.VMEM((1, LANES), jnp.int32),
            pltpu.VMEM((1, LANES), jnp.int32),
            pltpu.SemaphoreType.DMA((5,)),
        ],
        name="advect",
        hbm=(0, 1, 2),
    )
    swapped = swap("slab", far, near)
    part, split_0 = lax.optimization_barrier((part, split_half(schur, 0)))
    part, far, near, first_side, last_side = call(
        source_kernel,
        [(1, *whole), (2, *face), (2, *face), (3, *face), (3, *face)],
        (part, *swapped, brick, classes),
        [(3, *whole)],
        name="source",
    )
    part, far, near, ghost_classes = call(
        correct_kernel,
        [(2, *whole), (2, *face), (2, *face), (8, LANES)],
        (part, *swap("dom", far, near), first_side, last_side),
        name="correct",
    )
    swapped = swap("slab", far, near)
    part, split_1 = lax.optimization_barrier((part, split_half(schur, 1)))
    load, first, part, far, near = call(
        first_apply_kernel,
        [modes, modes, (1, *whole), (1, *face), (1, *face)],
        (part, *swapped, split_0, split_1, classes, ghost_classes),
        [(392, LANES), (392, LANES), modes, (2, *face), rights[0], rights[0]],
        name="first",
    )
    run, doms = lax.axis_size("slab") // 2, lax.axis_size("dom")
    rings = [[doms * run * half + doms * k + d for k in range(run)] for half in range(2) for d in range(doms)]
    sheets = [
        [doms * (run * half + k) + d for half in range(2) for d in range(doms)] for k in range(run)
    ]
    power, send, part, far, near = call(
        second_apply_kernel,
        [modes, (2 * doms, 8, LANES), (1, *whole), (1, *face), (1, *face)],
        (part, *swap("slab", far, near), split_0, split_1, classes, load, first, shell),
        [modes, (392, LANES), *rights],
        name="second",
    )
    got = lax.all_to_all(send, ("slab", "dom"), 0, 0, axis_index_groups=sheets)
    far_x, near_x = swap("slab", far, near)
    got, near_x = lax.optimization_barrier((got, near_x))
    low, high, send = call(
        middle_kernel, [face, face, (run, 8, LANES)], (got,), name="middle"
    )
    dots = lax.all_to_all(send, ("slab", "dom"), 0, 0, axis_index_groups=rings)
    return call(
        finish_kernel,
        [(MODES, LANES), (MODES, LANES)],
        (part, far_x, near_x, low, high, load, power, dots, slots),
        [(392, LANES), modes],
        name="finish",
    )


def solution(mesh):
    return jax.shard_map(
        per_device,
        mesh=mesh,
        in_specs=(
            P(None, None, ("slab", "dom")),
            P("slab", "dom", None),
            P("slab", "dom", None),
            P(),
        ),
        out_specs=(P(None, ("slab", "dom")), P(None, ("slab", "dom"))),
        check_vma=False,
    )
```

```python
import functools

import jax
import jax.numpy as jnp
import numpy as np
from jax import lax
from jax.experimental import pallas as pl
from jax.experimental.pallas import tpu as pltpu
from jax.sharding import PartitionSpec as P

CLASSES = 16
MODES = 218
NODES = 343
LANES = 128
BZ = 16
BY = 8
DELTA_T = 0.05
F32 = jnp.float32
BF16 = jnp.bfloat16


def gll_tables():
    degree = 6
    outer_point = 0.830223896278567
    inner_point = 0.46884879347071423
    points = np.array([-1.0, -outer_point, -inner_point, 0.0, inner_point, outer_point, 1.0])
    values = (231.0 * points**6 - 315.0 * points**4 + 105.0 * points**2 - 5.0) / 16.0
    weights = 2.0 / (degree * (degree + 1) * values**2)
    derivative = np.zeros((7, 7))
    for target in range(7):
        for source in range(7):
            if target != source:
                derivative[target, source] = values[target] / (
                    values[source] * (points[target] - points[source])
                )
    derivative[0, 0] = -degree * (degree + 1) / 4.0
    derivative[6, 6] = degree * (degree + 1) / 4.0
    return derivative, weights


DERIV, WEIGHTS = gll_tables()
FACTOR = np.where((np.arange(7) == 0) | (np.arange(7) == 6), 2.0, 1.0)


def shell_runs():
    runs, offset = [], 0
    for a in range(7):
        for b in range(7):
            base = 8 * (7 * a + b)
            if a in (0, 6) or b in (0, 6):
                runs.append((offset, base, 7))
                offset += 7
            else:
                runs.append((offset, base, 1))
                runs.append((offset + 1, base + 6, 1))
                offset += 2
    return runs


RUNS = shell_runs()
FACE_ROWS = {padded // 8: compact for compact, padded, rows in RUNS if rows == 7}


def shell_table():
    multiple = (FACTOR[:, None, None] * FACTOR[None, :, None] * FACTOR[None, None, :]).reshape(-1)
    surface = [
        i for i in range(NODES) if i // 49 in (0, 6) or i // 7 % 7 in (0, 6) or i % 7 in (0, 6)
    ]
    shell = np.zeros((224, LANES))
    shell[:MODES] = (1.0 / multiple[surface])[:, None]
    return shell.astype(np.float32)


SHELL = shell_table()


def span_vector(values):
    node = lax.broadcasted_iota(jnp.int32, (8, LANES), 0)
    table = jnp.zeros((8, LANES), F32)
    for c in range(7):
        table = jnp.where(node == c, float(values[c]), table)
    return table


def span_rolls():
    tables = []
    for shift in range(8):
        sources = [(target - shift) % 8 for target in range(7)]
        tables.append(
            span_vector([DERIV[t, c] if c < 7 else 0.0 for t, c in zip(range(7), sources)])
        )
    return tables


def even_place(axis, like):
    return jnp.full(like.shape, lax.axis_index(axis) % 2, jnp.int32) == 0


def lower_upper(axis, near, far):
    even = even_place(axis, near)
    return jnp.where(even, far, near), jnp.where(even, near, far)


def iotas(shape):
    lane = lax.broadcasted_iota(jnp.int32, shape, len(shape) - 1)
    node = lax.broadcasted_iota(jnp.int32, shape, len(shape) - 2)
    return lane % BZ, lane // BZ, node


def join_span(sheet):
    bz, _, node = iotas(sheet.shape)
    low = pltpu.roll(sheet, 2, 1)
    low = jnp.where(bz == 0, pltpu.roll(low, LANES - 15, 2), pltpu.roll(low, 1, 2))
    high = pltpu.roll(sheet, 6, 1)
    high = jnp.where(bz == BZ - 1, pltpu.roll(high, 15, 2), pltpu.roll(high, LANES - 1, 2))
    return sheet + jnp.where(node == 0, low, jnp.where(node == 6, high, 0.0))


def join_local(sheet):
    sheet = join_span(sheet)
    _, by, _ = iotas(sheet.shape[1:])
    first, last = sheet[0], sheet[6]
    new_first = first + jnp.where(by > 0, pltpu.roll(last, BZ, 1), 0.0)
    new_last = last + jnp.where(by < BY - 1, pltpu.roll(first, LANES - BZ, 1), 0.0)
    return jnp.concatenate([new_first[None], sheet[1:6], new_last[None]], axis=0)


def add_streamwise(a, sheet, far_x, near_x):
    if a == 0:
        sheet = sheet + lower_upper("slab", near_x, far_x)[0]
    if a == 6:
        sheet = sheet + lower_upper("slab", near_x, far_x)[1]
    return sheet


def add_second(sheet, low_y, high_y):
    _, by, _ = iotas(sheet.shape[1:])
    first = sheet[0] + jnp.where(by == 0, low_y, 0.0)
    last = sheet[6] + jnp.where(by == BY - 1, high_y, 0.0)
    return jnp.concatenate([first[None], sheet[1:6], last[None]], axis=0)


def pack_groups(blocks, start):
    _, group, _ = iotas(blocks[0].shape)
    total = jnp.zeros(blocks[0].shape, F32)
    for k, block in enumerate(blocks):
        shift = (BZ * k - start) % LANES
        total = jnp.where(group == k, pltpu.roll(block, shift, 1) if shift else block, total)
    return total


def lanes_from(packed, group, start):
    shift = (start - BZ * group) % LANES
    return pltpu.roll(packed, shift, 1) if shift else packed


def derive_line(sheets):
    sums = [sheets[j] + sheets[6 - j] for j in range(3)] + [sheets[3]]
    differences = [sheets[j] - sheets[6 - j] for j in range(3)]
    odd, even = [], []
    for i in range(4):
        mirrored = [0.5 * (DERIV[i, j] - DERIV[6 - i, 6 - j]) for j in range(7)]
        if i < 3:
            weights = [0.5 * (mirrored[j] + mirrored[6 - j]) for j in range(3)] + [mirrored[3]]
            total = float(weights[0]) * sums[0]
            for j in range(1, 4):
                total = total + float(weights[j]) * sums[j]
            odd.append(total)
        weights = [0.5 * (mirrored[j] - mirrored[6 - j]) for j in range(3)]
        total = float(weights[0]) * differences[0]
        for j in range(1, 3):
            total = total + float(weights[j]) * differences[j]
        even.append(total)
    low = [even[i] + odd[i] for i in range(3)]
    return [*low, even[3], *(even[i] - odd[i] for i in (2, 1, 0))]


def derive_span(rolls, sheet):
    total = rolls[0] * sheet
    for shift in range(1, 8):
        total = total + rolls[shift] * pltpu.roll(sheet, shift, 1)
    return total


def permutation(slot_ref):
    position = lax.broadcasted_iota(jnp.int32, (LANES, LANES), 0)
    return jnp.where(position == slot_ref[...], 1.0, 0.0).astype(BF16)


def moved(values, one_hot, dims):
    return sum(
        lax.dot_general(term, one_hot, (dims, ((), ())), preferred_element_type=F32)
        for term in terms(values)
    )


TO_BRICK = ((1,), (1,))
TO_STORED = ((1,), (0,))


def emit_faces(part_ref, far_ref, near_ref, index):
    low, high = part_ref[index, 0], part_ref[index, 6]
    even = even_place("slab", low)
    far_ref[index] = jnp.where(even, low, high)
    near_ref[index] = jnp.where(even, high, low)


def advect_kernel(
    vel_hbm, slot_hbm, class_hbm,
    brick_ref, part_ref, far_ref, near_ref, class_out,
    vel_ref, slot_ref, class_ref, sems,
):
    copies = [
        pltpu.make_async_copy(src, dst, sems.at[k])
        for k, (src, dst) in enumerate(
            (
                (slot_hbm, slot_ref), (class_hbm, class_ref),
                *((vel_hbm.at[i], vel_ref.at[i]) for i in range(3)),
            )
        )
    ]
    for copy in copies:
        copy.start()
    rolls = span_rolls()
    brick_ref[:, :, :, 7:8, :] = jnp.zeros((3, 7, 7, 1, LANES), F32)
    copies[0].wait()
    copies[1].wait()
    one_hot = permutation(slot_ref)
    class_out[...] = moved(
        jnp.broadcast_to(class_ref[...].astype(F32), (8, LANES)), one_hot, TO_BRICK
    )
    for i in range(3):
        copies[2 + i].wait()
        stored = moved(vel_ref[i], one_hot, TO_BRICK)
        for a in range(7):
            for b in range(7):
                row = 7 * (7 * a + b)
                brick_ref[i, a, b, 0:7, :] = stored[row : row + 7]

    def component(i, carry):
        for b in range(7):
            line = derive_line([brick_ref[i, a, b] for a in range(7)])
            for a in range(7):
                part_ref[i, a, b] = brick_ref[0, a, b] * line[a]
        for a in range(7):
            sheet = brick_ref[i, a]
            along_b = jnp.stack(derive_line([sheet[b] for b in range(7)]), axis=0)
            along_c = derive_span(rolls, sheet)
            advect = (
                part_ref[i, a] + brick_ref[1, a] * along_b + brick_ref[2, a] * along_c
            )
            part_ref[i, a] = join_local(advect)
        emit_faces(part_ref, far_ref, near_ref, i)
        return carry

    lax.fori_loop(0, 3, component, 0)


def source_kernel(
    part_ref, far_x_ref, near_x_ref, brick_ref, class_ref,
    out_ref, far_ref, near_ref, first_ref, last_ref, middle_ref,
):
    rolls = span_rolls()
    weights = span_vector(WEIGHTS)
    inverse = span_vector(1.0 / FACTOR)
    for i in range(3):
        for a in range(7):
            sheet = add_streamwise(a, part_ref[i, a], far_x_ref[i], near_x_ref[i])
            first_ref[i, a], last_ref[i, a] = sheet[0], sheet[6]
            scaled = [
                sheet[b] * (inverse * float(DELTA_T / (FACTOR[a] * FACTOR[b]))) for b in range(7)
            ]
            middle_ref[i, a] = brick_ref[i, a] - jnp.stack(scaled, axis=0)
    for b in range(7):
        line = derive_line([middle_ref[0, a, b] for a in range(7)])
        for a in range(7):
            out_ref[0, a, b] = line[a]
    for a in range(7):
        second = middle_ref[1, a]
        along_b = jnp.stack(derive_line([second[b] for b in range(7)]), axis=0)
        diverge = out_ref[0, a] + along_b + derive_span(rolls, middle_ref[2, a])
        source = [
            diverge[b] * (weights * float(-1.0 / DELTA_T * WEIGHTS[a] * WEIGHTS[b]))
            for b in range(7)
        ]
        out_ref[0, a] = join_local(jnp.stack(source, axis=0))
    classes = class_ref[...]
    even = even_place("dom", classes)
    for a in range(7):
        rows = [*(out_ref[0, a, b] for b in range(7)), classes]
        pairs = (
            (pack_groups(rows, 0), pack_groups(rows, LANES - BZ)),
            (
                pack_groups([first_ref[i, a] for i in range(3)], 0),
                pack_groups([last_ref[i, a] for i in range(3)], LANES - BZ),
            ),
        )
        for k, (down, up) in enumerate(pairs):
            far_ref[k, a] = jnp.where(even, down, up)
            near_ref[k, a] = jnp.where(even, up, down)


def face_source(rolls, weights, inverse, low, high):
    across = []
    for face in (low, high):
        for i in range(3):
            for a in range(7):
                face[i][a] = face[i][a] * (inverse * float(-DELTA_T / (2.0 * FACTOR[a])))
        line = derive_line(face[0])
        across.append([line[a] + derive_span(rolls, face[2][a][None])[0] for a in range(7)])
    sheets = []
    for a in range(7):
        rows = []
        for b in range(7):
            total = float(DERIV[b, 0]) * low[1][a] + float(DERIV[b, 6]) * high[1][a]
            if b == 0:
                total = total + across[0][a]
            if b == 6:
                total = total + across[1][a]
            rows.append(total * (weights * float(-1.0 / DELTA_T * WEIGHTS[a] * WEIGHTS[b])))
        sheets.append(jnp.stack(rows, axis=0))
    return sheets


def correct_kernel(
    part_ref, far_y_ref, near_y_ref, first_ref, last_ref, out_ref, far_ref, near_ref, class_out
):
    rolls = span_rolls()
    weights = span_vector(WEIGHTS)
    inverse = span_vector(1.0 / FACTOR)
    _, by, _ = iotas((8, LANES))
    received = [
        [lower_upper("dom", near_y_ref[k, a], far_y_ref[k, a]) for a in range(7)] for k in range(2)
    ]

    def chosen(place, values):
        return jnp.where(by == place, values, 0.0)

    each = [(i, range(7)) for i in range(3)]
    own = face_source(
        rolls, weights, inverse,
        [[chosen(0, lanes_from(received[1][a][0], i, 0)) for a in r] for i, r in each],
        [[chosen(BY - 1, lanes_from(received[1][a][1], i, LANES - BZ)) for a in r] for i, r in each],
    )
    other = face_source(
        rolls, weights, inverse,
        [[chosen(1, pltpu.roll(last_ref[i, a], 2 * BZ, 1)) for a in r] for i, r in each],
        [[chosen(0, first_ref[i, a]) for a in r] for i, r in each],
    )
    for a in range(7):
        mine = part_ref[0, a] + join_local(own[a])
        low, high = received[0][a]
        theirs = join_span(other[a]) + jnp.stack(
            [
                chosen(0, lanes_from(low, b, 0)) + chosen(1, lanes_from(high, b, BZ))
                for b in range(7)
            ],
            axis=0,
        )
        out_ref[0, a], out_ref[1, a] = mine, theirs
        out_ref[0, a, 0] = mine[0] + chosen(0, theirs[6])
        out_ref[0, a, 6] = mine[6] + chosen(BY - 1, pltpu.roll(theirs[0], LANES - 2 * BZ, 1))
        out_ref[1, a, 6] = theirs[6] + chosen(0, mine[0])
        out_ref[1, a, 0] = theirs[0] + chosen(1, pltpu.roll(mine[6], 2 * BZ, 1))
    for k in range(2):
        emit_faces(out_ref, far_ref, near_ref, k)
    low, high = received[0][0]
    class_out[...] = chosen(0, lanes_from(low, 7, 0)) + chosen(1, lanes_from(high, 7, BZ))


def gather_modes(full_ref, modes_ref):
    modes_ref[216:224] = jnp.zeros((8, LANES), F32)
    for compact, padded, rows in RUNS:
        modes_ref[compact : compact + rows] = full_ref[padded : padded + rows]


def terms(values):
    high = values.astype(BF16)
    rest = values - high.astype(F32)
    middle = rest.astype(BF16)
    return high, middle, (rest - middle.astype(F32)).astype(BF16)


HALF = 8


def split_kernel(half, schur_hbm, split_ref, schur_ref, left_ref, right_ref, sems):
    copies = [
        pltpu.make_async_copy(
            schur_hbm.at[pl.ds(109 * k, 109), pl.ds(HALF * half, HALF)],
            schur_ref.at[pl.ds(109 * k, 109)],
            sems.at[k],
        )
        for k in range(2)
    ]
    for copy in copies:
        copy.start()
    for k in range(2):
        split_ref[224 * k + 208 : 224 * k + 224] = jnp.zeros((16, 256 * HALF), BF16)
    right_ref[...] = jnp.zeros(right_ref.shape, F32)
    for copy in copies:
        copy.wait()
    left_ref[...] = schur_ref[:, :, :LANES].reshape(MODES * HALF, LANES)
    right_ref[:, : MODES - LANES] = schur_ref[:, :, LANES:].reshape(MODES * HALF, MODES - LANES)
    for c in range(HALF):
        for side, side_ref in enumerate((left_ref, right_ref)):
            block = side_ref[pl.ds(c, MODES, stride=HALF), :]
            place = LANES * (2 * c + side)
            for k, term in enumerate(terms(block)[:2]):
                split_ref[224 * k : 224 * k + MODES, place : place + LANES] = term


def split_half(schur, half):
    return call(
        functools.partial(split_kernel, half),
        [((448, 256 * HALF), BF16)],
        (schur,),
        [
            (MODES, HALF, MODES),
            *[(MODES * HALF, LANES)] * 2,
            pltpu.SemaphoreType.DMA((2,)),
        ],
        name="split",
        hbm=(0,),
    )[0]


def multiply_blocks(splits, class_ref, modes_ref, image_ref, right_ref, last_ref, ghost=None):
    high, middle, low = terms(modes_ref[...])
    pair = jnp.concatenate([high, middle], axis=1)
    mine = class_ref[0:1, :]
    both, last_both, rows = jnp.concatenate([mine, mine], axis=1), mine, 224
    if ghost is not None:
        modes, classes = (
            x + pltpu.roll(x, 32, 1) + pltpu.roll(x, 64, 1) for x in (ghost[0], ghost[1])
        )
        lane = lax.broadcasted_iota(jnp.int32, modes.shape, 1)
        three = [
            jnp.where((lane >= 32 * k) & (lane < 32 * k + 32), term.astype(F32), 0.0)
            for k, term in enumerate(terms(modes))
        ]
        low = jnp.concatenate([low, (three[0] + three[1] + three[2]).astype(BF16)], axis=1)
        last_both, rows = jnp.concatenate([mine, classes[0:1]], axis=1), 448
    zeros = jnp.zeros((32, 2 * LANES), BF16)
    for c in range(CLASSES):
        chosen, last_chosen = (
            jnp.where(jnp.abs(x - float(c)) < 0.5, 1.0, 0.0).astype(BF16) for x in (both, last_both)
        )
        right_ref[256 * c : 256 * c + 224] = pair * chosen
        right_ref[256 * c + 224 : 256 * c + 256] = zeros
        last_ref[256 * c : 256 * c + 224] = low * last_chosen
        last_ref[256 * c + 224 : 256 * c + 256] = zeros[:, : low.shape[1]]
    total, small = 0.0, 0.0
    for half, split_ref in enumerate(splits):
        part = pl.ds(256 * HALF * half, 256 * HALF)
        total = total + jnp.dot(split_ref[...], right_ref[part], preferred_element_type=F32)
        small = small + jnp.dot(split_ref[0:rows], last_ref[part], preferred_element_type=F32)
    total = total[:, :LANES] + total[:, LANES:]
    image_ref[...] = total[0:224] + (total[224:448] + small[0:224, :LANES])
    if ghost is None:
        return None
    extra = small[:, LANES:]
    extra = extra[0:224] + extra[224:448]
    return extra + (pltpu.roll(extra, LANES - 32, 1) + pltpu.roll(extra, LANES - 64, 1))


def scatter_modes(image_ref, full_ref, out_ref):
    full_ref[...] = jnp.zeros((392, LANES), F32)
    for compact, padded, rows in RUNS:
        full_ref[padded : padded + rows] = image_ref[compact : compact + rows]
    for a in range(7):
        out_ref[0, a] = join_local(full_ref[56 * a : 56 * a + 56].reshape(7, 8, LANES))


def first_apply_kernel(
    part_ref, far_x_ref, near_x_ref, split_0, split_1, class_ref, ghost_class_ref,
    load_ref, image_ref, out_ref, far_ref, near_ref,
    full_ref, ghost_ref, ghost_modes_ref, side_ref, right_ref, last_ref,
):
    _, by, _ = iotas((8, LANES))
    for k, padded_ref in enumerate((full_ref, ghost_ref)):
        for a in range(7):
            sheet = add_streamwise(a, part_ref[k, a], far_x_ref[k], near_x_ref[k])
            padded_ref[56 * a : 56 * a + 56] = sheet.reshape(56, LANES)
    gather_modes(full_ref, load_ref)
    gather_modes(ghost_ref, ghost_modes_ref)
    ghost_image = multiply_blocks(
        (split_0, split_1), class_ref, load_ref, image_ref, right_ref, last_ref,
        (ghost_modes_ref[...], ghost_class_ref[...]),
    )
    scatter_modes(image_ref, full_ref, out_ref)
    ghost_modes_ref[...] = ghost_image
    side_ref[...] = jnp.zeros(side_ref.shape, F32)
    for k, b in enumerate((6, 0)):
        for a in range(7):
            row = FACE_ROWS[7 * a + b]
            side_ref[k, a, 0:7] = ghost_modes_ref[row : row + 7]
    below, above = join_span(side_ref[0]), join_span(side_ref[1])
    for a in range(7):
        out_ref[0, a, 0] += jnp.where(by == 0, below[a], 0.0)
        out_ref[0, a, 6] += jnp.where(by == BY - 1, pltpu.roll(above[a], LANES - 2 * BZ, 1), 0.0)
    emit_faces(out_ref, far_ref, near_ref, 0)


def second_apply_kernel(
    part_ref, far_x_ref, near_x_ref, split_0, split_1, class_ref, load_ref, first_ref, shell_ref,
    power_ref, send_ref, out_ref, far_ref, near_ref, image_ref, full_ref, right_ref, last_ref,
):
    for a in range(7):
        sheet = add_streamwise(a, part_ref[0, a], far_x_ref[0], near_x_ref[0])
        full_ref[56 * a : 56 * a + 56] = sheet.reshape(56, LANES)
    gather_modes(full_ref, power_ref)
    multiply_blocks((split_0, split_1), class_ref, power_ref, image_ref, right_ref, last_ref)
    scatter_modes(image_ref, full_ref, out_ref)
    emit_faces(out_ref, far_ref, near_ref, 0)
    load, power, shell = load_ref[...], power_ref[...], shell_ref[...]
    first, image = first_ref[...], image_ref[...]
    lane = lax.broadcasted_iota(jnp.int32, (8, LANES), 1)
    node = lax.broadcasted_iota(jnp.int32, (8, LANES), 0)
    columns = jnp.zeros((8, LANES), F32)
    values = (
        load * load * shell, load * first, power * power * shell, load * image, power * image
    )
    for k, value in enumerate(values):
        columns = jnp.where(node == k, jnp.sum(value, axis=0, keepdims=True), columns)
    totals = jnp.sum(columns, axis=1, keepdims=True)
    dots = jnp.sum(jnp.where(lane == node, totals, 0.0), axis=0, keepdims=True)
    count = send_ref.shape[0]
    mine = lax.axis_index("dom")
    alone = jnp.where(node == 7, dots, 0.0)
    send_ref[...] = jnp.broadcast_to(alone[None], send_ref.shape)
    up = pack_groups([out_ref[0, a, 6] for a in range(7)], LANES - BZ)
    down = pack_groups([out_ref[0, a, 0] for a in range(7)], 0)
    send_ref[lax.rem(mine + 1, count)] = jnp.where(node == 7, dots, up)
    send_ref[lax.rem(mine + count - 1, count)] = jnp.where(node == 7, dots, down)


def middle_kernel(got_ref, low_ref, high_ref, send_ref):
    node = lax.broadcasted_iota(jnp.int32, (8, LANES), 0)
    _, by, _ = iotas((8, LANES))
    count = got_ref.shape[0]
    mine = lax.axis_index("dom")
    low = jnp.where(node < 7, got_ref[lax.rem(mine + count - 1, count)], 0.0)
    high = jnp.where(node < 7, got_ref[lax.rem(mine + 1, count)], 0.0)
    for a in range(7):
        low_ref[a], high_ref[a] = lanes_from(low, a, 0), lanes_from(high, a, LANES - BZ)
    total = jnp.sum(got_ref[...], axis=0)[7:8]
    send_ref[...] = jnp.broadcast_to(jnp.where(node == 7, total, 0.0)[None], send_ref.shape)
    slabs = send_ref.shape[0]
    place = lax.axis_index("slab")
    for a, step in ((6, 1), (0, slabs - 1)):
        edges = jnp.where(by == 0, low_ref[a], jnp.where(by == BY - 1, high_ref[a], 0.0))
        send_ref[lax.rem(place + step, slabs)] = jnp.where(node == 7, total, edges)


def finish_kernel(
    part_ref, far_x_ref, near_x_ref, low_ref, high_ref, load_ref, power_ref, dots_ref, slot_ref,
    pressure_ref, residual_ref, full_ref, modes_ref,
):
    node = lax.broadcasted_iota(jnp.int32, (8, LANES), 0)
    slabs = dots_ref.shape[0]
    place = lax.axis_index("slab")
    for a in range(7):
        sheet = add_streamwise(a, part_ref[0, a], far_x_ref[0], near_x_ref[0])
        sheet = add_second(sheet, low_ref[a], high_ref[a])
        if a in (0, 6):
            edges = dots_ref[lax.rem(place + (slabs - 1 if a == 0 else 1), slabs)]
            edges = jnp.where(node < 7, edges, 0.0)
            sheet = add_second(sheet, edges, edges)
        full_ref[56 * a : 56 * a + 56] = sheet.reshape(56, LANES)
    gather_modes(full_ref, modes_ref)
    dots = jnp.sum(dots_ref[...], axis=0)[7:8]
    square, energy, power_square, cross, power_energy = (dots[:, k : k + 1] for k in range(5))
    step = square / energy
    fresh = square - 2.0 * step * energy + step * step * power_square
    ratio = fresh / square
    grow = 1.0 + ratio
    curvature = (
        grow * grow * energy
        - step * grow * (cross + power_square)
        + step * step * power_energy
    )
    second = fresh / curvature
    load, power, twice = load_ref[...], power_ref[...], modes_ref[...]
    pressure = step * load + second * (grow * load - step * power)
    residual = load - step * power - second * (grow * power - step * twice)
    one_hot = permutation(slot_ref)
    pressure_ref[...] = moved(pressure, one_hot, TO_STORED)[:MODES]
    residual_ref[...] = moved(residual, one_hot, TO_STORED)[:MODES]


def call(kernel, outs, args, scratch=(), name=None, hbm=()):
    vmem = pl.BlockSpec(memory_space=pltpu.VMEM)
    places = [pl.BlockSpec(memory_space=pltpu.HBM) if k in hbm else vmem for k in range(len(args))]
    args = [
        pltpu.with_memory_space_constraint(x, pltpu.HBM) if k in hbm else x
        for k, x in enumerate(args)
    ]
    return pl.pallas_call(
        kernel,
        out_shape=tuple(
            jax.ShapeDtypeStruct(*(o if isinstance(o[0], tuple) else (o, F32))) for o in outs
        ),
        in_specs=places,
        out_specs=tuple([vmem] * len(outs)),
        scratch_shapes=[pltpu.VMEM(s, F32) if isinstance(s, tuple) else s for s in scratch],
        compiler_params=pltpu.CompilerParams(vmem_limit_bytes=24 << 20),
        name=name,
    )(*args)


def partners(axis):
    count = lax.axis_size(axis)
    far = [(i, (i + 1) % count if i % 2 else (i - 1) % count) for i in range(count)]
    near = [(i, i ^ 1) for i in range(count)]
    return far, near


def swap(axis, far, near):
    far_pairs, near_pairs = partners(axis)
    return lax.ppermute(far, axis, far_pairs), lax.ppermute(near, axis, near_pairs)


def per_device(velocity, slot_map, class_index, schur_blocks):
    slots = slot_map.reshape(1, LANES)
    shell = jnp.asarray(SHELL)
    schur = schur_blocks.transpose(1, 0, 2)
    face = (7, 8, LANES)
    whole = (7, 7, 8, LANES)
    modes = (224, LANES)
    rights = [pltpu.VMEM((256 * CLASSES, n), BF16) for n in (2 * LANES, LANES)]
    brick, part, far, near, classes = call(
        advect_kernel,
        [(3, *whole), (3, *whole), (3, *face), (3, *face), (8, LANES)],
        (velocity, slots, class_index.reshape(1, LANES)),
        [
            (3, NODES, LANES),
            pltpu.VMEM((1, LANES), jnp.int32),
            pltpu.VMEM((1, LANES), jnp.int32),
            pltpu.SemaphoreType.DMA((5,)),
        ],
        name="advect",
        hbm=(0, 1, 2),
    )
    swapped = swap("slab", far, near)
    part, split_0 = lax.optimization_barrier((part, split_half(schur, 0)))
    part, far, near, first_side, last_side = call(
        source_kernel,
        [(1, *whole), (2, *face), (2, *face), (3, *face), (3, *face)],
        (part, *swapped, brick, classes),
        [(3, *whole)],
        name="source",
    )
    part, far, near, ghost_classes = call(
        correct_kernel,
        [(2, *whole), (2, *face), (2, *face), (8, LANES)],
        (part, *swap("dom", far, near), first_side, last_side),
        name="correct",
    )
    swapped = swap("slab", far, near)
    part, split_1 = lax.optimization_barrier((part, split_half(schur, 1)))
    load, first, part, far, near = call(
        first_apply_kernel,
        [modes, modes, (1, *whole), (1, *face), (1, *face)],
        (part, *swapped, split_0, split_1, classes, ghost_classes),
        [(392, LANES), (392, LANES), modes, (2, *face), rights[0], rights[0]],
        name="first",
    )
    slabs, doms = lax.axis_size("slab"), lax.axis_size("dom")
    power, send, part, far, near = call(
        second_apply_kernel,
        [modes, (doms, 8, LANES), (1, *whole), (1, *face), (1, *face)],
        (part, *swap("slab", far, near), split_0, split_1, classes, load, first, shell),
        [modes, (392, LANES), *rights],
        name="second",
    )
    got = lax.all_to_all(send, "dom", 0, 0)
    far_x, near_x = swap("slab", far, near)
    got, near_x = lax.optimization_barrier((got, near_x))
    low, high, send = call(
        middle_kernel, [face, face, (slabs, 8, LANES)], (got,), name="middle"
    )
    dots = lax.all_to_all(send, "slab", 0, 0)
    return call(
        finish_kernel,
        [(MODES, LANES), (MODES, LANES)],
        (part, far_x, near_x, low, high, load, power, dots, slots),
        [(392, LANES), modes],
        name="finish",
    )


def solution(mesh):
    return jax.shard_map(
        per_device,
        mesh=mesh,
        in_specs=(
            P(None, None, ("slab", "dom")),
            P("slab", "dom", None),
            P("slab", "dom", None),
            P(),
        ),
        out_specs=(P(None, ("slab", "dom")), P(None, ("slab", "dom"))),
        check_vma=False,
    )
```

```python
import functools

import jax
import jax.numpy as jnp
import numpy as np
from jax import lax
from jax.experimental import pallas as pl
from jax.experimental.pallas import tpu as pltpu
from jax.sharding import PartitionSpec as P

CLASSES = 16
MODES = 218
NODES = 343
LANES = 128
BZ = 16
BY = 8
DELTA_T = 0.05
F32 = jnp.float32
BF16 = jnp.bfloat16


def gll_tables():
    degree = 6
    outer_point = 0.830223896278567
    inner_point = 0.46884879347071423
    points = np.array([-1.0, -outer_point, -inner_point, 0.0, inner_point, outer_point, 1.0])
    values = (231.0 * points**6 - 315.0 * points**4 + 105.0 * points**2 - 5.0) / 16.0
    weights = 2.0 / (degree * (degree + 1) * values**2)
    derivative = np.zeros((7, 7))
    for target in range(7):
        for source in range(7):
            if target != source:
                derivative[target, source] = values[target] / (
                    values[source] * (points[target] - points[source])
                )
    derivative[0, 0] = -degree * (degree + 1) / 4.0
    derivative[6, 6] = degree * (degree + 1) / 4.0
    return derivative, weights


DERIV, WEIGHTS = gll_tables()
FACTOR = np.where((np.arange(7) == 0) | (np.arange(7) == 6), 2.0, 1.0)


def shell_runs():
    runs, offset = [], 0
    for a in range(7):
        for b in range(7):
            base = 8 * (7 * a + b)
            if a in (0, 6) or b in (0, 6):
                runs.append((offset, base, 7))
                offset += 7
            else:
                runs.append((offset, base, 1))
                runs.append((offset + 1, base + 6, 1))
                offset += 2
    return runs


RUNS = shell_runs()
FACE_ROWS = {padded // 8: compact for compact, padded, rows in RUNS if rows == 7}


def shell_table():
    multiple = (FACTOR[:, None, None] * FACTOR[None, :, None] * FACTOR[None, None, :]).reshape(-1)
    surface = [
        i for i in range(NODES) if i // 49 in (0, 6) or i // 7 % 7 in (0, 6) or i % 7 in (0, 6)
    ]
    shell = np.zeros((224, LANES))
    shell[:MODES] = (1.0 / multiple[surface])[:, None]
    return shell.astype(np.float32)


SHELL = shell_table()


def span_vector(values):
    node = lax.broadcasted_iota(jnp.int32, (8, LANES), 0)
    table = jnp.zeros((8, LANES), F32)
    for c in range(7):
        table = jnp.where(node == c, float(values[c]), table)
    return table


def span_rolls():
    tables = []
    for shift in range(8):
        sources = [(target - shift) % 8 for target in range(7)]
        tables.append(
            span_vector([DERIV[t, c] if c < 7 else 0.0 for t, c in zip(range(7), sources)])
        )
    return tables


def even_place(axis, like):
    return jnp.full(like.shape, lax.axis_index(axis) % 2, jnp.int32) == 0


def lower_upper(axis, near, far):
    even = even_place(axis, near)
    return jnp.where(even, far, near), jnp.where(even, near, far)


def iotas(shape):
    lane = lax.broadcasted_iota(jnp.int32, shape, len(shape) - 1)
    node = lax.broadcasted_iota(jnp.int32, shape, len(shape) - 2)
    return lane % BZ, lane // BZ, node


def join_span(sheet):
    bz, _, node = iotas(sheet.shape)
    low = pltpu.roll(sheet, 2, 1)
    low = jnp.where(bz == 0, pltpu.roll(low, LANES - 15, 2), pltpu.roll(low, 1, 2))
    high = pltpu.roll(sheet, 6, 1)
    high = jnp.where(bz == BZ - 1, pltpu.roll(high, 15, 2), pltpu.roll(high, LANES - 1, 2))
    return sheet + jnp.where(node == 0, low, jnp.where(node == 6, high, 0.0))


def join_local(sheet):
    sheet = join_span(sheet)
    _, by, _ = iotas(sheet.shape[1:])
    first, last = sheet[0], sheet[6]
    new_first = first + jnp.where(by > 0, pltpu.roll(last, BZ, 1), 0.0)
    new_last = last + jnp.where(by < BY - 1, pltpu.roll(first, LANES - BZ, 1), 0.0)
    return jnp.concatenate([new_first[None], sheet[1:6], new_last[None]], axis=0)


def add_streamwise(a, sheet, far_x, near_x):
    if a == 0:
        sheet = sheet + lower_upper("slab", near_x, far_x)[0]
    if a == 6:
        sheet = sheet + lower_upper("slab", near_x, far_x)[1]
    return sheet


def add_second(sheet, low_y, high_y):
    _, by, _ = iotas(sheet.shape[1:])
    first = sheet[0] + jnp.where(by == 0, low_y, 0.0)
    last = sheet[6] + jnp.where(by == BY - 1, high_y, 0.0)
    return jnp.concatenate([first[None], sheet[1:6], last[None]], axis=0)


def pack_groups(blocks, start):
    _, group, _ = iotas(blocks[0].shape)
    total = jnp.zeros(blocks[0].shape, F32)
    for k, block in enumerate(blocks):
        shift = (BZ * k - start) % LANES
        total = jnp.where(group == k, pltpu.roll(block, shift, 1) if shift else block, total)
    return total


def lanes_from(packed, group, start):
    shift = (start - BZ * group) % LANES
    return pltpu.roll(packed, shift, 1) if shift else packed


def derive_line(sheets):
    sums = [sheets[j] + sheets[6 - j] for j in range(3)] + [sheets[3]]
    differences = [sheets[j] - sheets[6 - j] for j in range(3)]
    odd, even = [], []
    for i in range(4):
        mirrored = [0.5 * (DERIV[i, j] - DERIV[6 - i, 6 - j]) for j in range(7)]
        if i < 3:
            weights = [0.5 * (mirrored[j] + mirrored[6 - j]) for j in range(3)] + [mirrored[3]]
            total = float(weights[0]) * sums[0]
            for j in range(1, 4):
                total = total + float(weights[j]) * sums[j]
            odd.append(total)
        weights = [0.5 * (mirrored[j] - mirrored[6 - j]) for j in range(3)]
        total = float(weights[0]) * differences[0]
        for j in range(1, 3):
            total = total + float(weights[j]) * differences[j]
        even.append(total)
    low = [even[i] + odd[i] for i in range(3)]
    return [*low, even[3], *(even[i] - odd[i] for i in (2, 1, 0))]


def derive_span(rolls, sheet):
    total = rolls[0] * sheet
    for shift in range(1, 8):
        total = total + rolls[shift] * pltpu.roll(sheet, shift, 1)
    return total


def permutation(slot_ref):
    position = lax.broadcasted_iota(jnp.int32, (LANES, LANES), 0)
    return jnp.where(position == slot_ref[...], 1.0, 0.0).astype(BF16)


def moved(values, one_hot, dims):
    return sum(
        lax.dot_general(term, one_hot, (dims, ((), ())), preferred_element_type=F32)
        for term in terms(values)
    )


TO_BRICK = ((1,), (1,))
TO_STORED = ((1,), (0,))


def emit_faces(part_ref, far_ref, near_ref, index):
    low, high = part_ref[index, 0], part_ref[index, 6]
    even = even_place("slab", low)
    far_ref[index] = jnp.where(even, low, high)
    near_ref[index] = jnp.where(even, high, low)


def advect_kernel(
    vel_hbm, slot_hbm, class_hbm,
    brick_ref, part_ref, far_ref, near_ref, class_out,
    vel_ref, slot_ref, class_ref, sems,
):
    copies = [
        pltpu.make_async_copy(src, dst, sems.at[k])
        for k, (src, dst) in enumerate(
            (
                (slot_hbm, slot_ref), (class_hbm, class_ref),
                *((vel_hbm.at[i], vel_ref.at[i]) for i in range(3)),
            )
        )
    ]
    for copy in copies:
        copy.start()
    rolls = span_rolls()
    brick_ref[:, :, :, 7:8, :] = jnp.zeros((3, 7, 7, 1, LANES), F32)
    copies[0].wait()
    copies[1].wait()
    one_hot = permutation(slot_ref)
    class_out[...] = moved(
        jnp.broadcast_to(class_ref[...].astype(F32), (8, LANES)), one_hot, TO_BRICK
    )
    for i in range(3):
        copies[2 + i].wait()
        stored = moved(vel_ref[i], one_hot, TO_BRICK)
        for a in range(7):
            for b in range(7):
                row = 7 * (7 * a + b)
                brick_ref[i, a, b, 0:7, :] = stored[row : row + 7]

    def component(i, carry):
        for b in range(7):
            line = derive_line([brick_ref[i, a, b] for a in range(7)])
            for a in range(7):
                part_ref[i, a, b] = brick_ref[0, a, b] * line[a]
        for a in range(7):
            sheet = brick_ref[i, a]
            along_b = jnp.stack(derive_line([sheet[b] for b in range(7)]), axis=0)
            along_c = derive_span(rolls, sheet)
            advect = (
                part_ref[i, a] + brick_ref[1, a] * along_b + brick_ref[2, a] * along_c
            )
            part_ref[i, a] = join_local(advect)
        emit_faces(part_ref, far_ref, near_ref, i)
        return carry

    lax.fori_loop(0, 3, component, 0)


def source_kernel(
    part_ref, far_x_ref, near_x_ref, brick_ref, class_ref,
    out_ref, far_ref, near_ref, first_ref, last_ref, middle_ref,
):
    rolls = span_rolls()
    weights = span_vector(WEIGHTS)
    inverse = span_vector(1.0 / FACTOR)
    for i in range(3):
        for a in range(7):
            sheet = add_streamwise(a, part_ref[i, a], far_x_ref[i], near_x_ref[i])
            first_ref[i, a], last_ref[i, a] = sheet[0], sheet[6]
            scaled = [
                sheet[b] * (inverse * float(DELTA_T / (FACTOR[a] * FACTOR[b]))) for b in range(7)
            ]
            middle_ref[i, a] = brick_ref[i, a] - jnp.stack(scaled, axis=0)
    for b in range(7):
        line = derive_line([middle_ref[0, a, b] for a in range(7)])
        for a in range(7):
            out_ref[0, a, b] = line[a]
    for a in range(7):
        second = middle_ref[1, a]
        along_b = jnp.stack(derive_line([second[b] for b in range(7)]), axis=0)
        diverge = out_ref[0, a] + along_b + derive_span(rolls, middle_ref[2, a])
        source = [
            diverge[b] * (weights * float(-1.0 / DELTA_T * WEIGHTS[a] * WEIGHTS[b]))
            for b in range(7)
        ]
        out_ref[0, a] = join_local(jnp.stack(source, axis=0))
    classes = class_ref[...]
    even = even_place("dom", classes)
    for a in range(7):
        rows = [*(out_ref[0, a, b] for b in range(7)), classes]
        pairs = (
            (pack_groups(rows, 0), pack_groups(rows, LANES - BZ)),
            (
                pack_groups([first_ref[i, a] for i in range(3)], 0),
                pack_groups([last_ref[i, a] for i in range(3)], LANES - BZ),
            ),
        )
        for k, (down, up) in enumerate(pairs):
            far_ref[k, a] = jnp.where(even, down, up)
            near_ref[k, a] = jnp.where(even, up, down)


def face_source(rolls, weights, inverse, low, high):
    across = []
    for face in (low, high):
        for i in range(3):
            for a in range(7):
                face[i][a] = face[i][a] * (inverse * float(-DELTA_T / (2.0 * FACTOR[a])))
        line = derive_line(face[0])
        across.append([line[a] + derive_span(rolls, face[2][a][None])[0] for a in range(7)])
    sheets = []
    for a in range(7):
        rows = []
        for b in range(7):
            total = float(DERIV[b, 0]) * low[1][a] + float(DERIV[b, 6]) * high[1][a]
            if b == 0:
                total = total + across[0][a]
            if b == 6:
                total = total + across[1][a]
            rows.append(total * (weights * float(-1.0 / DELTA_T * WEIGHTS[a] * WEIGHTS[b])))
        sheets.append(jnp.stack(rows, axis=0))
    return sheets


def other_kernel(first_ref, last_ref, out_ref):
    _, by, _ = iotas((8, LANES))
    each = [(i, range(7)) for i in range(3)]
    other = face_source(
        span_rolls(), span_vector(WEIGHTS), span_vector(1.0 / FACTOR),
        [
            [jnp.where(by == 1, pltpu.roll(last_ref[i, a], 2 * BZ, 1), 0.0) for a in r]
            for i, r in each
        ],
        [[jnp.where(by == 0, first_ref[i, a], 0.0) for a in r] for i, r in each],
    )
    for a in range(7):
        out_ref[a] = join_span(other[a])


def correct_kernel(
    part_ref, far_y_ref, near_y_ref, other_ref, out_ref, far_ref, near_ref, class_out
):
    rolls = span_rolls()
    weights = span_vector(WEIGHTS)
    inverse = span_vector(1.0 / FACTOR)
    _, by, _ = iotas((8, LANES))
    received = [
        [lower_upper("dom", near_y_ref[k, a], far_y_ref[k, a]) for a in range(7)] for k in range(2)
    ]

    def chosen(place, values):
        return jnp.where(by == place, values, 0.0)

    each = [(i, range(7)) for i in range(3)]
    own = face_source(
        rolls, weights, inverse,
        [[chosen(0, lanes_from(received[1][a][0], i, 0)) for a in r] for i, r in each],
        [[chosen(BY - 1, lanes_from(received[1][a][1], i, LANES - BZ)) for a in r] for i, r in each],
    )
    for a in range(7):
        mine = part_ref[0, a] + join_local(own[a])
        low, high = received[0][a]
        theirs = other_ref[a] + jnp.stack(
            [
                chosen(0, lanes_from(low, b, 0)) + chosen(1, lanes_from(high, b, BZ))
                for b in range(7)
            ],
            axis=0,
        )
        out_ref[0, a], out_ref[1, a] = mine, theirs
        out_ref[0, a, 0] = mine[0] + chosen(0, theirs[6])
        out_ref[0, a, 6] = mine[6] + chosen(BY - 1, pltpu.roll(theirs[0], LANES - 2 * BZ, 1))
        out_ref[1, a, 6] = theirs[6] + chosen(0, mine[0])
        out_ref[1, a, 0] = theirs[0] + chosen(1, pltpu.roll(mine[6], 2 * BZ, 1))
    for k in range(2):
        emit_faces(out_ref, far_ref, near_ref, k)
    low, high = received[0][0]
    class_out[...] = chosen(0, lanes_from(low, 7, 0)) + chosen(1, lanes_from(high, 7, BZ))


def gather_modes(full_ref, modes_ref):
    modes_ref[216:224] = jnp.zeros((8, LANES), F32)
    for compact, padded, rows in RUNS:
        modes_ref[compact : compact + rows] = full_ref[padded : padded + rows]


def terms(values):
    high = values.astype(BF16)
    rest = values - high.astype(F32)
    middle = rest.astype(BF16)
    return high, middle, (rest - middle.astype(F32)).astype(BF16)


HALF = 8


def split_kernel(half, schur_hbm, split_ref, schur_ref, left_ref, right_ref, sems):
    copies = [
        pltpu.make_async_copy(
            schur_hbm.at[pl.ds(109 * k, 109), pl.ds(HALF * half, HALF)],
            schur_ref.at[pl.ds(109 * k, 109)],
            sems.at[k],
        )
        for k in range(2)
    ]
    for copy in copies:
        copy.start()
    for k in range(2):
        split_ref[224 * k + 208 : 224 * k + 224] = jnp.zeros((16, 256 * HALF), BF16)
    right_ref[...] = jnp.zeros(right_ref.shape, F32)
    for copy in copies:
        copy.wait()
    left_ref[...] = schur_ref[:, :, :LANES].reshape(MODES * HALF, LANES)
    right_ref[:, : MODES - LANES] = schur_ref[:, :, LANES:].reshape(MODES * HALF, MODES - LANES)
    for c in range(HALF):
        for side, side_ref in enumerate((left_ref, right_ref)):
            block = side_ref[pl.ds(c, MODES, stride=HALF), :]
            place = LANES * (2 * c + side)
            for k, term in enumerate(terms(block)[:2]):
                split_ref[224 * k : 224 * k + MODES, place : place + LANES] = term


def split_half(schur, half):
    return call(
        functools.partial(split_kernel, half),
        [((448, 256 * HALF), BF16)],
        (schur,),
        [
            (MODES, HALF, MODES),
            *[(MODES * HALF, LANES)] * 2,
            pltpu.SemaphoreType.DMA((2,)),
        ],
        name="split",
        hbm=(0,),
    )[0]


def multiply_blocks(splits, class_ref, modes_ref, image_ref, right_ref, last_ref, ghost=None):
    high, middle, low = terms(modes_ref[...])
    pair = jnp.concatenate([high, middle], axis=1)
    mine = class_ref[0:1, :]
    both, last_both, rows = jnp.concatenate([mine, mine], axis=1), mine, 224
    if ghost is not None:
        modes, classes = (
            x + pltpu.roll(x, 32, 1) + pltpu.roll(x, 64, 1) for x in (ghost[0], ghost[1])
        )
        lane = lax.broadcasted_iota(jnp.int32, modes.shape, 1)
        three = [
            jnp.where((lane >= 32 * k) & (lane < 32 * k + 32), term.astype(F32), 0.0)
            for k, term in enumerate(terms(modes))
        ]
        low = jnp.concatenate([low, (three[0] + three[1] + three[2]).astype(BF16)], axis=1)
        last_both, rows = jnp.concatenate([mine, classes[0:1]], axis=1), 448
    zeros = jnp.zeros((32, 2 * LANES), BF16)
    for c in range(CLASSES):
        chosen, last_chosen = (
            jnp.where(jnp.abs(x - float(c)) < 0.5, 1.0, 0.0).astype(BF16) for x in (both, last_both)
        )
        right_ref[256 * c : 256 * c + 224] = pair * chosen
        right_ref[256 * c + 224 : 256 * c + 256] = zeros
        last_ref[256 * c : 256 * c + 224] = low * last_chosen
        last_ref[256 * c + 224 : 256 * c + 256] = zeros[:, : low.shape[1]]
    total, small = 0.0, 0.0
    for half, split_ref in enumerate(splits):
        part = pl.ds(256 * HALF * half, 256 * HALF)
        total = total + jnp.dot(split_ref[...], right_ref[part], preferred_element_type=F32)
        small = small + jnp.dot(split_ref[0:rows], last_ref[part], preferred_element_type=F32)
    total = total[:, :LANES] + total[:, LANES:]
    image_ref[...] = total[0:224] + (total[224:448] + small[0:224, :LANES])
    if ghost is None:
        return None
    extra = small[:, LANES:]
    extra = extra[0:224] + extra[224:448]
    return extra + (pltpu.roll(extra, LANES - 32, 1) + pltpu.roll(extra, LANES - 64, 1))


def scatter_modes(image_ref, full_ref, out_ref):
    full_ref[...] = jnp.zeros((392, LANES), F32)
    for compact, padded, rows in RUNS:
        full_ref[padded : padded + rows] = image_ref[compact : compact + rows]
    for a in range(7):
        out_ref[0, a] = join_local(full_ref[56 * a : 56 * a + 56].reshape(7, 8, LANES))


def first_apply_kernel(
    part_ref, far_x_ref, near_x_ref, split_0, split_1, class_ref, ghost_class_ref,
    load_ref, image_ref, out_ref, far_ref, near_ref,
    full_ref, ghost_ref, ghost_modes_ref, side_ref, right_ref, last_ref,
):
    _, by, _ = iotas((8, LANES))
    for k, padded_ref in enumerate((full_ref, ghost_ref)):
        for a in range(7):
            sheet = add_streamwise(a, part_ref[k, a], far_x_ref[k], near_x_ref[k])
            padded_ref[56 * a : 56 * a + 56] = sheet.reshape(56, LANES)
    gather_modes(full_ref, load_ref)
    gather_modes(ghost_ref, ghost_modes_ref)
    ghost_image = multiply_blocks(
        (split_0, split_1), class_ref, load_ref, image_ref, right_ref, last_ref,
        (ghost_modes_ref[...], ghost_class_ref[...]),
    )
    scatter_modes(image_ref, full_ref, out_ref)
    ghost_modes_ref[...] = ghost_image
    side_ref[...] = jnp.zeros(side_ref.shape, F32)
    for k, b in enumerate((6, 0)):
        for a in range(7):
            row = FACE_ROWS[7 * a + b]
            side_ref[k, a, 0:7] = ghost_modes_ref[row : row + 7]
    below, above = join_span(side_ref[0]), join_span(side_ref[1])
    for a in range(7):
        out_ref[0, a, 0] += jnp.where(by == 0, below[a], 0.0)
        out_ref[0, a, 6] += jnp.where(by == BY - 1, pltpu.roll(above[a], LANES - 2 * BZ, 1), 0.0)
    emit_faces(out_ref, far_ref, near_ref, 0)


def second_apply_kernel(
    part_ref, far_x_ref, near_x_ref, split_0, split_1, class_ref, load_ref, first_ref, shell_ref,
    power_ref, send_ref, out_ref, far_ref, near_ref, image_ref, full_ref, right_ref, last_ref,
):
    for a in range(7):
        sheet = add_streamwise(a, part_ref[0, a], far_x_ref[0], near_x_ref[0])
        full_ref[56 * a : 56 * a + 56] = sheet.reshape(56, LANES)
    gather_modes(full_ref, power_ref)
    multiply_blocks((split_0, split_1), class_ref, power_ref, image_ref, right_ref, last_ref)
    scatter_modes(image_ref, full_ref, out_ref)
    emit_faces(out_ref, far_ref, near_ref, 0)
    load, power, shell = load_ref[...], power_ref[...], shell_ref[...]
    first, image = first_ref[...], image_ref[...]
    lane = lax.broadcasted_iota(jnp.int32, (8, LANES), 1)
    node = lax.broadcasted_iota(jnp.int32, (8, LANES), 0)
    columns = jnp.zeros((8, LANES), F32)
    values = (
        load * load * shell, load * first, power * power * shell, load * image, power * image
    )
    for k, value in enumerate(values):
        columns = jnp.where(node == k, jnp.sum(value, axis=0, keepdims=True), columns)
    totals = jnp.sum(columns, axis=1, keepdims=True)
    dots = jnp.sum(jnp.where(lane == node, totals, 0.0), axis=0, keepdims=True)
    count = send_ref.shape[0]
    mine = lax.axis_index("dom")
    alone = jnp.where(node == 7, dots, 0.0)
    send_ref[...] = jnp.broadcast_to(alone[None], send_ref.shape)
    up = pack_groups([out_ref[0, a, 6] for a in range(7)], LANES - BZ)
    down = pack_groups([out_ref[0, a, 0] for a in range(7)], 0)
    send_ref[lax.rem(mine + 1, count)] = jnp.where(node == 7, dots, up)
    send_ref[lax.rem(mine + count - 1, count)] = jnp.where(node == 7, dots, down)


def middle_kernel(got_ref, low_ref, high_ref, send_ref):
    node = lax.broadcasted_iota(jnp.int32, (8, LANES), 0)
    _, by, _ = iotas((8, LANES))
    count = got_ref.shape[0]
    mine = lax.axis_index("dom")
    low = jnp.where(node < 7, got_ref[lax.rem(mine + count - 1, count)], 0.0)
    high = jnp.where(node < 7, got_ref[lax.rem(mine + 1, count)], 0.0)
    for a in range(7):
        low_ref[a], high_ref[a] = lanes_from(low, a, 0), lanes_from(high, a, LANES - BZ)
    total = jnp.sum(got_ref[...], axis=0)[7:8]
    send_ref[...] = jnp.broadcast_to(jnp.where(node == 7, total, 0.0)[None], send_ref.shape)
    slabs = send_ref.shape[0]
    place = lax.axis_index("slab")
    for a, step in ((6, 1), (0, slabs - 1)):
        edges = jnp.where(by == 0, low_ref[a], jnp.where(by == BY - 1, high_ref[a], 0.0))
        send_ref[lax.rem(place + step, slabs)] = jnp.where(node == 7, total, edges)


def finish_kernel(
    part_ref, far_x_ref, near_x_ref, low_ref, high_ref, load_ref, power_ref, dots_ref, slot_ref,
    pressure_ref, residual_ref, full_ref, modes_ref,
):
    node = lax.broadcasted_iota(jnp.int32, (8, LANES), 0)
    slabs = dots_ref.shape[0]
    place = lax.axis_index("slab")
    for a in range(7):
        sheet = add_streamwise(a, part_ref[0, a], far_x_ref[0], near_x_ref[0])
        sheet = add_second(sheet, low_ref[a], high_ref[a])
        if a in (0, 6):
            edges = dots_ref[lax.rem(place + (slabs - 1 if a == 0 else 1), slabs)]
            edges = jnp.where(node < 7, edges, 0.0)
            sheet = add_second(sheet, edges, edges)
        full_ref[56 * a : 56 * a + 56] = sheet.reshape(56, LANES)
    gather_modes(full_ref, modes_ref)
    dots = jnp.sum(dots_ref[...], axis=0)[7:8]
    square, energy, power_square, cross, power_energy = (dots[:, k : k + 1] for k in range(5))
    step = square / energy
    fresh = square - 2.0 * step * energy + step * step * power_square
    ratio = fresh / square
    grow = 1.0 + ratio
    curvature = (
        grow * grow * energy
        - step * grow * (cross + power_square)
        + step * step * power_energy
    )
    second = fresh / curvature
    load, power, twice = load_ref[...], power_ref[...], modes_ref[...]
    pressure = step * load + second * (grow * load - step * power)
    residual = load - step * power - second * (grow * power - step * twice)
    one_hot = permutation(slot_ref)
    pressure_ref[...] = moved(pressure, one_hot, TO_STORED)[:MODES]
    residual_ref[...] = moved(residual, one_hot, TO_STORED)[:MODES]


def call(kernel, outs, args, scratch=(), name=None, hbm=()):
    vmem = pl.BlockSpec(memory_space=pltpu.VMEM)
    places = [pl.BlockSpec(memory_space=pltpu.HBM) if k in hbm else vmem for k in range(len(args))]
    args = [
        pltpu.with_memory_space_constraint(x, pltpu.HBM) if k in hbm else x
        for k, x in enumerate(args)
    ]
    return pl.pallas_call(
        kernel,
        out_shape=tuple(
            jax.ShapeDtypeStruct(*(o if isinstance(o[0], tuple) else (o, F32))) for o in outs
        ),
        in_specs=places,
        out_specs=tuple([vmem] * len(outs)),
        scratch_shapes=[pltpu.VMEM(s, F32) if isinstance(s, tuple) else s for s in scratch],
        compiler_params=pltpu.CompilerParams(vmem_limit_bytes=24 << 20),
        name=name,
    )(*args)


def partners(axis):
    count = lax.axis_size(axis)
    far = [(i, (i + 1) % count if i % 2 else (i - 1) % count) for i in range(count)]
    near = [(i, i ^ 1) for i in range(count)]
    return far, near


def swap(axis, far, near):
    far_pairs, near_pairs = partners(axis)
    return lax.ppermute(far, axis, far_pairs), lax.ppermute(near, axis, near_pairs)


def per_device(velocity, slot_map, class_index, schur_blocks):
    slots = slot_map.reshape(1, LANES)
    shell = jnp.asarray(SHELL)
    schur = schur_blocks.transpose(1, 0, 2)
    face = (7, 8, LANES)
    whole = (7, 7, 8, LANES)
    modes = (224, LANES)
    rights = [pltpu.VMEM((256 * CLASSES, n), BF16) for n in (2 * LANES, LANES)]
    brick, part, far, near, classes = call(
        advect_kernel,
        [(3, *whole), (3, *whole), (3, *face), (3, *face), (8, LANES)],
        (velocity, slots, class_index.reshape(1, LANES)),
        [
            (3, NODES, LANES),
            pltpu.VMEM((1, LANES), jnp.int32),
            pltpu.VMEM((1, LANES), jnp.int32),
            pltpu.SemaphoreType.DMA((5,)),
        ],
        name="advect",
        hbm=(0, 1, 2),
    )
    swapped = swap("slab", far, near)
    part, split_0 = lax.optimization_barrier((part, split_half(schur, 0)))
    part, far, near, first_side, last_side = call(
        source_kernel,
        [(1, *whole), (2, *face), (2, *face), (3, *face), (3, *face)],
        (part, *swapped, brick, classes),
        [(3, *whole)],
        name="source",
    )
    other = call(other_kernel, [whole], (first_side, last_side), name="other")[0]
    part, far, near, ghost_classes = call(
        correct_kernel,
        [(2, *whole), (2, *face), (2, *face), (8, LANES)],
        (part, *swap("dom", far, near), other),
        name="correct",
    )
    swapped = swap("slab", far, near)
    part, split_1 = lax.optimization_barrier((part, split_half(schur, 1)))
    load, first, part, far, near = call(
        first_apply_kernel,
        [modes, modes, (1, *whole), (1, *face), (1, *face)],
        (part, *swapped, split_0, split_1, classes, ghost_classes),
        [(392, LANES), (392, LANES), modes, (2, *face), rights[0], rights[0]],
        name="first",
    )
    slabs, doms = lax.axis_size("slab"), lax.axis_size("dom")
    power, send, part, far, near = call(
        second_apply_kernel,
        [modes, (doms, 8, LANES), (1, *whole), (1, *face), (1, *face)],
        (part, *swap("slab", far, near), split_0, split_1, classes, load, first, shell),
        [modes, (392, LANES), *rights],
        name="second",
    )
    got = lax.all_to_all(send, "dom", 0, 0)
    far_x, near_x = swap("slab", far, near)
    got, near_x = lax.optimization_barrier((got, near_x))
    low, high, send = call(
        middle_kernel, [face, face, (slabs, 8, LANES)], (got,), name="middle"
    )
    dots = lax.all_to_all(send, "slab", 0, 0)
    return call(
        finish_kernel,
        [(MODES, LANES), (MODES, LANES)],
        (part, far_x, near_x, low, high, load, power, dots, slots),
        [(392, LANES), modes],
        name="finish",
    )


def solution(mesh):
    return jax.shard_map(
        per_device,
        mesh=mesh,
        in_specs=(
            P(None, None, ("slab", "dom")),
            P("slab", "dom", None),
            P("slab", "dom", None),
            P(),
        ),
        out_specs=(P(None, ("slab", "dom")), P(None, ("slab", "dom"))),
        check_vma=False,
    )
```

```python
import functools

import jax
import jax.numpy as jnp
import numpy as np
from jax import lax
from jax.experimental import pallas as pl
from jax.experimental.pallas import tpu as pltpu
from jax.sharding import PartitionSpec as P

CLASSES = 16
MODES = 218
NODES = 343
LANES = 128
BZ = 16
BY = 8
DELTA_T = 0.05
F32 = jnp.float32
BF16 = jnp.bfloat16


def gll_tables():
    degree = 6
    outer_point = 0.830223896278567
    inner_point = 0.46884879347071423
    points = np.array([-1.0, -outer_point, -inner_point, 0.0, inner_point, outer_point, 1.0])
    values = (231.0 * points**6 - 315.0 * points**4 + 105.0 * points**2 - 5.0) / 16.0
    weights = 2.0 / (degree * (degree + 1) * values**2)
    derivative = np.zeros((7, 7))
    for target in range(7):
        for source in range(7):
            if target != source:
                derivative[target, source] = values[target] / (
                    values[source] * (points[target] - points[source])
                )
    derivative[0, 0] = -degree * (degree + 1) / 4.0
    derivative[6, 6] = degree * (degree + 1) / 4.0
    return derivative, weights


DERIV, WEIGHTS = gll_tables()
FACTOR = np.where((np.arange(7) == 0) | (np.arange(7) == 6), 2.0, 1.0)


def shell_runs():
    runs, offset = [], 0
    for a in range(7):
        for b in range(7):
            base = 8 * (7 * a + b)
            if a in (0, 6) or b in (0, 6):
                runs.append((offset, base, 7))
                offset += 7
            else:
                runs.append((offset, base, 1))
                runs.append((offset + 1, base + 6, 1))
                offset += 2
    return runs


RUNS = shell_runs()
FACE_ROWS = {padded // 8: compact for compact, padded, rows in RUNS if rows == 7}


def shell_table():
    multiple = (FACTOR[:, None, None] * FACTOR[None, :, None] * FACTOR[None, None, :]).reshape(-1)
    surface = [
        i for i in range(NODES) if i // 49 in (0, 6) or i // 7 % 7 in (0, 6) or i % 7 in (0, 6)
    ]
    shell = np.zeros((224, LANES))
    shell[:MODES] = (1.0 / multiple[surface])[:, None]
    return shell.astype(np.float32)


SHELL = shell_table()


def span_vector(values):
    node = lax.broadcasted_iota(jnp.int32, (8, LANES), 0)
    table = jnp.zeros((8, LANES), F32)
    for c in range(7):
        table = jnp.where(node == c, float(values[c]), table)
    return table


def span_rolls():
    tables = []
    for shift in range(8):
        sources = [(target - shift) % 8 for target in range(7)]
        tables.append(
            span_vector([DERIV[t, c] if c < 7 else 0.0 for t, c in zip(range(7), sources)])
        )
    return tables


def even_place(axis, like):
    return jnp.full(like.shape, lax.axis_index(axis) % 2, jnp.int32) == 0


def lower_upper(axis, near, far):
    even = even_place(axis, near)
    return jnp.where(even, far, near), jnp.where(even, near, far)


def iotas(shape):
    lane = lax.broadcasted_iota(jnp.int32, shape, len(shape) - 1)
    node = lax.broadcasted_iota(jnp.int32, shape, len(shape) - 2)
    return lane % BZ, lane // BZ, node


def join_span(sheet):
    bz, _, node = iotas(sheet.shape)
    low = pltpu.roll(sheet, 2, 1)
    low = jnp.where(bz == 0, pltpu.roll(low, LANES - 15, 2), pltpu.roll(low, 1, 2))
    high = pltpu.roll(sheet, 6, 1)
    high = jnp.where(bz == BZ - 1, pltpu.roll(high, 15, 2), pltpu.roll(high, LANES - 1, 2))
    return sheet + jnp.where(node == 0, low, jnp.where(node == 6, high, 0.0))


def join_local(sheet):
    sheet = join_span(sheet)
    _, by, _ = iotas(sheet.shape[1:])
    first, last = sheet[0], sheet[6]
    new_first = first + jnp.where(by > 0, pltpu.roll(last, BZ, 1), 0.0)
    new_last = last + jnp.where(by < BY - 1, pltpu.roll(first, LANES - BZ, 1), 0.0)
    return jnp.concatenate([new_first[None], sheet[1:6], new_last[None]], axis=0)


def add_streamwise(a, sheet, far_x, near_x):
    if a == 0:
        sheet = sheet + lower_upper("slab", near_x, far_x)[0]
    if a == 6:
        sheet = sheet + lower_upper("slab", near_x, far_x)[1]
    return sheet


def add_second(sheet, low_y, high_y):
    _, by, _ = iotas(sheet.shape[1:])
    first = sheet[0] + jnp.where(by == 0, low_y, 0.0)
    last = sheet[6] + jnp.where(by == BY - 1, high_y, 0.0)
    return jnp.concatenate([first[None], sheet[1:6], last[None]], axis=0)


def pack_groups(blocks, start):
    _, group, _ = iotas(blocks[0].shape)
    total = jnp.zeros(blocks[0].shape, F32)
    for k, block in enumerate(blocks):
        shift = (BZ * k - start) % LANES
        total = jnp.where(group == k, pltpu.roll(block, shift, 1) if shift else block, total)
    return total


def lanes_from(packed, group, start):
    shift = (start - BZ * group) % LANES
    return pltpu.roll(packed, shift, 1) if shift else packed


def derive_line(sheets):
    sums = [sheets[j] + sheets[6 - j] for j in range(3)] + [sheets[3]]
    differences = [sheets[j] - sheets[6 - j] for j in range(3)]
    odd, even = [], []
    for i in range(4):
        mirrored = [0.5 * (DERIV[i, j] - DERIV[6 - i, 6 - j]) for j in range(7)]
        if i < 3:
            weights = [0.5 * (mirrored[j] + mirrored[6 - j]) for j in range(3)] + [mirrored[3]]
            total = float(weights[0]) * sums[0]
            for j in range(1, 4):
                total = total + float(weights[j]) * sums[j]
            odd.append(total)
        weights = [0.5 * (mirrored[j] - mirrored[6 - j]) for j in range(3)]
        total = float(weights[0]) * differences[0]
        for j in range(1, 3):
            total = total + float(weights[j]) * differences[j]
        even.append(total)
    low = [even[i] + odd[i] for i in range(3)]
    return [*low, even[3], *(even[i] - odd[i] for i in (2, 1, 0))]


def derive_span(rolls, sheet):
    total = rolls[0] * sheet
    for shift in range(1, 8):
        total = total + rolls[shift] * pltpu.roll(sheet, shift, 1)
    return total


def permutation(slot_ref):
    position = lax.broadcasted_iota(jnp.int32, (LANES, LANES), 0)
    return jnp.where(position == slot_ref[...], 1.0, 0.0).astype(BF16)


def moved(values, one_hot, dims):
    return sum(
        lax.dot_general(term, one_hot, (dims, ((), ())), preferred_element_type=F32)
        for term in terms(values)
    )


TO_BRICK = ((1,), (1,))
TO_STORED = ((1,), (0,))


def emit_faces(part_ref, far_ref, near_ref, index):
    low, high = part_ref[index, 0], part_ref[index, 6]
    even = even_place("slab", low)
    far_ref[index] = jnp.where(even, low, high)
    near_ref[index] = jnp.where(even, high, low)


def advect_kernel(
    vel_hbm, slot_hbm, class_hbm,
    brick_ref, part_ref, far_ref, near_ref, class_out,
    vel_ref, slot_ref, class_ref, sems,
):
    copies = [
        pltpu.make_async_copy(src, dst, sems.at[k])
        for k, (src, dst) in enumerate(
            (
                (slot_hbm, slot_ref), (class_hbm, class_ref),
                *((vel_hbm.at[i], vel_ref.at[i]) for i in range(3)),
            )
        )
    ]
    for copy in copies:
        copy.start()
    rolls = span_rolls()
    brick_ref[:, :, :, 7:8, :] = jnp.zeros((3, 7, 7, 1, LANES), F32)
    copies[0].wait()
    copies[1].wait()
    one_hot = permutation(slot_ref)
    class_out[...] = moved(
        jnp.broadcast_to(class_ref[...].astype(F32), (8, LANES)), one_hot, TO_BRICK
    )
    for i in range(3):
        copies[2 + i].wait()
        stored = moved(vel_ref[i], one_hot, TO_BRICK)
        for a in range(7):
            for b in range(7):
                row = 7 * (7 * a + b)
                brick_ref[i, a, b, 0:7, :] = stored[row : row + 7]

    def component(i, carry):
        for b in range(7):
            line = derive_line([brick_ref[i, a, b] for a in range(7)])
            for a in range(7):
                part_ref[i, a, b] = brick_ref[0, a, b] * line[a]
        for a in range(7):
            sheet = brick_ref[i, a]
            along_b = jnp.stack(derive_line([sheet[b] for b in range(7)]), axis=0)
            along_c = derive_span(rolls, sheet)
            advect = (
                part_ref[i, a] + brick_ref[1, a] * along_b + brick_ref[2, a] * along_c
            )
            part_ref[i, a] = join_local(advect)
        emit_faces(part_ref, far_ref, near_ref, i)
        return carry

    lax.fori_loop(0, 3, component, 0)


def source_kernel(
    part_ref, far_x_ref, near_x_ref, brick_ref, class_ref,
    out_ref, far_ref, near_ref, first_ref, last_ref, middle_ref,
):
    rolls = span_rolls()
    weights = span_vector(WEIGHTS)
    inverse = span_vector(1.0 / FACTOR)
    for i in range(3):
        for a in range(7):
            sheet = add_streamwise(a, part_ref[i, a], far_x_ref[i], near_x_ref[i])
            first_ref[i, a], last_ref[i, a] = sheet[0], sheet[6]
            scaled = [
                sheet[b] * (inverse * float(DELTA_T / (FACTOR[a] * FACTOR[b]))) for b in range(7)
            ]
            middle_ref[i, a] = brick_ref[i, a] - jnp.stack(scaled, axis=0)
    for b in range(7):
        line = derive_line([middle_ref[0, a, b] for a in range(7)])
        for a in range(7):
            out_ref[0, a, b] = line[a]
    for a in range(7):
        second = middle_ref[1, a]
        along_b = jnp.stack(derive_line([second[b] for b in range(7)]), axis=0)
        diverge = out_ref[0, a] + along_b + derive_span(rolls, middle_ref[2, a])
        source = [
            diverge[b] * (weights * float(-1.0 / DELTA_T * WEIGHTS[a] * WEIGHTS[b]))
            for b in range(7)
        ]
        out_ref[0, a] = join_local(jnp.stack(source, axis=0))
    classes = class_ref[...]
    even = even_place("dom", classes)
    for a in range(7):
        rows = [*(out_ref[0, a, b] for b in range(7)), classes]
        pairs = (
            (pack_groups(rows, 0), pack_groups(rows, LANES - BZ)),
            (
                pack_groups([first_ref[i, a] for i in range(3)], 0),
                pack_groups([last_ref[i, a] for i in range(3)], LANES - BZ),
            ),
        )
        for k, (down, up) in enumerate(pairs):
            far_ref[k, a] = jnp.where(even, down, up)
            near_ref[k, a] = jnp.where(even, up, down)


def face_source(rolls, weights, inverse, low, high):
    across = []
    for face in (low, high):
        for i in range(3):
            for a in range(7):
                face[i][a] = face[i][a] * (inverse * float(-DELTA_T / (2.0 * FACTOR[a])))
        line = derive_line(face[0])
        across.append([line[a] + derive_span(rolls, face[2][a][None])[0] for a in range(7)])
    sheets = []
    for a in range(7):
        rows = []
        for b in range(7):
            total = float(DERIV[b, 0]) * low[1][a] + float(DERIV[b, 6]) * high[1][a]
            if b == 0:
                total = total + across[0][a]
            if b == 6:
                total = total + across[1][a]
            rows.append(total * (weights * float(-1.0 / DELTA_T * WEIGHTS[a] * WEIGHTS[b])))
        sheets.append(jnp.stack(rows, axis=0))
    return sheets


def correct_kernel(
    part_ref, far_y_ref, near_y_ref, first_ref, last_ref, out_ref, far_ref, near_ref, class_out
):
    rolls = span_rolls()
    weights = span_vector(WEIGHTS)
    inverse = span_vector(1.0 / FACTOR)
    _, by, _ = iotas((8, LANES))
    received = [
        [lower_upper("dom", near_y_ref[k, a], far_y_ref[k, a]) for a in range(7)] for k in range(2)
    ]

    def chosen(place, values):
        return jnp.where(by == place, values, 0.0)

    each = [(i, range(7)) for i in range(3)]
    own = face_source(
        rolls, weights, inverse,
        [[chosen(0, lanes_from(received[1][a][0], i, 0)) for a in r] for i, r in each],
        [[chosen(BY - 1, lanes_from(received[1][a][1], i, LANES - BZ)) for a in r] for i, r in each],
    )
    other = face_source(
        rolls, weights, inverse,
        [[chosen(1, pltpu.roll(last_ref[i, a], 2 * BZ, 1)) for a in r] for i, r in each],
        [[chosen(0, first_ref[i, a]) for a in r] for i, r in each],
    )
    for a in range(7):
        mine = part_ref[0, a] + join_local(own[a])
        low, high = received[0][a]
        theirs = join_span(other[a]) + jnp.stack(
            [
                chosen(0, lanes_from(low, b, 0)) + chosen(1, lanes_from(high, b, BZ))
                for b in range(7)
            ],
            axis=0,
        )
        out_ref[0, a], out_ref[1, a] = mine, theirs
        out_ref[0, a, 0] = mine[0] + chosen(0, theirs[6])
        out_ref[0, a, 6] = mine[6] + chosen(BY - 1, pltpu.roll(theirs[0], LANES - 2 * BZ, 1))
        out_ref[1, a, 6] = theirs[6] + chosen(0, mine[0])
        out_ref[1, a, 0] = theirs[0] + chosen(1, pltpu.roll(mine[6], 2 * BZ, 1))
    for k in range(2):
        emit_faces(out_ref, far_ref, near_ref, k)
    low, high = received[0][0]
    class_out[...] = chosen(0, lanes_from(low, 7, 0)) + chosen(1, lanes_from(high, 7, BZ))


def gather_modes(full_ref, modes_ref):
    modes_ref[216:224] = jnp.zeros((8, LANES), F32)
    for compact, padded, rows in RUNS:
        modes_ref[compact : compact + rows] = full_ref[padded : padded + rows]


def terms(values):
    high = values.astype(BF16)
    rest = values - high.astype(F32)
    middle = rest.astype(BF16)
    return high, middle, (rest - middle.astype(F32)).astype(BF16)


HALF = 8


def split_kernel(half, schur_hbm, split_ref, schur_ref, left_ref, right_ref, sems):
    copies = [
        pltpu.make_async_copy(
            schur_hbm.at[pl.ds(109 * k, 109), pl.ds(HALF * half, HALF)],
            schur_ref.at[pl.ds(109 * k, 109)],
            sems.at[k],
        )
        for k in range(2)
    ]
    for copy in copies:
        copy.start()
    for k in range(2):
        split_ref[224 * k + 208 : 224 * k + 224] = jnp.zeros((16, 256 * HALF), BF16)
    right_ref[...] = jnp.zeros(right_ref.shape, F32)
    for copy in copies:
        copy.wait()
    left_ref[...] = schur_ref[:, :, :LANES].reshape(MODES * HALF, LANES)
    right_ref[:, : MODES - LANES] = schur_ref[:, :, LANES:].reshape(MODES * HALF, MODES - LANES)
    for c in range(HALF):
        for side, side_ref in enumerate((left_ref, right_ref)):
            block = side_ref[pl.ds(c, MODES, stride=HALF), :]
            place = LANES * (2 * c + side)
            for k, term in enumerate(terms(block)[:2]):
                split_ref[224 * k : 224 * k + MODES, place : place + LANES] = term


def split_half(schur, half):
    return call(
        functools.partial(split_kernel, half),
        [((448, 256 * HALF), BF16)],
        (schur,),
        [
            (MODES, HALF, MODES),
            *[(MODES * HALF, LANES)] * 2,
            pltpu.SemaphoreType.DMA((2,)),
        ],
        name="split",
        hbm=(0,),
    )[0]


def multiply_blocks(splits, class_ref, modes_ref, image_ref, right_ref, last_ref, ghost=None):
    high, middle, low = terms(modes_ref[...])
    pair = jnp.concatenate([high, middle], axis=1)
    mine = class_ref[0:1, :]
    both, rows = jnp.concatenate([mine, mine], axis=1), 224
    last_both = both
    if ghost is None:
        low = jnp.concatenate([low, jnp.zeros(low.shape, BF16)], axis=1)
    else:
        modes, classes = (
            x + pltpu.roll(x, 32, 1) + pltpu.roll(x, 64, 1) for x in (ghost[0], ghost[1])
        )
        lane = lax.broadcasted_iota(jnp.int32, modes.shape, 1)
        three = [
            jnp.where((lane >= 32 * k) & (lane < 32 * k + 32), term.astype(F32), 0.0)
            for k, term in enumerate(terms(modes))
        ]
        low = jnp.concatenate([low, (three[0] + three[1] + three[2]).astype(BF16)], axis=1)
        last_both, rows = jnp.concatenate([mine, classes[0:1]], axis=1), 448
    zeros = jnp.zeros((32, 2 * LANES), BF16)
    for c in range(CLASSES):
        chosen, last_chosen = (
            jnp.where(jnp.abs(x - float(c)) < 0.5, 1.0, 0.0).astype(BF16) for x in (both, last_both)
        )
        right_ref[256 * c : 256 * c + 224] = pair * chosen
        right_ref[256 * c + 224 : 256 * c + 256] = zeros
        last_ref[256 * c : 256 * c + 224] = low * last_chosen
        last_ref[256 * c + 224 : 256 * c + 256] = zeros[:, : low.shape[1]]
    total, small = 0.0, 0.0
    for half, split_ref in enumerate(splits):
        part = pl.ds(256 * HALF * half, 256 * HALF)
        total = total + jnp.dot(split_ref[...], right_ref[part], preferred_element_type=F32)
        small = small + jnp.dot(split_ref[0:rows], last_ref[part], preferred_element_type=F32)
    total = total[:, :LANES] + total[:, LANES:]
    image_ref[...] = total[0:224] + (total[224:448] + small[0:224, :LANES])
    if ghost is None:
        return None
    extra = small[:, LANES:]
    extra = extra[0:224] + extra[224:448]
    return extra + (pltpu.roll(extra, LANES - 32, 1) + pltpu.roll(extra, LANES - 64, 1))


def scatter_modes(image_ref, full_ref, out_ref):
    full_ref[...] = jnp.zeros((392, LANES), F32)
    for compact, padded, rows in RUNS:
        full_ref[padded : padded + rows] = image_ref[compact : compact + rows]
    for a in range(7):
        out_ref[0, a] = join_local(full_ref[56 * a : 56 * a + 56].reshape(7, 8, LANES))


def first_apply_kernel(
    part_ref, far_x_ref, near_x_ref, split_0, split_1, class_ref, ghost_class_ref,
    load_ref, image_ref, out_ref, far_ref, near_ref,
    full_ref, ghost_ref, ghost_modes_ref, side_ref, right_ref, last_ref,
):
    _, by, _ = iotas((8, LANES))
    for k, padded_ref in enumerate((full_ref, ghost_ref)):
        for a in range(7):
            sheet = add_streamwise(a, part_ref[k, a], far_x_ref[k], near_x_ref[k])
            padded_ref[56 * a : 56 * a + 56] = sheet.reshape(56, LANES)
    gather_modes(full_ref, load_ref)
    gather_modes(ghost_ref, ghost_modes_ref)
    ghost_image = multiply_blocks(
        (split_0, split_1), class_ref, load_ref, image_ref, right_ref, last_ref,
        (ghost_modes_ref[...], ghost_class_ref[...]),
    )
    scatter_modes(image_ref, full_ref, out_ref)
    ghost_modes_ref[...] = ghost_image
    side_ref[...] = jnp.zeros(side_ref.shape, F32)
    for k, b in enumerate((6, 0)):
        for a in range(7):
            row = FACE_ROWS[7 * a + b]
            side_ref[k, a, 0:7] = ghost_modes_ref[row : row + 7]
    below, above = join_span(side_ref[0]), join_span(side_ref[1])
    for a in range(7):
        out_ref[0, a, 0] += jnp.where(by == 0, below[a], 0.0)
        out_ref[0, a, 6] += jnp.where(by == BY - 1, pltpu.roll(above[a], LANES - 2 * BZ, 1), 0.0)
    emit_faces(out_ref, far_ref, near_ref, 0)


def second_apply_kernel(
    part_ref, far_x_ref, near_x_ref, split_0, split_1, class_ref, load_ref, first_ref, shell_ref,
    power_ref, send_ref, out_ref, far_ref, near_ref, image_ref, full_ref, right_ref, last_ref,
):
    for a in range(7):
        sheet = add_streamwise(a, part_ref[0, a], far_x_ref[0], near_x_ref[0])
        full_ref[56 * a : 56 * a + 56] = sheet.reshape(56, LANES)
    gather_modes(full_ref, power_ref)
    multiply_blocks((split_0, split_1), class_ref, power_ref, image_ref, right_ref, last_ref)
    scatter_modes(image_ref, full_ref, out_ref)
    emit_faces(out_ref, far_ref, near_ref, 0)
    load, power, shell = load_ref[...], power_ref[...], shell_ref[...]
    first, image = first_ref[...], image_ref[...]
    lane = lax.broadcasted_iota(jnp.int32, (8, LANES), 1)
    node = lax.broadcasted_iota(jnp.int32, (8, LANES), 0)
    columns = jnp.zeros((8, LANES), F32)
    values = (
        load * load * shell, load * first, power * power * shell, load * image, power * image
    )
    for k, value in enumerate(values):
        columns = jnp.where(node == k, jnp.sum(value, axis=0, keepdims=True), columns)
    totals = jnp.sum(columns, axis=1, keepdims=True)
    dots = jnp.sum(jnp.where(lane == node, totals, 0.0), axis=0, keepdims=True)
    count = send_ref.shape[0]
    mine = lax.axis_index("dom")
    alone = jnp.where(node == 7, dots, 0.0)
    send_ref[...] = jnp.broadcast_to(alone[None], send_ref.shape)
    up = pack_groups([out_ref[0, a, 6] for a in range(7)], LANES - BZ)
    down = pack_groups([out_ref[0, a, 0] for a in range(7)], 0)
    send_ref[lax.rem(mine + 1, count)] = jnp.where(node == 7, dots, up)
    send_ref[lax.rem(mine + count - 1, count)] = jnp.where(node == 7, dots, down)


def middle_kernel(got_ref, low_ref, high_ref, send_ref):
    node = lax.broadcasted_iota(jnp.int32, (8, LANES), 0)
    _, by, _ = iotas((8, LANES))
    count = got_ref.shape[0]
    mine = lax.axis_index("dom")
    low = jnp.where(node < 7, got_ref[lax.rem(mine + count - 1, count)], 0.0)
    high = jnp.where(node < 7, got_ref[lax.rem(mine + 1, count)], 0.0)
    for a in range(7):
        low_ref[a], high_ref[a] = lanes_from(low, a, 0), lanes_from(high, a, LANES - BZ)
    total = jnp.sum(got_ref[...], axis=0)[7:8]
    send_ref[...] = jnp.broadcast_to(jnp.where(node == 7, total, 0.0)[None], send_ref.shape)
    slabs = send_ref.shape[0]
    place = lax.axis_index("slab")
    for a, step in ((6, 1), (0, slabs - 1)):
        edges = jnp.where(by == 0, low_ref[a], jnp.where(by == BY - 1, high_ref[a], 0.0))
        send_ref[lax.rem(place + step, slabs)] = jnp.where(node == 7, total, edges)


def finish_kernel(
    part_ref, far_x_ref, near_x_ref, low_ref, high_ref, load_ref, power_ref, dots_ref, slot_ref,
    pressure_ref, residual_ref, full_ref, modes_ref,
):
    node = lax.broadcasted_iota(jnp.int32, (8, LANES), 0)
    slabs = dots_ref.shape[0]
    place = lax.axis_index("slab")
    for a in range(7):
        sheet = add_streamwise(a, part_ref[0, a], far_x_ref[0], near_x_ref[0])
        sheet = add_second(sheet, low_ref[a], high_ref[a])
        if a in (0, 6):
            edges = dots_ref[lax.rem(place + (slabs - 1 if a == 0 else 1), slabs)]
            edges = jnp.where(node < 7, edges, 0.0)
            sheet = add_second(sheet, edges, edges)
        full_ref[56 * a : 56 * a + 56] = sheet.reshape(56, LANES)
    gather_modes(full_ref, modes_ref)
    dots = jnp.sum(dots_ref[...], axis=0)[7:8]
    square, energy, power_square, cross, power_energy = (dots[:, k : k + 1] for k in range(5))
    step = square / energy
    fresh = square - 2.0 * step * energy + step * step * power_square
    ratio = fresh / square
    grow = 1.0 + ratio
    curvature = (
        grow * grow * energy
        - step * grow * (cross + power_square)
        + step * step * power_energy
    )
    second = fresh / curvature
    load, power, twice = load_ref[...], power_ref[...], modes_ref[...]
    pressure = step * load + second * (grow * load - step * power)
    residual = load - step * power - second * (grow * power - step * twice)
    one_hot = permutation(slot_ref)
    pressure_ref[...] = moved(pressure, one_hot, TO_STORED)[:MODES]
    residual_ref[...] = moved(residual, one_hot, TO_STORED)[:MODES]


def call(kernel, outs, args, scratch=(), name=None, hbm=()):
    vmem = pl.BlockSpec(memory_space=pltpu.VMEM)
    places = [pl.BlockSpec(memory_space=pltpu.HBM) if k in hbm else vmem for k in range(len(args))]
    args = [
        pltpu.with_memory_space_constraint(x, pltpu.HBM) if k in hbm else x
        for k, x in enumerate(args)
    ]
    return pl.pallas_call(
        kernel,
        out_shape=tuple(
            jax.ShapeDtypeStruct(*(o if isinstance(o[0], tuple) else (o, F32))) for o in outs
        ),
        in_specs=places,
        out_specs=tuple([vmem] * len(outs)),
        scratch_shapes=[pltpu.VMEM(s, F32) if isinstance(s, tuple) else s for s in scratch],
        compiler_params=pltpu.CompilerParams(vmem_limit_bytes=24 << 20),
        name=name,
    )(*args)


def partners(axis):
    count = lax.axis_size(axis)
    far = [(i, (i + 1) % count if i % 2 else (i - 1) % count) for i in range(count)]
    near = [(i, i ^ 1) for i in range(count)]
    return far, near


def swap(axis, far, near):
    far_pairs, near_pairs = partners(axis)
    return lax.ppermute(far, axis, far_pairs), lax.ppermute(near, axis, near_pairs)


def per_device(velocity, slot_map, class_index, schur_blocks):
    slots = slot_map.reshape(1, LANES)
    shell = jnp.asarray(SHELL)
    schur = schur_blocks.transpose(1, 0, 2)
    face = (7, 8, LANES)
    whole = (7, 7, 8, LANES)
    modes = (224, LANES)
    rights = [pltpu.VMEM((256 * CLASSES, n), BF16) for n in (2 * LANES, LANES)]
    brick, part, far, near, classes = call(
        advect_kernel,
        [(3, *whole), (3, *whole), (3, *face), (3, *face), (8, LANES)],
        (velocity, slots, class_index.reshape(1, LANES)),
        [
            (3, NODES, LANES),
            pltpu.VMEM((1, LANES), jnp.int32),
            pltpu.VMEM((1, LANES), jnp.int32),
            pltpu.SemaphoreType.DMA((5,)),
        ],
        name="advect",
        hbm=(0, 1, 2),
    )
    swapped = swap("slab", far, near)
    part, split_0 = lax.optimization_barrier((part, split_half(schur, 0)))
    part, far, near, first_side, last_side = call(
        source_kernel,
        [(1, *whole), (2, *face), (2, *face), (3, *face), (3, *face)],
        (part, *swapped, brick, classes),
        [(3, *whole)],
        name="source",
    )
    part, far, near, ghost_classes = call(
        correct_kernel,
        [(2, *whole), (2, *face), (2, *face), (8, LANES)],
        (part, *swap("dom", far, near), first_side, last_side),
        name="correct",
    )
    swapped = swap("slab", far, near)
    part, split_1 = lax.optimization_barrier((part, split_half(schur, 1)))
    load, first, part, far, near = call(
        first_apply_kernel,
        [modes, modes, (1, *whole), (1, *face), (1, *face)],
        (part, *swapped, split_0, split_1, classes, ghost_classes),
        [(392, LANES), (392, LANES), modes, (2, *face), rights[0], rights[0]],
        name="first",
    )
    slabs, doms = lax.axis_size("slab"), lax.axis_size("dom")
    power, send, part, far, near = call(
        second_apply_kernel,
        [modes, (doms, 8, LANES), (1, *whole), (1, *face), (1, *face)],
        (part, *swap("slab", far, near), split_0, split_1, classes, load, first, shell),
        [modes, (392, LANES), rights[0], rights[0]],
        name="second",
    )
    got = lax.all_to_all(send, "dom", 0, 0)
    far_x, near_x = swap("slab", far, near)
    got, near_x = lax.optimization_barrier((got, near_x))
    low, high, send = call(
        middle_kernel, [face, face, (slabs, 8, LANES)], (got,), name="middle"
    )
    dots = lax.all_to_all(send, "slab", 0, 0)
    return call(
        finish_kernel,
        [(MODES, LANES), (MODES, LANES)],
        (part, far_x, near_x, low, high, load, power, dots, slots),
        [(392, LANES), modes],
        name="finish",
    )


def solution(mesh):
    return jax.shard_map(
        per_device,
        mesh=mesh,
        in_specs=(
            P(None, None, ("slab", "dom")),
            P("slab", "dom", None),
            P("slab", "dom", None),
            P(),
        ),
        out_specs=(P(None, ("slab", "dom")), P(None, ("slab", "dom"))),
        check_vma=False,
    )
```
